32 devices in a mesh: patch: 8 (over z, x), sub: 4 (over y, core).
Axes of the slice: x: 2, y: 2, z: 4, core: 2. Of those that a mesh axis runs over, the one named last changes fastest.
Arguments:
- displacement: float32 [3, 64, 8192], P(None, 'patch', 'sub'), may hold values from -3 to 3
- load: float32 [3, 64, 8192], P(None, 'patch', 'sub'), may hold values from -6 to 6
- foundation: float32 [3, 64, 8192], P(None, 'patch', 'sub'), may hold values from 0.2 to 2
- layup: int32 [64, 8192], P('patch', 'sub'), may hold values from 0 to 7
- layup_stiffness: float32 [8, 6, 6], replicated, as said below
- w_first: bfloat16 [128, 6], replicated, may hold values from -2.5 to 2.5
- w_mid: bfloat16 [3, 128, 128], replicated, may hold values from -0.5 to 0.5
- w_last: bfloat16 [6, 128], replicated, may hold values from -0.5 to 0.5
Outputs:
- residual: float32 [3, 64, 8192], P(None, 'patch', 'sub')
- adjoint: float32 [3, 64, 8192], P(None, 'patch', 'sub')
- grad_first: float32 [128, 6], replicated
- grad_mid: float32 [3, 128, 128], replicated
- grad_last: float32 [6, 128], replicated
The draws below stay inside these ranges and needn't reach their ends.
Inputs may be any that keep to these rules, and one draw needn't show every extreme that they name: `layup_stiffness`: each of the 8 matrices is symmetric positive definite.
All inputs are finite; a program needn't handle non-finite values.
Results may differ from the reference program's by a relative error of at most 0.0006.
The reference program's roundings to bfloat16 on the way count: a program that leaves them out, or rounds other values in their place, can miss the bound.
Values sent between devices are 32-bit elements; how exact they have to be, the bound alone decides.
No kernel may reach another device: no remote copies, remote signals or barrier semaphores. Data moves between devices by JAX's collectives and lax.ppermute only.
A program may use at most 128 MiB of HBM per device.

```python
import math
import jax
import jax.numpy as jnp
from jax import lax

H = 128
MID = 3
NL = 8
ITERS = 4
NX = 64
NY = 8192


def draw_layup_stiffness(key, part):
    first_key, second_key = jax.random.split(jax.random.fold_in(key, 17))
    mixing = jax.random.normal(first_key, (NL, 6, 6), jnp.float32) * 0.9
    diagonal = jax.random.uniform(second_key, (NL, 6), jnp.float32, 1.0, 3.0)
    coupling = jnp.einsum('lab,lcb->lac', mixing, mixing) / 6.0
    return coupling + diagonal[:, :, None] * jnp.eye(6, dtype=jnp.float32)


def touch_ends(values, key, low, top_value):
    longest = values.shape.index(max(values.shape))
    spots = []
    for shift in (0, 1):
        where = [jax.random.randint(jax.random.fold_in(key, axis), (), 0, length) for axis, length in enumerate(values.shape)]
        where[longest] = (where[longest] + shift) % values.shape[longest]
        spots.append(tuple(where))
    return values.at[spots[0]].set(low).at[spots[1]].set(top_value)


def shard_levels(key, dims, pieces, low, top_value):
    level, own = 1.0, jax.random.fold_in(key, 6)
    for position, parts in pieces:
        draws = jnp.exp(jax.random.uniform(jax.random.fold_in(own, position), (parts,), jnp.float32, low / len(pieces), top_value / len(pieces)))
        level = level * jnp.repeat(draws, dims[position] // parts).reshape([-1 if axis == position else 1 for axis in range(len(dims))])
    return level


def bell_draw(rng, extent, width, limit, shards=(), kind=jnp.bfloat16):
    loudness = shard_levels(rng, extent, shards, -0.22, 0.18) if shards else 1.0
    array = jax.random.normal(rng, extent, jnp.float32) * width * loudness
    return jnp.minimum(jnp.maximum(array, -limit), limit).astype(kind)


def setup_inputs(seed: int = 0) -> dict:
    arg_keys = jax.random.split(jax.random.key(seed), 9)
    return {
        "displacement": bell_draw(arg_keys[0], (3, NX, NY), 0.4, 3.0, ((1, 8), (2, 4)), jnp.float32),
        "load": bell_draw(arg_keys[1], (3, NX, NY), 1.0, 6.0, ((1, 8), (2, 4)), jnp.float32),
        "foundation": jnp.clip(jnp.exp(math.log(2.0) - 2.3025851 * jax.random.uniform(arg_keys[2], (3, NX, NY), jnp.float32) ** shard_levels(arg_keys[2], (3, NX, NY), ((1, 8), (2, 4)), -0.2, 0.2)), 0.2, 2.0),
        "layup": touch_ends(jax.random.randint(arg_keys[3], (NX, NY), 0, NL), jax.random.fold_in(arg_keys[3], 1), 0, NL - 1).astype(jnp.int32),
        "layup_stiffness": draw_layup_stiffness(jax.random.fold_in(arg_keys[8], 71), 0),
        "w_first": bell_draw(arg_keys[5], (H, 6), 6 ** -0.5, 2.5),
        "w_mid": bell_draw(arg_keys[6], (MID, H, H), H ** -0.5, 0.5),
        "w_last": bell_draw(arg_keys[7], (6, H), H ** -0.5, 0.5),
    }


BASIS_VALUE = (0.125, 0.75, 0.125)
BASIS_SLOPE = (-0.5, 0.0, 0.5)
BASIS_CURVE = (1.0, -2.0, 1.0)
HOOP_CURVATURE = 0.25


def correlate(padded, along_x, along_y):
    row_count = padded.shape[-2] - 2
    col_count = padded.shape[-1] - 2
    partial_x = None
    for offset in range(3):
        if along_x[offset] != 0.0:
            weighted = along_x[offset] * padded[..., offset:offset + row_count, :]
            partial_x = weighted if partial_x is None else partial_x + weighted
    running = None
    for offset in range(3):
        if along_y[offset] != 0.0:
            weighted = along_y[offset] * partial_x[..., offset:offset + col_count]
            running = weighted if running is None else running + weighted
    return running


def mirrored(padded, along_x, along_y):
    return correlate(padded, along_x[::-1], along_y[::-1])


def strains(padded):
    along_u, along_v, along_w = padded[0], padded[1], padded[2]
    return jnp.stack([
        correlate(along_u, BASIS_SLOPE, BASIS_VALUE),
        correlate(along_v, BASIS_VALUE, BASIS_SLOPE) + HOOP_CURVATURE * correlate(along_w, BASIS_VALUE, BASIS_VALUE),
        correlate(along_u, BASIS_VALUE, BASIS_SLOPE) + correlate(along_v, BASIS_SLOPE, BASIS_VALUE),
        -correlate(along_w, BASIS_CURVE, BASIS_VALUE),
        -correlate(along_w, BASIS_VALUE, BASIS_CURVE),
        -2.0 * correlate(along_w, BASIS_SLOPE, BASIS_SLOPE)])


def forces(spread):
    force_u = mirrored(spread[0], BASIS_SLOPE, BASIS_VALUE) + mirrored(spread[2], BASIS_VALUE, BASIS_SLOPE)
    force_v = mirrored(spread[1], BASIS_VALUE, BASIS_SLOPE) + mirrored(spread[2], BASIS_SLOPE, BASIS_VALUE)
    force_w = (HOOP_CURVATURE * mirrored(spread[1], BASIS_VALUE, BASIS_VALUE)
               - mirrored(spread[3], BASIS_CURVE, BASIS_VALUE)
               - mirrored(spread[4], BASIS_VALUE, BASIS_CURVE)
               - 2.0 * mirrored(spread[5], BASIS_SLOPE, BASIS_SLOPE))
    return jnp.stack([force_u, force_v, force_w])


def apply_layup(stiffness_map, strain):
    running = stiffness_map[:, 0] * strain[0]
    for column in range(1, 6):
        running = running + stiffness_map[:, column] * strain[column]
    return running


def outer_product(left, right):
    return lax.dot_general(left, right, (((1,), (1,)), ((), ())), preferred_element_type=jnp.float32)


def forward_mlp(inputs, w_first, w_mid, w_last):
    hidden_layer = jnp.tanh(jnp.dot(w_first, inputs, preferred_element_type=jnp.float32)).astype(jnp.bfloat16)
    activations = [hidden_layer]
    for layer_index in range(w_mid.shape[0]):
        hidden_layer = jnp.tanh(jnp.dot(w_mid[layer_index], hidden_layer, preferred_element_type=jnp.float32)).astype(jnp.bfloat16)
        activations.append(hidden_layer)
    return jnp.dot(w_last, hidden_layer, preferred_element_type=jnp.float32), activations


def backward_mlp(inputs, activations, upstream, w_mid, w_last):
    grad_last = outer_product(upstream, activations[-1])
    signal = jnp.dot(w_last.T, upstream, preferred_element_type=jnp.float32)
    derivative = (signal * (1.0 - jnp.square(activations[-1].astype(jnp.float32)))).astype(jnp.bfloat16)
    mid_grads = []
    for layer_index in range(w_mid.shape[0] - 1, -1, -1):
        mid_grads.append(outer_product(derivative, activations[layer_index]))
        signal = jnp.dot(w_mid[layer_index].T, derivative, preferred_element_type=jnp.float32)
        derivative = (signal * (1.0 - jnp.square(activations[layer_index].astype(jnp.float32)))).astype(jnp.bfloat16)
    grad_first = outer_product(derivative, inputs)
    return grad_first, jnp.stack(mid_grads[::-1]), grad_last


def periodic(field, rim_width):
    return jnp.pad(field, ((0, 0), (rim_width, rim_width), (rim_width, rim_width)), mode="wrap")


def reference(displacement, load, foundation, layup, layup_stiffness, w_first, w_mid, w_last):
    def material(strain):
        result = jnp.zeros_like(strain)
        for layup_index in range(NL):
            mixed = apply_layup(layup_stiffness[layup_index][:, :, None, None], strain)
            result = jnp.where(layup[None] == layup_index, mixed, result)
        return result

    strain = strains(periodic(displacement, 1))
    inputs = strain.astype(jnp.bfloat16)
    by_row = jnp.moveaxis(inputs, 1, 0)

    def learned_row(row_inputs):
        outcome, activations = forward_mlp(row_inputs, w_first, w_mid, w_last)
        return outcome

    learned = jnp.moveaxis(lax.map(learned_row, by_row), 0, 1)
    stress = material(strain) + learned
    residual = forces(periodic(stress, 1)) + foundation * displacement - load

    def operate(search):
        return forces(periodic(material(strains(periodic(search, 1))), 1)) + foundation * search

    adjoint = jnp.zeros_like(residual)
    remainder = residual
    direction = residual
    norm_now = jnp.sum(remainder * remainder)
    for step_index in range(ITERS):
        mapped = operate(direction)
        step_size = norm_now / jnp.sum(direction * mapped)
        adjoint = adjoint + step_size * direction
        remainder = remainder - step_size * mapped
        norm_next = jnp.sum(remainder * remainder)
        direction = remainder + (norm_next / norm_now) * direction
        norm_now = norm_next

    upstream = strains(periodic(adjoint, 1)).astype(jnp.bfloat16)

    def accumulate(running, row_pair):
        row_inputs, row_upstream = row_pair
        outcome, activations = forward_mlp(row_inputs, w_first, w_mid, w_last)
        gradients = backward_mlp(row_inputs, activations, row_upstream, w_mid, w_last)
        return jax.tree.map(jnp.add, running, gradients), None

    start = (jnp.zeros((H, 6), jnp.float32), jnp.zeros((MID, H, H), jnp.float32), jnp.zeros((6, H), jnp.float32))
    totals, unused = lax.scan(accumulate, start, (by_row, jnp.moveaxis(upstream, 1, 0)))
    return residual, adjoint, totals[0], totals[1], totals[2]
```

```python
import jax
import jax.numpy as jnp
from jax import lax
from jax.sharding import PartitionSpec as P

HY = 16
LANES = 128
AXES = ("patch", "sub")


def ring(axis, step):
    count = lax.axis_size(axis)
    return [(i, (i + step) % count) for i in range(count)]


def from_both(array, axis, dim, width):
    size = array.shape[dim]
    tail = lax.slice_in_dim(array, size - width, size, axis=dim)
    head = lax.slice_in_dim(array, 0, width, axis=dim)
    before = lax.ppermute(tail, axis, ring(axis, 1))
    after = lax.ppermute(head, axis, ring(axis, -1))
    return before, after


def rolled(array, shift, axis):
    return jnp.roll(array, shift, axis=axis)


def y_parts(field):
    before, after = rolled(field, 1, -1), rolled(field, -1, -1)
    both = before + after
    return 0.125 * both + 0.75 * field, 0.5 * (after - before), both - 2.0 * field


def x_value(f):
    return 0.125 * (rolled(f, 1, -2) + rolled(f, -1, -2)) + 0.75 * f


def x_slope(f):
    return 0.5 * (rolled(f, -1, -2) - rolled(f, 1, -2))


def x_curve(f):
    return rolled(f, 1, -2) + rolled(f, -1, -2) - 2.0 * f


def strains(nodal):
    value_u, slope_u, _ = y_parts(nodal[0])
    value_v, slope_v, _ = y_parts(nodal[1])
    value_w, slope_w, curve_w = y_parts(nodal[2])
    return jnp.stack(
        [
            x_slope(value_u),
            x_value(slope_v + 0.25 * value_w),
            x_value(slope_u) + x_slope(value_v),
            -x_curve(value_w),
            -x_value(curve_w),
            -2.0 * x_slope(slope_w),
        ]
    )


def forces(s):
    def y_value(f):
        return y_parts(f)[0]

    def y_slope(f):
        return -y_parts(f)[1]

    def y_curve(f):
        return y_parts(f)[2]

    value_1 = x_value(s[1])
    return jnp.stack(
        [
            y_value(-x_slope(s[0])) + y_slope(x_value(s[2])),
            y_slope(value_1) + y_value(-x_slope(s[2])),
            y_value(0.25 * value_1 - x_curve(s[3]))
            - y_curve(x_value(s[4]))
            - 2.0 * y_slope(-x_slope(s[5])),
        ]
    )


def apply_layup(stiffness, strain):
    running = stiffness[:, 0] * strain[0]
    for column in range(1, 6):
        running = running + stiffness[:, column] * strain[column]
    return running


def outer_product(left, right):
    return lax.dot_general(
        left, right, (((1,), (1,)), ((), ())), preferred_element_type=jnp.float32
    )


def forward_mlp(inputs, w_first, w_mid, w_last):
    hidden = jnp.tanh(jnp.dot(w_first, inputs, preferred_element_type=jnp.float32)).astype(
        jnp.bfloat16
    )
    activations = [hidden]
    for k in range(w_mid.shape[0]):
        hidden = jnp.tanh(
            jnp.dot(w_mid[k], hidden, preferred_element_type=jnp.float32)
        ).astype(jnp.bfloat16)
        activations.append(hidden)
    return jnp.dot(w_last, hidden, preferred_element_type=jnp.float32), activations


def backward_mlp(inputs, activations, upstream, w_mid, w_last):
    grad_last = outer_product(upstream, activations[-1])
    signal = jnp.dot(w_last.T, upstream, preferred_element_type=jnp.float32)
    derivative = (signal * (1.0 - jnp.square(activations[-1].astype(jnp.float32)))).astype(
        jnp.bfloat16
    )
    mid_grads = []
    for k in range(w_mid.shape[0] - 1, -1, -1):
        mid_grads.append(outer_product(derivative, activations[k]))
        signal = jnp.dot(w_mid[k].T, derivative, preferred_element_type=jnp.float32)
        derivative = (signal * (1.0 - jnp.square(activations[k].astype(jnp.float32)))).astype(
            jnp.bfloat16
        )
    grad_first = outer_product(derivative, inputs)
    return grad_first, jnp.stack(mid_grads[::-1]), grad_last


def everyone(rows):
    return lax.all_to_all(rows, AXES, 0, 0, tiled=True)


def galerkin(matrix, target):
    size = len(target)
    matrix = [list(row) for row in matrix]
    target = list(target)
    scale = [matrix[i][i] for i in range(size)]
    inverse = []
    for i in range(size):
        pivot = matrix[i][i]
        usable = pivot > 1e-6 * scale[i]
        inverse.append(jnp.where(usable, 1.0 / jnp.where(usable, pivot, 1.0), 0.0))
        for j in range(i + 1, size):
            factor = matrix[i][j] * inverse[i]
            for k in range(j, size):
                matrix[j][k] = matrix[j][k] - factor * matrix[i][k]
            target[j] = target[j] - factor * target[i]
    answer = [None] * size
    for i in reversed(range(size)):
        running = target[i]
        for j in range(i + 1, size):
            running = running - matrix[i][j] * answer[j]
        answer[i] = running * inverse[i]
    return answer


def basis_constants(layup_stiffness):
    bending = 0.5 * (jnp.mean(layup_stiffness[:, 3, 3]) + jnp.mean(layup_stiffness[:, 4, 4]))
    centres = [11.5 * bending + 1.1, 9.8 * bending + 1.1, 8.4 * bending + 1.1]
    widths = [3.9 * bending + 0.4, 5.6 * bending + 0.4, 4.8 * bending + 0.4]
    return centres, widths


def per_device(displacement, load, foundation, layup, layup_stiffness, w_first, w_mid, w_last):
    rows, cols = layup.shape
    devices = lax.axis_size("patch") * lax.axis_size("sub")
    wide = cols + LANES
    fields = jnp.concatenate(
        [displacement, foundation, layup.astype(jnp.float32)[None], load]
    )
    before, after = from_both(fields, "sub", 2, HY)
    fields = jnp.concatenate(
        [fields, after, jnp.zeros(fields.shape[:2] + (LANES - 2 * HY,), jnp.float32), before], axis=2
    )
    up, down = from_both(fields[:3], "patch", 1, 2)
    nodal = jnp.concatenate([up, fields[:3], down], axis=1)
    up, down = from_both(fields[3:7], "patch", 1, 6)
    gap = jnp.zeros((4, rows - 6, wide), jnp.float32)
    around = jnp.concatenate([gap, up, fields[3:7], down, gap], axis=1)
    support = around[:3]
    layups = around[3].astype(jnp.int32)
    onehot = (
        layups[None] == jnp.arange(layup_stiffness.shape[0], dtype=jnp.int32)[:, None, None]
    ).astype(jnp.float32)
    stiffness = jnp.einsum(
        "lab,lxy->abxy", layup_stiffness, onehot, precision=lax.Precision.HIGHEST
    )

    strain = strains(nodal)[:, 1:-1]
    own = strain[:, 1:-1, :cols]
    inputs = own.reshape(6, -1).astype(jnp.bfloat16)
    learned, activations = forward_mlp(inputs, w_first, w_mid, w_last)
    edge = jnp.concatenate(
        [strain[:, 0], strain[:, -1], strain[:, 1:-1, cols:].reshape(6, -1)], axis=1
    ).astype(jnp.bfloat16)
    learned_edge, _ = forward_mlp(edge, w_first, w_mid, w_last)
    learned = jnp.concatenate(
        [
            learned_edge[:, None, :wide],
            jnp.concatenate(
                [
                    learned.reshape(6, rows, cols),
                    learned_edge[:, 2 * wide :].reshape(6, rows, LANES),
                ],
                axis=2,
            ),
            learned_edge[:, None, wide : 2 * wide],
        ],
        axis=1,
    )
    stress = apply_layup(stiffness[:, :, rows - 1 : 2 * rows + 1], strain) + learned
    wide_residual = forces(stress)[:, 1:-1] + fields[3:6] * fields[:3] - fields[7:]
    residual = wide_residual[:, :, :cols]

    up, down = from_both(wide_residual, "patch", 1, rows)
    start = jnp.concatenate([up, wide_residual, down], axis=1)

    def mine(array):
        return array[:, rows : 2 * rows, :cols]

    centres, widths = basis_constants(layup_stiffness)
    basis, images = [start], []
    for k in range(3):
        image = forces(apply_layup(stiffness, strains(basis[k]))) + support * basis[k]
        images.append(image)
        following = image - centres[k] * basis[k]
        if k:
            following = following - widths[k - 1] * basis[k - 1]
        basis.append(following * (1.0 / widths[k]))
    last = strains(basis[3])
    energy = jnp.sum(mine(last * apply_layup(stiffness, last))) + jnp.sum(
        mine(support * basis[3] * basis[3])
    )
    sums = [jnp.sum(mine(basis[0] * v)) for v in basis]
    for j in range(3):
        sums += [jnp.sum(mine(images[j] * basis[k])) for k in range(j, 4)]
    sums.append(energy)
    sums = jnp.stack(sums)
    sums = everyone(jnp.broadcast_to(sums, (devices,) + sums.shape)).sum(0)
    matrix = [[None] * 4 for _ in range(4)]
    index = 4
    for j in range(4):
        for k in range(j, 4):
            matrix[j][k] = matrix[k][j] = sums[index]
            index += 1
    weights = galerkin(matrix, [sums[k] for k in range(4)])
    adjoint = weights[0] * basis[0]
    for k in range(1, 4):
        adjoint = adjoint + weights[k] * basis[k]
    upstream = mine(strains(adjoint)).reshape(6, -1).astype(jnp.bfloat16)
    grads = backward_mlp(inputs, activations, upstream, w_mid, w_last)
    flat = jnp.concatenate([g.reshape(-1) for g in grads])
    chunk = -(-flat.shape[0] // devices)
    padded = jnp.pad(flat, (0, devices * chunk - flat.shape[0])).reshape(devices, chunk)
    part = everyone(padded).sum(0)
    total = everyone(jnp.broadcast_to(part, padded.shape)).reshape(-1)
    outs, at = [], 0
    for g in grads:
        outs.append(total[at : at + g.size].reshape(g.shape))
        at += g.size
    return (residual, mine(adjoint), *outs)


def solution(mesh):
    field = P(None, "patch", "sub")
    return jax.shard_map(
        per_device,
        mesh=mesh,
        in_specs=(field, field, field, P("patch", "sub"), P(), P(), P(), P()),
        out_specs=(field, field, P(), P(), P()),
        check_vma=False,
    )
```

```python
import jax
import jax.numpy as jnp
from jax import lax
from jax.experimental import pallas as pl
from jax.experimental.pallas import tpu as pltpu
from jax.sharding import PartitionSpec as P

HY = 16
LANES = 128
AXES = ("patch", "sub")


def ring(axis, step):
    count = lax.axis_size(axis)
    return [(i, (i + step) % count) for i in range(count)]


def from_both(array, axis, dim, width):
    size = array.shape[dim]
    tail = lax.slice_in_dim(array, size - width, size, axis=dim)
    head = lax.slice_in_dim(array, 0, width, axis=dim)
    before = lax.ppermute(tail, axis, ring(axis, 1))
    after = lax.ppermute(head, axis, ring(axis, -1))
    return before, after


def rolled(array, shift, axis):
    return jnp.roll(array, shift, axis=axis)


def y_parts(field):
    before, after = rolled(field, 1, -1), rolled(field, -1, -1)
    both = before + after
    return 0.125 * both + 0.75 * field, 0.5 * (after - before), both - 2.0 * field


def x_value(f):
    return 0.125 * (rolled(f, 1, -2) + rolled(f, -1, -2)) + 0.75 * f


def x_slope(f):
    return 0.5 * (rolled(f, -1, -2) - rolled(f, 1, -2))


def x_curve(f):
    return rolled(f, 1, -2) + rolled(f, -1, -2) - 2.0 * f


def strains(nodal):
    value_u, slope_u, _ = y_parts(nodal[0])
    value_v, slope_v, _ = y_parts(nodal[1])
    value_w, slope_w, curve_w = y_parts(nodal[2])
    return jnp.stack(
        [
            x_slope(value_u),
            x_value(slope_v + 0.25 * value_w),
            x_value(slope_u) + x_slope(value_v),
            -x_curve(value_w),
            -x_value(curve_w),
            -2.0 * x_slope(slope_w),
        ]
    )


def forces(s):
    def y_value(f):
        return y_parts(f)[0]

    def y_slope(f):
        return -y_parts(f)[1]

    def y_curve(f):
        return y_parts(f)[2]

    value_1 = x_value(s[1])
    return jnp.stack(
        [
            y_value(-x_slope(s[0])) + y_slope(x_value(s[2])),
            y_slope(value_1) + y_value(-x_slope(s[2])),
            y_value(0.25 * value_1 - x_curve(s[3]))
            - y_curve(x_value(s[4]))
            - 2.0 * y_slope(-x_slope(s[5])),
        ]
    )


def apply_layup(stiffness, strain):
    running = stiffness[:, 0] * strain[0]
    for column in range(1, 6):
        running = running + stiffness[:, column] * strain[column]
    return running


def outer_product(left, right):
    return lax.dot_general(
        left, right, (((1,), (1,)), ((), ())), preferred_element_type=jnp.float32
    )


def forward_mlp(inputs, w_first, w_mid, w_last):
    hidden = jnp.tanh(jnp.dot(w_first, inputs, preferred_element_type=jnp.float32)).astype(
        jnp.bfloat16
    )
    activations = [hidden]
    for k in range(w_mid.shape[0]):
        hidden = jnp.tanh(
            jnp.dot(w_mid[k], hidden, preferred_element_type=jnp.float32)
        ).astype(jnp.bfloat16)
        activations.append(hidden)
    return jnp.dot(w_last, hidden, preferred_element_type=jnp.float32), activations


def backward_mlp(inputs, activations, upstream, w_mid, w_last):
    grad_last = outer_product(upstream, activations[-1])
    signal = jnp.dot(w_last.T, upstream, preferred_element_type=jnp.float32)
    derivative = (signal * (1.0 - jnp.square(activations[-1].astype(jnp.float32)))).astype(
        jnp.bfloat16
    )
    mid_grads = []
    for k in range(w_mid.shape[0] - 1, -1, -1):
        mid_grads.append(outer_product(derivative, activations[k]))
        signal = jnp.dot(w_mid[k].T, derivative, preferred_element_type=jnp.float32)
        derivative = (signal * (1.0 - jnp.square(activations[k].astype(jnp.float32)))).astype(
            jnp.bfloat16
        )
    grad_first = outer_product(derivative, inputs)
    return grad_first, jnp.stack(mid_grads[::-1]), grad_last


def everyone(rows):
    return lax.all_to_all(rows, AXES, 0, 0, tiled=True)


def galerkin(matrix, target):
    size = len(target)
    matrix = [list(row) for row in matrix]
    target = list(target)
    scale = [matrix[i][i] for i in range(size)]
    inverse = []
    for i in range(size):
        pivot = matrix[i][i]
        usable = pivot > 1e-6 * scale[i]
        inverse.append(jnp.where(usable, 1.0 / jnp.where(usable, pivot, 1.0), 0.0))
        for j in range(i + 1, size):
            factor = matrix[i][j] * inverse[i]
            for k in range(j, size):
                matrix[j][k] = matrix[j][k] - factor * matrix[i][k]
            target[j] = target[j] - factor * target[i]
    answer = [None] * size
    for i in reversed(range(size)):
        running = target[i]
        for j in range(i + 1, size):
            running = running - matrix[i][j] * answer[j]
        answer[i] = running * inverse[i]
    return answer


DEGREE = 3
UPPER = [(a, b) for a in range(6) for b in range(a, 6)]
HALVING = (0.0625, 0.0625, 0.0625, -0.125, -0.125, -0.5)
SUMS = 14


def lanes_of(tile):
    if isinstance(tile, int):
        return pl.ds(tile * LANES, LANES)
    return pl.ds(pl.multiple_of(tile * LANES, LANES), LANES)


def beside(tile, tiles):
    if isinstance(tile, int):
        return (tile - 1) % tiles, (tile + 1) % tiles
    return jnp.where(tile == 0, tiles - 1, tile - 1), jnp.where(tile == tiles - 1, 0, tile + 1)


def x_pair(f):
    return pltpu.roll(f, 1, 0), pltpu.roll(f, f.shape[0] - 1, 0)


def spread_strains(u, v, w):
    value_u, slope_u = u[0] + u[1] + 6.0 * u[2], u[1] - u[0]
    value_v, slope_v = v[0] + v[1] + 6.0 * v[2], v[1] - v[0]
    both_w = w[0] + w[1]
    value_w, slope_w, curve_w = both_w + 6.0 * w[2], w[1] - w[0], both_w - 2.0 * w[2]
    b, a = x_pair(value_u)
    e0 = a - b
    hoop = slope_v + 0.0625 * value_w
    b, a = x_pair(hoop)
    e1 = b + a + 6.0 * hoop
    b = pltpu.roll(slope_u - value_v, 1, 0)
    a = pltpu.roll(slope_u + value_v, slope_u.shape[0] - 1, 0)
    e2 = b + a + 6.0 * slope_u
    b, a = x_pair(value_w)
    e3 = b + a - 2.0 * value_w
    b, a = x_pair(curve_w)
    e4 = b + a + 6.0 * curve_w
    b, a = x_pair(slope_w)
    e5 = a - b
    return e0, e1, e2, e3, e4, e5


def spread_forces(s):
    b, a = x_pair(s[0])
    lean_u = b - a
    b, a = x_pair(s[2])
    lean_v = b - a
    turn_u = b + a + 6.0 * s[2]
    b, a = x_pair(s[1])
    turn_v = b + a + 6.0 * s[1]
    b, a = x_pair(s[3])
    lean_w = 0.0625 * turn_v + (b + a - 2.0 * s[3])
    b, a = x_pair(s[4])
    bent_w = b + a + 6.0 * s[4]
    b, a = x_pair(s[5])
    turn_w = a - b
    sum_w = lean_w + bent_w
    return (
        (lean_u + turn_u, lean_u - turn_u, 6.0 * lean_u),
        (lean_v + turn_v, lean_v - turn_v, 6.0 * lean_v),
        (sum_w - turn_w, sum_w + turn_w, 6.0 * lean_w - 2.0 * bent_w),
    )


def chosen(layers, bits):
    if len(layers) == 1:
        return layers[0]
    half = len(layers) // 2
    return jnp.where(bits[-1], chosen(layers[half:], bits[:-1]), chosen(layers[:half], bits[:-1]))


def krylov_kernel(
    table, numbers, r_mid, r_up, r_down, fields, fl_up, fl_down, basis, sums,
    stiff, before, after, ahead, behind, middle, support,
):
    layups = table.shape[0] // 36
    rows = r_mid.shape[1]
    wide = r_mid.shape[2]
    tiles = wide // LANES
    own_tiles = tiles - 1
    halo = fl_up.shape[1]
    tall = 3 * rows
    lane = lax.broadcasted_iota(jnp.int32, (tall, LANES), 1)
    first, final = lane == 0, lane == LANES - 1
    depth = 1
    while (1 << depth) < layups:
        depth += 1

    def place(k, c, at, value):
        basis[k, c, :, at] = value
        before[c, :, at] = pltpu.roll(value, 1, 1)
        after[c, :, at] = pltpu.roll(value, LANES - 1, 1)

    def set_up(tile, carry):
        at = lanes_of(tile)
        for c in range(3):
            value = jnp.concatenate([r_up[c, :, at], r_mid[c, :, at], r_down[c, :, at]], axis=0)
            place(0, c, at, value)
        edge = jnp.zeros((rows - halo, LANES), jnp.float32)
        for c in range(4):
            support[c, 0 : rows - halo, at] = edge
            support[c, rows - halo : rows, at] = fl_up[c, :, at]
            support[c, rows : 2 * rows, at] = fields[3 + c, :, at]
            support[c, 2 * rows : 2 * rows + halo, at] = fl_down[c, :, at]
            support[c, 2 * rows + halo : tall, at] = edge
        ids = support[3, :, at].astype(jnp.int32)
        bits = [(ids & (1 << k)) != 0 for k in range(depth)]
        for n, (a, b) in enumerate(UPPER):
            layers = [table[min(l, layups - 1) * 36 + a * 6 + b] for l in range(1 << depth)]
            stiff[n, :, at] = jnp.broadcast_to(chosen(layers, bits), (tall, LANES))
        return carry

    lax.fori_loop(0, tiles, set_up, 0)

    def strain_of(k, tile):
        at = lanes_of(tile)
        left, right = beside(tile, tiles)
        at_left, at_right = lanes_of(left), lanes_of(right)
        triples = [
            (
                jnp.where(first, before[c, :, at_left], before[c, :, at]),
                jnp.where(final, after[c, :, at_right], after[c, :, at]),
                basis[k, c, :, at],
            )
            for c in range(3)
        ]
        return spread_strains(*triples)

    def stress_of(e, at):
        s = [None] * 6
        for n, (a, b) in enumerate(UPPER):
            value = stiff[n, :, at]
            for p, q in ((a, b), (b, a))[: 1 if a == b else 2]:
                term = value * e[q]
                s[p] = term if s[p] is None else s[p] + term
        return s

    def mine(value):
        return value[rows : 2 * rows]

    zero = jnp.zeros((rows, LANES), jnp.float32)
    totals = [None] * SUMS

    for k in range(DEGREE):
        def push(tile, carry, k=k):
            at = lanes_of(tile)
            for c, (alpha, beta, gamma) in enumerate(
                spread_forces(stress_of(strain_of(k, tile), at))
            ):
                ahead[c, :, at] = pltpu.roll(alpha, 1, 1)
                behind[c, :, at] = pltpu.roll(beta, LANES - 1, 1)
                middle[c, :, at] = gamma
            return carry

        lax.fori_loop(0, tiles, push, 0)

        centre, width, inverse = numbers[k], numbers[3 + k], numbers[6 + k]
        former = numbers[2 + k]

        def advance(tile, carry, k=k):
            at = lanes_of(tile)
            left, right = beside(tile, tiles)
            at_left, at_right = lanes_of(left), lanes_of(right)
            image, here, following = [], [], []
            for c in range(3):
                vector = basis[k, c, :, at]
                value = (
                    middle[c, :, at]
                    + jnp.where(first, ahead[c, :, at_left], ahead[c, :, at])
                    + jnp.where(final, behind[c, :, at_right], behind[c, :, at])
                    + support[c, :, at] * vector
                )
                step = value - centre * vector
                if k:
                    step = step - former * basis[k - 1, c, :, at]
                step = step * inverse
                place(k + 1, c, at, step)
                image.append(mine(value))
                here.append(mine(vector))
                following.append(mine(step))
            if carry is None:
                return None

            def dot(left_side, right_side):
                return (
                    left_side[0] * right_side[0]
                    + left_side[1] * right_side[1]
                    + left_side[2] * right_side[2]
                )

            def old(m):
                return [basis[m, c, rows : 2 * rows, at] for c in range(3)]

            fresh = []
            origin = here if k == 0 else old(0)
            if k == 0:
                fresh.append(dot(here, here))
            fresh.append(dot(origin, following))
            for j in range(k + 1):
                fresh.append(dot(here if j == k else (origin if j == 0 else old(j)), image))
            if k == DEGREE - 1:
                fresh.append(dot(old(1), following))
                fresh.append(dot(here, following))
                fresh.append(dot(following, following))
            return tuple(p + q for p, q in zip(carry, fresh))

        names = ([0] if k == 0 else []) + [k + 1] + [4 + k * (k + 1) // 2 + j for j in range(k + 1)]
        if k == DEGREE - 1:
            names += [10, 11, 12]
        found = lax.fori_loop(0, own_tiles, advance, (zero,) * len(names))
        advance(own_tiles, None)
        for name, value in zip(names, found):
            totals[name] = value

    def energy(tile, running):
        at = lanes_of(tile)
        e = strain_of(DEGREE, tile)
        e = [mine(value) for value in e]
        for n, (a, b) in enumerate(UPPER):
            term = stiff[n, rows : 2 * rows, at] * e[b] * e[a]
            running = running + (term if a == b else 2.0 * term)
        for c in range(3):
            vector = basis[DEGREE, c, rows : 2 * rows, at]
            running = running + support[c, rows : 2 * rows, at] * vector * vector
        return running

    totals[13] = lax.fori_loop(0, own_tiles, energy, zero)
    place_of = lax.broadcasted_iota(jnp.int32, (1, LANES), 1)
    line = jnp.zeros((1, LANES), jnp.float32)
    for n in range(SUMS):
        total = jnp.sum(jnp.sum(totals[n], axis=0, keepdims=True), axis=1, keepdims=True)
        line = jnp.where(place_of == n, jnp.broadcast_to(total, (1, LANES)), line)
    sums[...] = jnp.broadcast_to(line[None], sums.shape)


def solve_kernel(numbers, sums, basis, adjoint, upstream, combined):
    rows = adjoint.shape[1]
    wide = basis.shape[3]
    tiles = wide // LANES
    own_tiles = tiles - 1
    tall = 3 * rows
    line = jnp.sum(sums[...], axis=0)
    picks = [jnp.broadcast_to(line[:, n : n + 1], (1, LANES)) for n in range(SUMS)]
    centre = [numbers[k] for k in range(3)]
    width = [numbers[3 + k] for k in range(3)]
    matrix = [[None] * 4 for _ in range(4)]
    for k in range(3):
        for j in range(k + 1):
            matrix[j][k] = picks[4 + k * (k + 1) // 2 + j]
    cross = [picks[3], picks[10], picks[11], picks[12]]
    for j in range(3):
        value = width[j] * cross[j + 1] + centre[j] * cross[j]
        matrix[j][3] = value + width[j - 1] * cross[j - 1] if j else value
    matrix[3][3] = picks[13]
    weights = [jnp.broadcast_to(x, (tall, LANES)) for x in galerkin(matrix, picks[:4])]

    def combine(tile, carry):
        at = lanes_of(tile)
        for c in range(3):
            value = weights[0] * basis[0, c, :, at]
            for k in range(1, DEGREE + 1):
                value = value + weights[k] * basis[k, c, :, at]
            combined[c, :, at] = value
            combined[3 + c, :, at] = pltpu.roll(value, 1, 1)
            combined[6 + c, :, at] = pltpu.roll(value, LANES - 1, 1)
        return carry

    lax.fori_loop(0, tiles, combine, 0)
    lane = lax.broadcasted_iota(jnp.int32, (tall, LANES), 1)
    first, final = lane == 0, lane == LANES - 1

    def strain(tile, carry):
        at = lanes_of(tile)
        left, right = beside(tile, tiles)
        at_left, at_right = lanes_of(left), lanes_of(right)
        triples = [
            (
                jnp.where(first, combined[3 + c, :, at_left], combined[3 + c, :, at]),
                jnp.where(final, combined[6 + c, :, at_right], combined[6 + c, :, at]),
                combined[c, :, at],
            )
            for c in range(3)
        ]
        for c in range(3):
            adjoint[c, :, at] = combined[c, rows : 2 * rows, at]
        for n, value in enumerate(spread_strains(*triples)):
            upstream[n, :, at] = HALVING[n] * value[rows : 2 * rows]
        return carry

    lax.fori_loop(0, own_tiles, strain, 0)


def basis_constants(layup_stiffness):
    bending = 0.5 * (jnp.mean(layup_stiffness[:, 3, 3]) + jnp.mean(layup_stiffness[:, 4, 4]))
    centres = [11.5 * bending + 1.1, 9.8 * bending + 1.1, 8.4 * bending + 1.1]
    widths = [3.9 * bending + 0.4, 5.6 * bending + 0.4, 4.8 * bending + 0.4]
    return centres, widths


def per_device(displacement, load, foundation, layup, layup_stiffness, w_first, w_mid, w_last):
    rows, cols = layup.shape
    devices = lax.axis_size("patch") * lax.axis_size("sub")
    wide = cols + LANES
    fields = jnp.concatenate(
        [displacement, foundation, layup.astype(jnp.float32)[None], load]
    )
    before, after = from_both(fields, "sub", 2, HY)
    fields = jnp.concatenate(
        [fields, after, jnp.zeros(fields.shape[:2] + (LANES - 2 * HY,), jnp.float32), before], axis=2
    )
    up, down = from_both(fields[:3], "patch", 1, 2)
    nodal = jnp.concatenate([up, fields[:3], down], axis=1)
    up, down = from_both(fields[3:7], "patch", 1, 6)
    near = jnp.concatenate([up[3, -1:], fields[6], down[3, :1]], axis=0).astype(jnp.int32)
    onehot = (
        near[None] == jnp.arange(layup_stiffness.shape[0], dtype=jnp.int32)[:, None, None]
    ).astype(jnp.float32)
    stiffness = jnp.einsum(
        "lab,lxy->abxy", layup_stiffness, onehot, precision=lax.Precision.HIGHEST
    )
    beyond = (up, down)

    strain = strains(nodal)[:, 1:-1]
    own = strain[:, 1:-1, :cols]
    inputs = own.reshape(6, -1).astype(jnp.bfloat16)
    learned, activations = forward_mlp(inputs, w_first, w_mid, w_last)
    edge = jnp.concatenate(
        [strain[:, 0], strain[:, -1], strain[:, 1:-1, cols:].reshape(6, -1)], axis=1
    ).astype(jnp.bfloat16)
    learned_edge, _ = forward_mlp(edge, w_first, w_mid, w_last)
    learned = jnp.concatenate(
        [
            learned_edge[:, None, :wide],
            jnp.concatenate(
                [
                    learned.reshape(6, rows, cols),
                    learned_edge[:, 2 * wide :].reshape(6, rows, LANES),
                ],
                axis=2,
            ),
            learned_edge[:, None, wide : 2 * wide],
        ],
        axis=1,
    )
    stress = apply_layup(stiffness, strain) + learned
    wide_residual = forces(stress)[:, 1:-1] + fields[3:6] * fields[:3] - fields[7:]
    residual = wide_residual[:, :, :cols]

    up, down = from_both(wide_residual, "patch", 1, rows)
    halving = jnp.array(HALVING, jnp.float32)
    table = (layup_stiffness * halving[:, None] * halving[None, :]).reshape(-1)
    centres, widths = basis_constants(layup_stiffness)
    numbers = jnp.stack(centres + widths + [1.0 / x for x in widths])
    on_chip = pl.BlockSpec(memory_space=pltpu.VMEM)
    scalars = pl.BlockSpec(memory_space=pltpu.SMEM)
    tall = 3 * rows
    block = pltpu.VMEM((3, tall, wide), jnp.float32)
    basis, sums = pl.pallas_call(
        krylov_kernel,
        name="krylov",
        in_specs=[scalars, scalars] + [on_chip] * 6,
        out_specs=[on_chip, on_chip],
        out_shape=[
            jax.ShapeDtypeStruct((DEGREE + 1, 3, tall, wide), jnp.float32),
            jax.ShapeDtypeStruct((devices, 1, LANES), jnp.float32),
        ],
        scratch_shapes=[pltpu.VMEM((len(UPPER), tall, wide), jnp.float32)]
        + [block] * 5
        + [pltpu.VMEM((4, tall, wide), jnp.float32)],
        compiler_params=pltpu.CompilerParams(vmem_limit_bytes=32 << 20),
    )(table, numbers, wide_residual, up, down, fields, *beyond)
    sums = everyone(sums)
    adjoint, upstream = pl.pallas_call(
        solve_kernel,
        name="solve",
        in_specs=[scalars, on_chip, on_chip],
        out_specs=[on_chip, on_chip],
        out_shape=[
            jax.ShapeDtypeStruct((3, rows, cols), jnp.float32),
            jax.ShapeDtypeStruct((6, rows, cols), jnp.float32),
        ],
        scratch_shapes=[pltpu.VMEM((9, tall, wide), jnp.float32)],
        compiler_params=pltpu.CompilerParams(vmem_limit_bytes=32 << 20),
    )(numbers, sums, basis)
    upstream = upstream.reshape(6, -1).astype(jnp.bfloat16)
    grads = backward_mlp(inputs, activations, upstream, w_mid, w_last)
    flat = jnp.concatenate([g.reshape(-1) for g in grads])
    chunk = -(-flat.shape[0] // devices)
    padded = jnp.pad(flat, (0, devices * chunk - flat.shape[0])).reshape(devices, chunk)
    part = everyone(padded).sum(0)
    total = everyone(jnp.broadcast_to(part, padded.shape)).reshape(-1)
    outs, at = [], 0
    for g in grads:
        outs.append(total[at : at + g.size].reshape(g.shape))
        at += g.size
    return (residual, adjoint, *outs)


def solution(mesh):
    field = P(None, "patch", "sub")
    return jax.shard_map(
        per_device,
        mesh=mesh,
        in_specs=(field, field, field, P("patch", "sub"), P(), P(), P(), P()),
        out_specs=(field, field, P(), P(), P()),
        check_vma=False,
    )
```

```python
import jax
import jax.numpy as jnp
from jax import lax
from jax.experimental import pallas as pl
from jax.experimental.pallas import tpu as pltpu
from jax.sharding import PartitionSpec as P

HY = 16
LANES = 128
AXES = ("patch", "sub")


def ring(axis, step):
    count = lax.axis_size(axis)
    return [(i, (i + step) % count) for i in range(count)]


def from_both(array, axis, dim, width):
    size = array.shape[dim]
    tail = lax.slice_in_dim(array, size - width, size, axis=dim)
    head = lax.slice_in_dim(array, 0, width, axis=dim)
    before = lax.ppermute(tail, axis, ring(axis, 1))
    after = lax.ppermute(head, axis, ring(axis, -1))
    return before, after


def everyone(rows):
    return lax.all_to_all(rows, AXES, 0, 0, tiled=True)


def galerkin(matrix, target):
    size = len(target)
    matrix = [list(row) for row in matrix]
    target = list(target)
    scale = [matrix[i][i] for i in range(size)]
    inverse = []
    for i in range(size):
        pivot = matrix[i][i]
        usable = pivot > 1e-6 * scale[i]
        inverse.append(jnp.where(usable, 1.0 / jnp.where(usable, pivot, 1.0), 0.0))
        for j in range(i + 1, size):
            factor = matrix[i][j] * inverse[i]
            for k in range(j, size):
                matrix[j][k] = matrix[j][k] - factor * matrix[i][k]
            target[j] = target[j] - factor * target[i]
    answer = [None] * size
    for i in reversed(range(size)):
        running = target[i]
        for j in range(i + 1, size):
            running = running - matrix[i][j] * answer[j]
        answer[i] = running * inverse[i]
    return answer


DEGREE = 3
UPPER = [(a, b) for a in range(6) for b in range(a, 6)]
HALVING = (0.0625, 0.0625, 0.0625, -0.125, -0.125, -0.5)
SUMS = 14


def lanes_of(tile):
    if isinstance(tile, int):
        return pl.ds(tile * LANES, LANES)
    return pl.ds(pl.multiple_of(tile * LANES, LANES), LANES)


def beside(tile, tiles):
    if isinstance(tile, int):
        return (tile - 1) % tiles, (tile + 1) % tiles
    return jnp.where(tile == 0, tiles - 1, tile - 1), jnp.where(tile == tiles - 1, 0, tile + 1)


def x_pair(f):
    return pltpu.roll(f, 1, 0), pltpu.roll(f, f.shape[0] - 1, 0)


def spread_strains(u, v, w):
    value_u, slope_u = u[0] + u[1] + 6.0 * u[2], u[1] - u[0]
    value_v, slope_v = v[0] + v[1] + 6.0 * v[2], v[1] - v[0]
    both_w = w[0] + w[1]
    value_w, slope_w, curve_w = both_w + 6.0 * w[2], w[1] - w[0], both_w - 2.0 * w[2]
    b, a = x_pair(value_u)
    e0 = a - b
    hoop = slope_v + 0.0625 * value_w
    b, a = x_pair(hoop)
    e1 = b + a + 6.0 * hoop
    b = pltpu.roll(slope_u - value_v, 1, 0)
    a = pltpu.roll(slope_u + value_v, slope_u.shape[0] - 1, 0)
    e2 = b + a + 6.0 * slope_u
    b, a = x_pair(value_w)
    e3 = b + a - 2.0 * value_w
    b, a = x_pair(curve_w)
    e4 = b + a + 6.0 * curve_w
    b, a = x_pair(slope_w)
    e5 = a - b
    return e0, e1, e2, e3, e4, e5


def spread_forces(s):
    b, a = x_pair(s[0])
    lean_u = b - a
    b, a = x_pair(s[2])
    lean_v = b - a
    turn_u = b + a + 6.0 * s[2]
    b, a = x_pair(s[1])
    turn_v = b + a + 6.0 * s[1]
    b, a = x_pair(s[3])
    lean_w = 0.0625 * turn_v + (b + a - 2.0 * s[3])
    b, a = x_pair(s[4])
    bent_w = b + a + 6.0 * s[4]
    b, a = x_pair(s[5])
    turn_w = a - b
    sum_w = lean_w + bent_w
    return (
        (lean_u + turn_u, lean_u - turn_u, 6.0 * lean_u),
        (lean_v + turn_v, lean_v - turn_v, 6.0 * lean_v),
        (sum_w - turn_w, sum_w + turn_w, 6.0 * lean_w - 2.0 * bent_w),
    )


def chosen(layers, bits):
    if len(layers) == 1:
        return layers[0]
    half = len(layers) // 2
    return jnp.where(bits[-1], chosen(layers[half:], bits[:-1]), chosen(layers[:half], bits[:-1]))


MARGIN = 2
FIELDS = 8
PADDED = 16


def triples_of(centre, before, after, tile, tiles, first, final):
    at = lanes_of(tile)
    left, right = beside(tile, tiles)
    at_left, at_right = lanes_of(left), lanes_of(right)
    return [
        (
            jnp.where(first, before[c, :, at_left], before[c, :, at]),
            jnp.where(final, after[c, :, at_right], after[c, :, at]),
            centre[c, :, at],
        )
        for c in range(3)
    ]


def mixed(values, e):
    s = [None] * 6
    for n, (a, b) in enumerate(UPPER):
        for p, q in ((a, b), (b, a))[: 1 if a == b else 2]:
            term = values[n] * e[q]
            s[p] = term if s[p] is None else s[p] + term
    return s


def product(left, right):
    return jnp.dot(left, right, preferred_element_type=jnp.float32)


def widened(x):
    return jnp.concatenate([x, jnp.zeros_like(x)], axis=0).astype(jnp.bfloat16)


def learn(x, w_first, w_mid, w_last, keep=None):
    h = jnp.tanh(product(w_first[...], x)).astype(jnp.bfloat16)
    if keep is not None:
        keep(0, h)
    for k in range(w_mid.shape[0]):
        h = jnp.tanh(product(w_mid[k], h)).astype(jnp.bfloat16)
        if keep is not None:
            keep(k + 1, h)
    return product(w_last[...], h)[:FIELDS]


def pieces_of(cols):
    step = cols
    while step > 1024 and step % 256 == 0:
        step //= 2
    return [(at, step) for at in range(0, cols, step)]


def gathered(array, row, spread, at, size):
    tiles = range(at // LANES, (at + size) // LANES)
    return jnp.concatenate(
        [array[t, pl.ds(row, FIELDS, stride=spread), :] for t in tiles], axis=1
    )


def learn_line(row, line, strain, learned, spread, cols, weights, hidden, inputs):
    for at, size in pieces_of(cols):
        x = widened(gathered(strain, row, spread, at, size))
        keep = None
        if line is not None:
            where = line * cols + at
            if not isinstance(where, int):
                where = pl.multiple_of(where, LANES)
            inputs[:, pl.ds(where, size)] = x

            def keep(k, h, where=where, size=size):
                hidden[k, :, pl.ds(where, size)] = h

        out = learn(x, *weights, keep)
        for n in range(size // LANES):
            piece = out[:, n * LANES : (n + 1) * LANES]
            learned[at // LANES + n, pl.ds(row, FIELDS, stride=spread), :] = piece


def learn_rims(rows, strain, learned, spread, cols, weights):
    rim = cols // LANES
    x = [strain[rim, pl.ds(row, FIELDS, stride=spread), :] for row in rows]
    out = learn(widened(jnp.concatenate(x, axis=1)), *weights)
    for n, row in enumerate(rows):
        learned[rim, pl.ds(row, FIELDS, stride=spread), :] = out[:, n * LANES : (n + 1) * LANES]


def inner_kernel(
    fields, w_first, w_mid, w_last, learned, hidden, inputs, before, after, strain
):
    rows, wide = fields.shape[1], fields.shape[2]
    tiles = wide // LANES
    cols = wide - LANES
    lane = lax.broadcasted_iota(jnp.int32, (rows, LANES), 1)
    first, final = lane == 0, lane == LANES - 1

    def set_up(tile, carry):
        at = lanes_of(tile)
        for c in range(3):
            value = fields[c, :, at]
            before[c, :, at] = pltpu.roll(value, 1, 1)
            after[c, :, at] = pltpu.roll(value, LANES - 1, 1)
        return carry

    lax.fori_loop(0, tiles, set_up, 0)

    def strains(tile, carry):
        at = lanes_of(tile)
        e = spread_strains(*triples_of(fields.at[0:3], before, after, tile, tiles, first, final))
        for n in range(FIELDS):
            value = HALVING[n] * e[n] if n < 6 else jnp.zeros((rows, LANES), jnp.float32)
            strain[tile, n * rows : (n + 1) * rows] = value
        return carry

    lax.fori_loop(0, tiles, strains, 0)
    weights = (w_first, w_mid, w_last)

    def line(row, carry):
        learn_line(row, row - 1, strain, learned, rows, cols, weights, hidden, inputs)
        return carry

    lax.fori_loop(1, rows - 1, line, 0)
    learn_rims(range(1, rows - 1), strain, learned, rows, cols, weights)


def outer_kernel(
    table, fields, up, down, fl_up, fl_down, inner, w_first, w_mid, w_last,
    residual, own_residual, stiff, support, hidden, inputs,
    centre, before, after, ahead, behind, middle, strain, learned,
):
    layups = table.shape[0] // 36
    rows, wide = fields.shape[1], fields.shape[2]
    tiles = wide // LANES
    cols = wide - LANES
    tall = 3 * rows
    halo = fl_up.shape[1]
    lane = lax.broadcasted_iota(jnp.int32, (tall, LANES), 1)
    first, final = lane == 0, lane == LANES - 1
    depth = 1
    while (1 << depth) < layups:
        depth += 1
    rim = jnp.zeros((rows - MARGIN, LANES), jnp.float32)
    edge = jnp.zeros((rows - halo, LANES), jnp.float32)

    def set_up(tile, carry):
        at = lanes_of(tile)
        for c in range(3):
            value = jnp.concatenate(
                [rim, up[c, :, at], fields[c, :, at], down[c, :, at], rim], axis=0
            )
            centre[c, :, at] = value
            before[c, :, at] = pltpu.roll(value, 1, 1)
            after[c, :, at] = pltpu.roll(value, LANES - 1, 1)
        around = [
            jnp.concatenate(
                [edge, fl_up[c, :, at], fields[3 + c, :, at], fl_down[c, :, at], edge], axis=0
            )
            for c in range(4)
        ]
        for c in range(3):
            support[c, :, at] = around[c]
        ids = around[3].astype(jnp.int32)
        bits = [(ids & (1 << k)) != 0 for k in range(depth)]
        for n, (a, b) in enumerate(UPPER):
            layers = [table[min(l, layups - 1) * 36 + a * 6 + b] for l in range(1 << depth)]
            stiff[n, :, at] = jnp.broadcast_to(chosen(layers, bits), (tall, LANES))
        return carry

    lax.fori_loop(0, tiles, set_up, 0)

    def strains(tile, carry):
        at = lanes_of(tile)
        e = spread_strains(*triples_of(centre, before, after, tile, tiles, first, final))
        for n in range(FIELDS):
            value = HALVING[n] * e[n] if n < 6 else jnp.zeros((tall, LANES), jnp.float32)
            strain[tile, n * tall : (n + 1) * tall] = value
        for n in range(6):
            learned[tile, n * tall + rows + 1 : n * tall + 2 * rows - 1] = inner[
                tile, n * rows + 1 : (n + 1) * rows - 1
            ]
        return carry

    lax.fori_loop(0, tiles, strains, 0)
    weights = (w_first, w_mid, w_last)
    rim_rows = (rows - 1, rows, 2 * rows - 1, 2 * rows)
    for row, line in zip(rim_rows, (None, 0, 1, None)):
        learn_line(row, line, strain, learned, tall, cols, weights, hidden, inputs)
    learn_rims(rim_rows, strain, learned, tall, cols, weights)

    def push(tile, carry):
        at = lanes_of(tile)
        e = [strain[tile, n * tall : (n + 1) * tall] * (1.0 / HALVING[n]) for n in range(6)]
        s = mixed([stiff[n, :, at] for n in range(len(UPPER))], e)
        s = [s[n] + HALVING[n] * learned[tile, n * tall : (n + 1) * tall] for n in range(6)]
        for c, (alpha, beta, gamma) in enumerate(spread_forces(s)):
            ahead[c, :, at] = pltpu.roll(alpha, 1, 1)
            behind[c, :, at] = pltpu.roll(beta, LANES - 1, 1)
            middle[c, :, at] = gamma
        return carry

    lax.fori_loop(0, tiles, push, 0)
    own = slice(rows, 2 * rows)

    def finish(tile, carry):
        at = lanes_of(tile)
        left, right = beside(tile, tiles)
        at_left, at_right = lanes_of(left), lanes_of(right)
        for c in range(3):
            value = (
                middle[c, own, at]
                + jnp.where(first[:rows], ahead[c, own, at_left], ahead[c, own, at])
                + jnp.where(final[:rows], behind[c, own, at_right], behind[c, own, at])
            )
            value = value + fields[3 + c, :, at] * fields[c, :, at] - fields[7 + c, :, at]
            residual[c, :, at] = value
            if carry is not None:
                own_residual[c, :, at] = value
        return carry

    lax.fori_loop(0, tiles - 1, finish, 0)
    finish(tiles - 1, None)


def outer(left, right):
    return lax.dot_general(
        left, right, (((1,), (1,)), ((), ())), preferred_element_type=jnp.float32
    )


def slope_of(signal, h):
    h = h.astype(jnp.float32)
    return (signal * (1.0 - h * h)).astype(jnp.bfloat16)


def backward_kernel(
    upstream, inner_hidden, inner_inputs, outer_hidden, outer_inputs, w_mid_t, w_last_t,
    packed, grads,
):
    layers = w_mid_t.shape[0]
    hid = w_mid_t.shape[1]
    cols = upstream.shape[0] * LANES
    rows = upstream.shape[1] // FIELDS
    last_at = layers * hid
    first_at = last_at + FIELDS
    grads[...] = jnp.zeros_like(grads)

    def line(row, at_line, hidden, inputs):
        for at, size in pieces_of(cols):
            where = at_line * cols + at
            if not isinstance(where, int):
                where = pl.multiple_of(where, LANES)
            here = pl.ds(where, size)
            signal = widened(gathered(upstream, row, rows, at, size))
            h = hidden[layers, :, here]
            grads[last_at : last_at + FIELDS] += outer(signal, h)[:FIELDS]
            d = slope_of(product(w_last_t[...], signal), h)
            for k in range(layers - 1, -1, -1):
                h = hidden[k, :, here]
                grads[k * hid : (k + 1) * hid] += outer(d, h)
                d = slope_of(product(w_mid_t[k], d), h)
            grads[first_at : first_at + FIELDS] += outer(inputs[:, here], d)[:FIELDS]

    def inside(row, carry):
        line(row, row - 1, inner_hidden, inner_inputs)
        return carry

    lax.fori_loop(1, rows - 1, inside, 0)
    line(0, 0, outer_hidden, outer_inputs)
    line(rows - 1, 1, outer_hidden, outer_inputs)
    chunk = packed.shape[1]
    for n in range(packed.shape[0]):
        packed[n] = grads[n * chunk : (n + 1) * chunk]


def gather_kernel(parts, total):
    total[...] = jnp.broadcast_to(jnp.sum(parts[...], axis=0, keepdims=True), total.shape)


def deliver_kernel(parts, grad_first, grad_mid, grad_last, flat):
    chunk = parts.shape[1]
    for n in range(parts.shape[0]):
        flat[n * chunk : (n + 1) * chunk] = parts[n]
    layers, hid = grad_mid.shape[0], grad_mid.shape[1]
    for k in range(layers):
        grad_mid[k] = flat[k * hid : (k + 1) * hid]
    at = layers * hid
    grad_last[...] = flat[at : at + FIELDS][: grad_last.shape[0]]
    grad_first[...] = flat[at + FIELDS : at + 2 * FIELDS].T[:, : grad_first.shape[1]]


def krylov_kernel(
    numbers, r_mid, r_up, r_down, stiff, support, basis, sums,
    before, after, ahead, behind, middle,
):
    rows = r_mid.shape[1]
    wide = r_mid.shape[2]
    tiles = wide // LANES
    own_tiles = tiles - 1
    tall = 3 * rows
    lane = lax.broadcasted_iota(jnp.int32, (tall, LANES), 1)
    first, final = lane == 0, lane == LANES - 1
    def place(k, c, at, value):
        basis[k, c, :, at] = value
        before[c, :, at] = pltpu.roll(value, 1, 1)
        after[c, :, at] = pltpu.roll(value, LANES - 1, 1)

    def set_up(tile, carry):
        at = lanes_of(tile)
        for c in range(3):
            value = jnp.concatenate([r_up[c, :, at], r_mid[c, :, at], r_down[c, :, at]], axis=0)
            place(0, c, at, value)
        return carry

    lax.fori_loop(0, tiles, set_up, 0)

    def strain_of(k, tile):
        return spread_strains(*triples_of(basis.at[k], before, after, tile, tiles, first, final))

    def stress_of(e, at):
        return mixed([stiff[n, :, at] for n in range(len(UPPER))], e)

    def mine(value):
        return value[rows : 2 * rows]

    zero = jnp.zeros((rows, LANES), jnp.float32)
    totals = [None] * SUMS

    for k in range(DEGREE):
        def push(tile, carry, k=k):
            at = lanes_of(tile)
            for c, (alpha, beta, gamma) in enumerate(
                spread_forces(stress_of(strain_of(k, tile), at))
            ):
                ahead[c, :, at] = pltpu.roll(alpha, 1, 1)
                behind[c, :, at] = pltpu.roll(beta, LANES - 1, 1)
                middle[c, :, at] = gamma
            return carry

        lax.fori_loop(0, tiles, push, 0)

        centre, width, inverse = numbers[k], numbers[3 + k], numbers[6 + k]
        former = numbers[2 + k]

        def advance(tile, carry, k=k):
            at = lanes_of(tile)
            left, right = beside(tile, tiles)
            at_left, at_right = lanes_of(left), lanes_of(right)
            image, here, following = [], [], []
            for c in range(3):
                vector = basis[k, c, :, at]
                value = (
                    middle[c, :, at]
                    + jnp.where(first, ahead[c, :, at_left], ahead[c, :, at])
                    + jnp.where(final, behind[c, :, at_right], behind[c, :, at])
                    + support[c, :, at] * vector
                )
                step = value - centre * vector
                if k:
                    step = step - former * basis[k - 1, c, :, at]
                step = step * inverse
                place(k + 1, c, at, step)
                image.append(mine(value))
                here.append(mine(vector))
                following.append(mine(step))
            if carry is None:
                return None

            def dot(left_side, right_side):
                return (
                    left_side[0] * right_side[0]
                    + left_side[1] * right_side[1]
                    + left_side[2] * right_side[2]
                )

            def old(m):
                return [basis[m, c, rows : 2 * rows, at] for c in range(3)]

            fresh = []
            origin = here if k == 0 else old(0)
            if k == 0:
                fresh.append(dot(here, here))
            fresh.append(dot(origin, following))
            for j in range(k + 1):
                fresh.append(dot(here if j == k else (origin if j == 0 else old(j)), image))
            if k == DEGREE - 1:
                fresh.append(dot(old(1), following))
                fresh.append(dot(here, following))
                fresh.append(dot(following, following))
            return tuple(p + q for p, q in zip(carry, fresh))

        names = ([0] if k == 0 else []) + [k + 1] + [4 + k * (k + 1) // 2 + j for j in range(k + 1)]
        if k == DEGREE - 1:
            names += [10, 11, 12]
        found = lax.fori_loop(0, own_tiles, advance, (zero,) * len(names))
        advance(own_tiles, None)
        for name, value in zip(names, found):
            totals[name] = value

    def energy(tile, running):
        at = lanes_of(tile)
        e = strain_of(DEGREE, tile)
        e = [mine(value) for value in e]
        for n, (a, b) in enumerate(UPPER):
            term = stiff[n, rows : 2 * rows, at] * e[b] * e[a]
            running = running + (term if a == b else 2.0 * term)
        for c in range(3):
            vector = basis[DEGREE, c, rows : 2 * rows, at]
            running = running + support[c, rows : 2 * rows, at] * vector * vector
        return running

    totals[13] = lax.fori_loop(0, own_tiles, energy, zero)
    place_of = lax.broadcasted_iota(jnp.int32, (1, LANES), 1)
    line = jnp.zeros((1, LANES), jnp.float32)
    for n in range(SUMS):
        total = jnp.sum(jnp.sum(totals[n], axis=0, keepdims=True), axis=1, keepdims=True)
        line = jnp.where(place_of == n, jnp.broadcast_to(total, (1, LANES)), line)
    sums[...] = jnp.broadcast_to(line[None], sums.shape)


def solve_kernel(numbers, sums, basis, adjoint, upstream, combined):
    rows = adjoint.shape[1]
    wide = basis.shape[3]
    tiles = wide // LANES
    own_tiles = tiles - 1
    tall = 3 * rows
    line = jnp.sum(sums[...], axis=0)
    picks = [jnp.broadcast_to(line[:, n : n + 1], (1, LANES)) for n in range(SUMS)]
    centre = [numbers[k] for k in range(3)]
    width = [numbers[3 + k] for k in range(3)]
    matrix = [[None] * 4 for _ in range(4)]
    for k in range(3):
        for j in range(k + 1):
            matrix[j][k] = picks[4 + k * (k + 1) // 2 + j]
    cross = [picks[3], picks[10], picks[11], picks[12]]
    for j in range(3):
        value = width[j] * cross[j + 1] + centre[j] * cross[j]
        matrix[j][3] = value + width[j - 1] * cross[j - 1] if j else value
    matrix[3][3] = picks[13]
    weights = [jnp.broadcast_to(x, (tall, LANES)) for x in galerkin(matrix, picks[:4])]

    def combine(tile, carry):
        at = lanes_of(tile)
        for c in range(3):
            value = weights[0] * basis[0, c, :, at]
            for k in range(1, DEGREE + 1):
                value = value + weights[k] * basis[k, c, :, at]
            combined[c, :, at] = value
            combined[3 + c, :, at] = pltpu.roll(value, 1, 1)
            combined[6 + c, :, at] = pltpu.roll(value, LANES - 1, 1)
        return carry

    lax.fori_loop(0, tiles, combine, 0)
    lane = lax.broadcasted_iota(jnp.int32, (tall, LANES), 1)
    first, final = lane == 0, lane == LANES - 1

    def strain(tile, carry):
        at = lanes_of(tile)
        triples = triples_of(
            combined.at[0:3], combined.at[3:6], combined.at[6:9], tile, tiles, first, final
        )
        for c in range(3):
            adjoint[c, :, at] = combined[c, rows : 2 * rows, at]
        for n, value in enumerate(spread_strains(*triples)):
            upstream[tile, n * rows : (n + 1) * rows] = HALVING[n] * value[rows : 2 * rows]
        for n in range(6, FIELDS):
            upstream[tile, n * rows : (n + 1) * rows] = jnp.zeros((rows, LANES), jnp.float32)
        return carry

    lax.fori_loop(0, own_tiles, strain, 0)


def basis_constants(layup_stiffness):
    bending = 0.5 * (jnp.mean(layup_stiffness[:, 3, 3]) + jnp.mean(layup_stiffness[:, 4, 4]))
    centres = [11.5 * bending + 1.1, 9.8 * bending + 1.1, 8.4 * bending + 1.1]
    widths = [3.9 * bending + 0.4, 5.6 * bending + 0.4, 4.8 * bending + 0.4]
    return centres, widths


ON_CHIP = pl.BlockSpec(memory_space=pltpu.VMEM)
SCALARS = pl.BlockSpec(memory_space=pltpu.SMEM)


def kernel_call(body, name, scalars, outs, scratch, *operands):
    return pl.pallas_call(
        body,
        name=name,
        in_specs=[SCALARS] * scalars + [ON_CHIP] * (len(operands) - scalars),
        out_specs=[ON_CHIP] * len(outs),
        out_shape=[jax.ShapeDtypeStruct(*out) for out in outs],
        scratch_shapes=[pltpu.VMEM(*s) for s in scratch],
        compiler_params=pltpu.CompilerParams(vmem_limit_bytes=LIMITS[name] << 20),
    )(*operands)


LIMITS = {"inner": 8, "outer": 14, "krylov": 10, "solve": 10, "backward": 8, "gather": 4, "deliver": 4}


def per_device(displacement, load, foundation, layup, layup_stiffness, w_first, w_mid, w_last):
    f32, bf16 = jnp.float32, jnp.bfloat16
    rows, cols = layup.shape
    layers, hid = w_mid.shape[0], w_mid.shape[1]
    devices = lax.axis_size("patch") * lax.axis_size("sub")
    wide = cols + LANES
    tall = 3 * rows
    tiles = wide // LANES
    fields = jnp.concatenate([displacement, foundation, layup.astype(f32)[None], load])
    before, after = from_both(fields, "sub", 2, HY)
    gap = jnp.zeros(fields.shape[:2] + (LANES - 2 * HY,), f32)
    fields = jnp.concatenate([fields, after, gap, before], axis=2)
    up, down = from_both(fields[:3], "patch", 1, MARGIN)
    fl_up, fl_down = from_both(fields[3:7], "patch", 1, 6)

    halving = jnp.array(HALVING, f32)
    table = (layup_stiffness * halving[:, None] * halving[None, :]).reshape(-1)
    centres, widths = basis_constants(layup_stiffness)
    numbers = jnp.stack(centres + widths + [1.0 / x for x in widths])
    thin = w_first.shape[1]
    first_pad = jnp.pad(w_first, ((0, 0), (0, PADDED - thin)))
    last_pad = jnp.pad(w_last, ((0, PADDED - thin), (0, 0)))
    mid_t, last_t = jnp.swapaxes(w_mid, 1, 2), last_pad.T

    learned, inner_hidden, inner_inputs = kernel_call(
        inner_kernel, "inner", 0,
        [((tiles, FIELDS * rows, LANES), f32), ((layers + 1, hid, (rows - 2) * cols), bf16),
         ((PADDED, (rows - 2) * cols), bf16)],
        [((3, rows, wide), f32)] * 2 + [((tiles, FIELDS * rows, LANES), f32)],
        fields, first_pad, w_mid, last_pad,
    )
    wide_residual, residual, stiff, support, outer_hidden, outer_inputs = kernel_call(
        outer_kernel, "outer", 1,
        [((3, rows, wide), f32), ((3, rows, cols), f32), ((len(UPPER), tall, wide), f32),
         ((3, tall, wide), f32), ((layers + 1, hid, 2 * cols), bf16), ((PADDED, 2 * cols), bf16)],
        [((3, tall, wide), f32)] * 6 + [((tiles, FIELDS * tall, LANES), f32)] * 2,
        table, fields, up, down, fl_up, fl_down, learned, first_pad, w_mid, last_pad,
    )
    up, down = from_both(wide_residual, "patch", 1, rows)
    basis, sums = kernel_call(
        krylov_kernel, "krylov", 1,
        [((DEGREE + 1, 3, tall, wide), f32), ((devices, 1, LANES), f32)],
        [((3, tall, wide), f32)] * 5,
        numbers, wide_residual, up, down, stiff, support,
    )
    sums = everyone(sums)
    adjoint, upstream = kernel_call(
        solve_kernel, "solve", 1,
        [((3, rows, cols), f32), ((tiles - 1, FIELDS * rows, LANES), f32)],
        [((9, tall, wide), f32)],
        numbers, sums, basis,
    )
    count = layers * hid + 2 * FIELDS
    chunk = -(-count // devices)
    (packed,) = kernel_call(
        backward_kernel, "backward", 0,
        [((devices, chunk, LANES), f32)],
        [((devices * chunk, LANES), f32)],
        upstream, inner_hidden, inner_inputs, outer_hidden, outer_inputs, mid_t, last_t,
    )
    (total,) = kernel_call(
        gather_kernel, "gather", 0, [(packed.shape, f32)], [], everyone(packed)
    )
    grad_first, grad_mid, grad_last = kernel_call(
        deliver_kernel, "deliver", 0,
        [(w_first.shape, f32), (w_mid.shape, f32), (w_last.shape, f32)],
        [((devices * chunk, LANES), f32)],
        everyone(total),
    )
    return residual, adjoint, grad_first, grad_mid, grad_last


def solution(mesh):
    field = P(None, "patch", "sub")
    return jax.shard_map(
        per_device,
        mesh=mesh,
        in_specs=(field, field, field, P("patch", "sub"), P(), P(), P(), P()),
        out_specs=(field, field, P(), P(), P()),
        check_vma=False,
    )
```

```python
import jax
import jax.numpy as jnp
from jax import lax
from jax.experimental import pallas as pl
from jax.experimental.pallas import tpu as pltpu
from jax.sharding import PartitionSpec as P

HY = 16
LANES = 128
AXES = ("patch", "sub")


def ring(axis, step):
    count = lax.axis_size(axis)
    return [(i, (i + step) % count) for i in range(count)]


def from_both(array, axis, dim, width):
    size = array.shape[dim]
    tail = lax.slice_in_dim(array, size - width, size, axis=dim)
    head = lax.slice_in_dim(array, 0, width, axis=dim)
    before = lax.ppermute(tail, axis, ring(axis, 1))
    after = lax.ppermute(head, axis, ring(axis, -1))
    return before, after


def everyone(rows):
    return lax.all_to_all(rows, AXES, 0, 0, tiled=True)


def galerkin(matrix, target):
    size = len(target)
    matrix = [list(row) for row in matrix]
    target = list(target)
    scale = [matrix[i][i] for i in range(size)]
    inverse = []
    for i in range(size):
        pivot = matrix[i][i]
        usable = pivot > 1e-6 * scale[i]
        inverse.append(jnp.where(usable, 1.0 / jnp.where(usable, pivot, 1.0), 0.0))
        for j in range(i + 1, size):
            factor = matrix[i][j] * inverse[i]
            for k in range(j, size):
                matrix[j][k] = matrix[j][k] - factor * matrix[i][k]
            target[j] = target[j] - factor * target[i]
    answer = [None] * size
    for i in reversed(range(size)):
        running = target[i]
        for j in range(i + 1, size):
            running = running - matrix[i][j] * answer[j]
        answer[i] = running * inverse[i]
    return answer


DEGREE = 3
UPPER = [(a, b) for a in range(6) for b in range(a, 6)]
HALVING = (0.0625, 0.0625, 0.0625, -0.125, -0.125, -0.5)
SUMS = 14


def lanes_of(tile):
    if isinstance(tile, int):
        return pl.ds(tile * LANES, LANES)
    return pl.ds(pl.multiple_of(tile * LANES, LANES), LANES)


def beside(tile, tiles):
    if isinstance(tile, int):
        return (tile - 1) % tiles, (tile + 1) % tiles
    return jnp.where(tile == 0, tiles - 1, tile - 1), jnp.where(tile == tiles - 1, 0, tile + 1)


def x_pair(f):
    return pltpu.roll(f, 1, 0), pltpu.roll(f, f.shape[0] - 1, 0)


def spread_strains(u, v, w):
    value_u, slope_u = u[0] + u[1] + 6.0 * u[2], u[1] - u[0]
    value_v, slope_v = v[0] + v[1] + 6.0 * v[2], v[1] - v[0]
    both_w = w[0] + w[1]
    value_w, slope_w, curve_w = both_w + 6.0 * w[2], w[1] - w[0], both_w - 2.0 * w[2]
    b, a = x_pair(value_u)
    e0 = a - b
    hoop = slope_v + 0.0625 * value_w
    b, a = x_pair(hoop)
    e1 = b + a + 6.0 * hoop
    b = pltpu.roll(slope_u - value_v, 1, 0)
    a = pltpu.roll(slope_u + value_v, slope_u.shape[0] - 1, 0)
    e2 = b + a + 6.0 * slope_u
    b, a = x_pair(value_w)
    e3 = b + a - 2.0 * value_w
    b, a = x_pair(curve_w)
    e4 = b + a + 6.0 * curve_w
    b, a = x_pair(slope_w)
    e5 = a - b
    return e0, e1, e2, e3, e4, e5


def spread_forces(s):
    b, a = x_pair(s[0])
    lean_u = b - a
    b, a = x_pair(s[2])
    lean_v = b - a
    turn_u = b + a + 6.0 * s[2]
    b, a = x_pair(s[1])
    turn_v = b + a + 6.0 * s[1]
    b, a = x_pair(s[3])
    lean_w = 0.0625 * turn_v + (b + a - 2.0 * s[3])
    b, a = x_pair(s[4])
    bent_w = b + a + 6.0 * s[4]
    b, a = x_pair(s[5])
    turn_w = a - b
    sum_w = lean_w + bent_w
    return (
        (lean_u + turn_u, lean_u - turn_u, 6.0 * lean_u),
        (lean_v + turn_v, lean_v - turn_v, 6.0 * lean_v),
        (sum_w - turn_w, sum_w + turn_w, 6.0 * lean_w - 2.0 * bent_w),
    )


def chosen(layers, bits):
    if len(layers) == 1:
        return layers[0]
    half = len(layers) // 2
    return jnp.where(bits[-1], chosen(layers[half:], bits[:-1]), chosen(layers[:half], bits[:-1]))


MARGIN = 2
FIELDS = 8
PADDED = 16


def triples_of(centre, before, after, tile, tiles, first, final):
    at = lanes_of(tile)
    left, right = beside(tile, tiles)
    at_left, at_right = lanes_of(left), lanes_of(right)
    return [
        (
            jnp.where(first, before[c, :, at_left], before[c, :, at]),
            jnp.where(final, after[c, :, at_right], after[c, :, at]),
            centre[c, :, at],
        )
        for c in range(3)
    ]


def mixed(values, e):
    s = [None] * 6
    for n, (a, b) in enumerate(UPPER):
        for p, q in ((a, b), (b, a))[: 1 if a == b else 2]:
            term = values[n] * e[q]
            s[p] = term if s[p] is None else s[p] + term
    return s


def contract(left, right, left_dim, right_dim):
    return lax.dot_general(
        left, right, (((left_dim,), (right_dim,)), ((), ())), preferred_element_type=jnp.float32
    )


def widened(x):
    return jnp.concatenate([x, jnp.zeros_like(x)], axis=0).astype(jnp.bfloat16)


def learn(x, w_first, w_mid, w_last, keep=None):
    h = jnp.tanh(contract(x, w_first[...], 0, 1)).astype(jnp.bfloat16)
    if keep is not None:
        keep(0, h)
    for k in range(w_mid.shape[0]):
        h = jnp.tanh(contract(h, w_mid[k], 1, 1)).astype(jnp.bfloat16)
        if keep is not None:
            keep(k + 1, h)
    return contract(w_last[...], h, 1, 1)[:FIELDS]


def pieces_of(cols):
    step = cols
    while step > 2048 and step % 256 == 0:
        step //= 2
    return [(at, step) for at in range(0, cols, step)]


def gathered(array, row, spread, at, size):
    tiles = range(at // LANES, (at + size) // LANES)
    return jnp.concatenate(
        [array[t, pl.ds(row, FIELDS, stride=spread), :] for t in tiles], axis=1
    )


def learn_line(row, line, strain, learned, spread, cols, weights, hidden, inputs):
    for at, size in pieces_of(cols):
        x = widened(gathered(strain, row, spread, at, size))
        keep = None
        if line is not None:
            where = line * cols + at
            if not isinstance(where, int):
                where = pl.multiple_of(where, LANES)
            inputs[:, pl.ds(where, size)] = x

            def keep(k, h, where=where, size=size):
                hidden[k, pl.ds(where, size), :] = h

        out = learn(x, *weights, keep)
        for n in range(size // LANES):
            piece = out[:, n * LANES : (n + 1) * LANES]
            learned[at // LANES + n, pl.ds(row, FIELDS, stride=spread), :] = piece


def learn_rims(rows, strain, learned, spread, cols, weights):
    rim = cols // LANES
    x = [strain[rim, pl.ds(row, FIELDS, stride=spread), :] for row in rows]
    out = learn(widened(jnp.concatenate(x, axis=1)), *weights)
    for n, row in enumerate(rows):
        learned[rim, pl.ds(row, FIELDS, stride=spread), :] = out[:, n * LANES : (n + 1) * LANES]


def line_copy(line, cols, source, target, flags):
    where = line * cols
    if not isinstance(where, int):
        where = pl.multiple_of(where, LANES)
    here = pl.ds(where, cols)
    return pltpu.make_async_copy(source.at[:, here, :], target.at[:, here, :], flags.at[line])


def inner_kernel(
    fields, w_first, w_mid, w_last, learned, stored, inputs, before, after, strain, hidden, flags
):
    rows, wide = fields.shape[1], fields.shape[2]
    tiles = wide // LANES
    cols = wide - LANES
    lane = lax.broadcasted_iota(jnp.int32, (rows, LANES), 1)
    first, final = lane == 0, lane == LANES - 1

    def set_up(tile, carry):
        at = lanes_of(tile)
        for c in range(3):
            value = fields[c, :, at]
            before[c, :, at] = pltpu.roll(value, 1, 1)
            after[c, :, at] = pltpu.roll(value, LANES - 1, 1)
        return carry

    lax.fori_loop(0, tiles, set_up, 0)

    def strains(tile, carry):
        at = lanes_of(tile)
        e = spread_strains(*triples_of(fields.at[0:3], before, after, tile, tiles, first, final))
        for n in range(FIELDS):
            value = HALVING[n] * e[n] if n < 6 else jnp.zeros((rows, LANES), jnp.float32)
            strain[tile, n * rows : (n + 1) * rows] = value
        return carry

    lax.fori_loop(0, tiles, strains, 0)
    weights = (w_first, w_mid, w_last)

    def line(row, carry):
        learn_line(row, row - 1, strain, learned, rows, cols, weights, hidden, inputs)
        line_copy(row - 1, cols, hidden, stored, flags).start()
        return carry

    lax.fori_loop(1, rows - 1, line, 0)
    learn_rims(range(1, rows - 1), strain, learned, rows, cols, weights)
    for n in range(rows - 2):
        line_copy(n, cols, hidden, stored, flags).wait()


def stiffness_of(table, ids, depth, target, at):
    layups = table.shape[0] // 36
    bits = [(ids & (1 << k)) != 0 for k in range(depth)]
    for n, (a, b) in enumerate(UPPER):
        layers = [table[min(l, layups - 1) * 36 + a * 6 + b] for l in range(1 << depth)]
        target[n, :, at] = jnp.broadcast_to(chosen(layers, bits), ids.shape)


def depth_of(table):
    depth = 1
    while (1 << depth) < table.shape[0] // 36:
        depth += 1
    return depth


def prepare_kernel(table, fields, fl_up, fl_down, stiff, support):
    rows, wide = fields.shape[1], fields.shape[2]
    halo = fl_up.shape[1]
    edge = jnp.zeros((rows - halo, LANES), jnp.float32)

    def fill(tile, carry):
        at = lanes_of(tile)
        around = [
            jnp.concatenate(
                [edge, fl_up[c, :, at], fields[3 + c, :, at], fl_down[c, :, at], edge], axis=0
            )
            for c in range(4)
        ]
        for c in range(3):
            support[c, :, at] = around[c]
        stiffness_of(table, around[3].astype(jnp.int32), depth_of(table), stiff, at)
        return carry

    lax.fori_loop(0, wide // LANES, fill, 0)


def outer_kernel(
    table, fields, up, down, inner, w_first, w_mid, w_last,
    residual, own_residual, stored, inputs,
    centre, before, after, ahead, behind, middle, strain, learned, stiff, hidden, flags,
):
    rows, wide = fields.shape[1], fields.shape[2]
    tiles = wide // LANES
    cols = wide - LANES
    tall = 3 * rows
    lane = lax.broadcasted_iota(jnp.int32, (tall, LANES), 1)
    first, final = lane == 0, lane == LANES - 1
    rim = jnp.zeros((rows - MARGIN, LANES), jnp.float32)
    last = 3 * MARGIN

    def set_up(tile, carry):
        at = lanes_of(tile)
        for c in range(3):
            above, below = up[MARGIN * c : MARGIN * (c + 1), at], down[MARGIN * c : MARGIN * (c + 1), at]
            value = jnp.concatenate([rim, above, fields[c, :, at], below, rim], axis=0)
            centre[c, :, at] = value
            before[c, :, at] = pltpu.roll(value, 1, 1)
            after[c, :, at] = pltpu.roll(value, LANES - 1, 1)
        wall = jnp.zeros((rows - 1, LANES), jnp.float32)
        ids = jnp.concatenate(
            [wall, up[last : last + 1, at], fields[6, :, at], down[last : last + 1, at], wall],
            axis=0,
        ).astype(jnp.int32)
        stiffness_of(table, ids, depth_of(table), stiff, at)
        return carry

    lax.fori_loop(0, tiles, set_up, 0)

    def strains(tile, carry):
        at = lanes_of(tile)
        e = spread_strains(*triples_of(centre, before, after, tile, tiles, first, final))
        for n in range(FIELDS):
            value = HALVING[n] * e[n] if n < 6 else jnp.zeros((tall, LANES), jnp.float32)
            strain[tile, n * tall : (n + 1) * tall] = value
        for n in range(6):
            learned[tile, n * tall + rows + 1 : n * tall + 2 * rows - 1] = inner[
                tile, n * rows + 1 : (n + 1) * rows - 1
            ]
        return carry

    lax.fori_loop(0, tiles, strains, 0)
    weights = (w_first, w_mid, w_last)
    rim_rows = (rows - 1, rows, 2 * rows - 1, 2 * rows)
    for row, line in zip(rim_rows, (None, 0, 1, None)):
        learn_line(row, line, strain, learned, tall, cols, weights, hidden, inputs)
        if line is not None:
            line_copy(line, cols, hidden, stored, flags).start()
    learn_rims(rim_rows, strain, learned, tall, cols, weights)

    def push(tile, carry):
        at = lanes_of(tile)
        e = [strain[tile, n * tall : (n + 1) * tall] * (1.0 / HALVING[n]) for n in range(6)]
        s = mixed([stiff[n, :, at] for n in range(len(UPPER))], e)
        s = [s[n] + HALVING[n] * learned[tile, n * tall : (n + 1) * tall] for n in range(6)]
        for c, (alpha, beta, gamma) in enumerate(spread_forces(s)):
            ahead[c, :, at] = pltpu.roll(alpha, 1, 1)
            behind[c, :, at] = pltpu.roll(beta, LANES - 1, 1)
            middle[c, :, at] = gamma
        return carry

    lax.fori_loop(0, tiles, push, 0)
    own = slice(rows, 2 * rows)

    def finish(tile, carry):
        at = lanes_of(tile)
        left, right = beside(tile, tiles)
        at_left, at_right = lanes_of(left), lanes_of(right)
        for c in range(3):
            value = (
                middle[c, own, at]
                + jnp.where(first[:rows], ahead[c, own, at_left], ahead[c, own, at])
                + jnp.where(final[:rows], behind[c, own, at_right], behind[c, own, at])
            )
            value = value + fields[3 + c, :, at] * fields[c, :, at] - fields[7 + c, :, at]
            residual[c, :, at] = value
            if carry is not None:
                own_residual[c, :, at] = value
        return carry

    lax.fori_loop(0, tiles - 1, finish, 0)
    finish(tiles - 1, None)
    for n in range(2):
        line_copy(n, cols, hidden, stored, flags).wait()


def solve(numbers, sums, basis, adjoint, upstream, combined):
    rows = adjoint.shape[1]
    wide = basis.shape[3]
    tiles = wide // LANES
    own_tiles = tiles - 1
    tall = 3 * rows
    line = jnp.sum(sums[...], axis=0)
    picks = [jnp.broadcast_to(line[:, n : n + 1], (1, LANES)) for n in range(SUMS)]
    centre = [numbers[k] for k in range(3)]
    width = [numbers[3 + k] for k in range(3)]
    matrix = [[None] * 4 for _ in range(4)]
    for k in range(3):
        for j in range(k + 1):
            matrix[j][k] = picks[4 + k * (k + 1) // 2 + j]
    cross = [picks[3], picks[10], picks[11], picks[12]]
    for j in range(3):
        value = width[j] * cross[j + 1] + centre[j] * cross[j]
        matrix[j][3] = value + width[j - 1] * cross[j - 1] if j else value
    matrix[3][3] = picks[13]
    weights = [jnp.broadcast_to(x, (tall, LANES)) for x in galerkin(matrix, picks[:4])]

    def combine(tile, carry):
        at = lanes_of(tile)
        for c in range(3):
            value = weights[0] * basis[0, c, :, at]
            for k in range(1, DEGREE + 1):
                value = value + weights[k] * basis[k, c, :, at]
            combined[c, :, at] = value
            combined[3 + c, :, at] = pltpu.roll(value, 1, 1)
            combined[6 + c, :, at] = pltpu.roll(value, LANES - 1, 1)
        return carry

    lax.fori_loop(0, tiles, combine, 0)
    lane = lax.broadcasted_iota(jnp.int32, (tall, LANES), 1)
    first, final = lane == 0, lane == LANES - 1

    def strain(tile, carry):
        at = lanes_of(tile)
        triples = triples_of(
            combined.at[0:3], combined.at[3:6], combined.at[6:9], tile, tiles, first, final
        )
        for c in range(3):
            adjoint[c, :, at] = combined[c, rows : 2 * rows, at]
        for n, value in enumerate(spread_strains(*triples)):
            upstream[tile, n * rows : (n + 1) * rows] = HALVING[n] * value[rows : 2 * rows]
        for n in range(6, FIELDS):
            upstream[tile, n * rows : (n + 1) * rows] = jnp.zeros((rows, LANES), jnp.float32)
        return carry

    lax.fori_loop(0, own_tiles, strain, 0)


def slope_of(signal, h):
    h = h.astype(jnp.float32)
    return (signal * (1.0 - h * h)).astype(jnp.bfloat16)


def backward_kernel(
    numbers, sums, basis, inner_hidden, inner_inputs, outer_hidden, outer_inputs, w_mid, w_last,
    adjoint, packed,
    combined, upstream, grads, near_hidden, far_hidden, near_flags, far_flags,
):
    layers = w_mid.shape[0]
    hid = w_mid.shape[1]
    cols = upstream.shape[0] * LANES
    rows = upstream.shape[1] // FIELDS
    last_at = layers * hid
    first_at = last_at + FIELDS
    for n in range(rows - 2):
        line_copy(n, cols, inner_hidden, near_hidden, near_flags).start()
    for n in range(2):
        line_copy(n, cols, outer_hidden, far_hidden, far_flags).start()
    grads[...] = jnp.zeros_like(grads)
    solve(numbers, sums, basis, adjoint, upstream, combined)

    def line(row, at_line, hidden, inputs):
        for at, size in pieces_of(cols):
            where = at_line * cols + at
            if not isinstance(where, int):
                where = pl.multiple_of(where, LANES)
            here = pl.ds(where, size)
            signal = widened(gathered(upstream, row, rows, at, size))
            h = hidden[layers, here, :]
            grads[last_at : last_at + FIELDS] += contract(signal, h, 1, 0)[:FIELDS]
            d = slope_of(contract(signal, w_last[...], 0, 0), h)
            for k in range(layers - 1, -1, -1):
                h = hidden[k, here, :]
                grads[k * hid : (k + 1) * hid] += contract(d, h, 0, 0)
                d = slope_of(contract(d, w_mid[k], 1, 0), h)
            grads[first_at : first_at + FIELDS] += contract(inputs[:, here], d, 1, 0)[:FIELDS]

    def inside(row, carry):
        line_copy(row - 1, cols, inner_hidden, near_hidden, near_flags).wait()
        line(row, row - 1, near_hidden, inner_inputs)
        return carry

    lax.fori_loop(1, rows - 1, inside, 0)
    for n, row in enumerate((0, rows - 1)):
        line_copy(n, cols, outer_hidden, far_hidden, far_flags).wait()
        line(row, n, far_hidden, outer_inputs)
    chunk = packed.shape[1]
    for n in range(packed.shape[0]):
        packed[n] = grads[n * chunk : (n + 1) * chunk]


def gather_kernel(parts, total):
    total[...] = jnp.broadcast_to(jnp.sum(parts[...], axis=0, keepdims=True), total.shape)


def deliver_kernel(parts, grad_first, grad_mid, grad_last, flat):
    chunk = parts.shape[1]
    for n in range(parts.shape[0]):
        flat[n * chunk : (n + 1) * chunk] = parts[n]
    layers, hid = grad_mid.shape[0], grad_mid.shape[1]
    for k in range(layers):
        grad_mid[k] = flat[k * hid : (k + 1) * hid]
    at = layers * hid
    grad_last[...] = flat[at : at + FIELDS][: grad_last.shape[0]]
    grad_first[...] = flat[at + FIELDS : at + 2 * FIELDS].T[:, : grad_first.shape[1]]


def krylov_kernel(
    numbers, r_mid, r_up, r_down, stiff, support, basis, sums,
    before, after, ahead, behind, middle,
):
    rows = r_mid.shape[1]
    wide = r_mid.shape[2]
    tiles = wide // LANES
    own_tiles = tiles - 1
    tall = 3 * rows
    lane = lax.broadcasted_iota(jnp.int32, (tall, LANES), 1)
    first, final = lane == 0, lane == LANES - 1
    def place(k, c, at, value):
        basis[k, c, :, at] = value
        before[c, :, at] = pltpu.roll(value, 1, 1)
        after[c, :, at] = pltpu.roll(value, LANES - 1, 1)

    def set_up(tile, carry):
        at = lanes_of(tile)
        for c in range(3):
            value = jnp.concatenate([r_up[c, :, at], r_mid[c, :, at], r_down[c, :, at]], axis=0)
            place(0, c, at, value)
        return carry

    lax.fori_loop(0, tiles, set_up, 0)

    def strain_of(k, tile):
        return spread_strains(*triples_of(basis.at[k], before, after, tile, tiles, first, final))

    def stress_of(e, at):
        return mixed([stiff[n, :, at] for n in range(len(UPPER))], e)

    def mine(value):
        return value[rows : 2 * rows]

    zero = jnp.zeros((rows, LANES), jnp.float32)
    totals = [None] * SUMS

    for k in range(DEGREE):
        def push(tile, carry, k=k):
            at = lanes_of(tile)
            for c, (alpha, beta, gamma) in enumerate(
                spread_forces(stress_of(strain_of(k, tile), at))
            ):
                ahead[c, :, at] = pltpu.roll(alpha, 1, 1)
                behind[c, :, at] = pltpu.roll(beta, LANES - 1, 1)
                middle[c, :, at] = gamma
            return carry

        lax.fori_loop(0, tiles, push, 0)

        centre, width, inverse = numbers[k], numbers[3 + k], numbers[6 + k]
        former = numbers[2 + k]

        def advance(tile, carry, k=k):
            at = lanes_of(tile)
            left, right = beside(tile, tiles)
            at_left, at_right = lanes_of(left), lanes_of(right)
            image, here, following = [], [], []
            for c in range(3):
                vector = basis[k, c, :, at]
                value = (
                    middle[c, :, at]
                    + jnp.where(first, ahead[c, :, at_left], ahead[c, :, at])
                    + jnp.where(final, behind[c, :, at_right], behind[c, :, at])
                    + support[c, :, at] * vector
                )
                step = value - centre * vector
                if k:
                    step = step - former * basis[k - 1, c, :, at]
                step = step * inverse
                place(k + 1, c, at, step)
                image.append(mine(value))
                here.append(mine(vector))
                following.append(mine(step))
            if carry is None:
                return None

            def dot(left_side, right_side):
                return (
                    left_side[0] * right_side[0]
                    + left_side[1] * right_side[1]
                    + left_side[2] * right_side[2]
                )

            def old(m):
                return [basis[m, c, rows : 2 * rows, at] for c in range(3)]

            fresh = []
            origin = here if k == 0 else old(0)
            if k == 0:
                fresh.append(dot(here, here))
            fresh.append(dot(origin, following))
            for j in range(k + 1):
                fresh.append(dot(here if j == k else (origin if j == 0 else old(j)), image))
            if k == DEGREE - 1:
                fresh.append(dot(old(1), following))
                fresh.append(dot(here, following))
                fresh.append(dot(following, following))
            return tuple(p + q for p, q in zip(carry, fresh))

        names = ([0] if k == 0 else []) + [k + 1] + [4 + k * (k + 1) // 2 + j for j in range(k + 1)]
        if k == DEGREE - 1:
            names += [10, 11, 12]
        found = lax.fori_loop(0, own_tiles, advance, (zero,) * len(names))
        advance(own_tiles, None)
        for name, value in zip(names, found):
            totals[name] = value

    def energy(tile, running):
        at = lanes_of(tile)
        e = strain_of(DEGREE, tile)
        e = [mine(value) for value in e]
        for n, (a, b) in enumerate(UPPER):
            term = stiff[n, rows : 2 * rows, at] * e[b] * e[a]
            running = running + (term if a == b else 2.0 * term)
        for c in range(3):
            vector = basis[DEGREE, c, rows : 2 * rows, at]
            running = running + support[c, rows : 2 * rows, at] * vector * vector
        return running

    totals[13] = lax.fori_loop(0, own_tiles, energy, zero)
    place_of = lax.broadcasted_iota(jnp.int32, (1, LANES), 1)
    line = jnp.zeros((1, LANES), jnp.float32)
    for n in range(SUMS):
        total = jnp.sum(jnp.sum(totals[n], axis=0, keepdims=True), axis=1, keepdims=True)
        line = jnp.where(place_of == n, jnp.broadcast_to(total, (1, LANES)), line)
    sums[...] = jnp.broadcast_to(line[None], sums.shape)


def basis_constants(layup_stiffness):
    bending = 0.5 * (jnp.mean(layup_stiffness[:, 3, 3]) + jnp.mean(layup_stiffness[:, 4, 4]))
    centres = [11.5 * bending + 1.1, 9.8 * bending + 1.1, 8.4 * bending + 1.1]
    widths = [3.9 * bending + 0.4, 5.6 * bending + 0.4, 4.8 * bending + 0.4]
    return centres, widths


ON_CHIP = pl.BlockSpec(memory_space=pltpu.VMEM)
SCALARS = pl.BlockSpec(memory_space=pltpu.SMEM)


IN_PLACE = pl.BlockSpec(memory_space=pltpu.HBM)


def kernel_call(body, name, scalars, outs, scratch, *operands, far=(), far_outs=()):
    specs = [SCALARS] * scalars + [ON_CHIP] * (len(operands) - scalars)
    for n in far:
        specs[n] = IN_PLACE
    return pl.pallas_call(
        body,
        name=name,
        in_specs=specs,
        out_specs=[IN_PLACE if n in far_outs else ON_CHIP for n in range(len(outs))],
        out_shape=[jax.ShapeDtypeStruct(*out) for out in outs],
        scratch_shapes=[
            pltpu.VMEM(*s) if isinstance(s, tuple) else pltpu.SemaphoreType.DMA((s,))
            for s in scratch
        ],
        compiler_params=pltpu.CompilerParams(vmem_limit_bytes=LIMITS[name] << 20),
    )(*operands)


LIMITS = {
    "inner": 24, "outer": 24, "prepare": 8, "krylov": 10, "backward": 32, "gather": 4, "deliver": 4,
}


def per_device(displacement, load, foundation, layup, layup_stiffness, w_first, w_mid, w_last):
    f32, bf16 = jnp.float32, jnp.bfloat16
    rows, cols = layup.shape
    layers, hid = w_mid.shape[0], w_mid.shape[1]
    devices = lax.axis_size("patch") * lax.axis_size("sub")
    wide = cols + LANES
    tall = 3 * rows
    tiles = wide // LANES
    fields = jnp.concatenate([displacement, foundation, layup.astype(f32)[None], load])
    before, after = from_both(fields, "sub", 2, HY)
    gap = jnp.zeros(fields.shape[:2] + (LANES - 2 * HY,), f32)
    fields = jnp.concatenate([fields, after, gap, before], axis=2)
    sends = [
        jnp.concatenate([*[fields[c, edge] for c in range(3)], fields[6, edge][near]])
        for edge, near in ((slice(rows - MARGIN, rows), slice(1, 2)), (slice(0, MARGIN), slice(0, 1)))
    ]
    up = lax.ppermute(sends[0], "patch", ring("patch", 1))
    down = lax.ppermute(sends[1], "patch", ring("patch", -1))

    halving = jnp.array(HALVING, f32)
    table = (layup_stiffness * halving[:, None] * halving[None, :]).reshape(-1)
    centres, widths = basis_constants(layup_stiffness)
    numbers = jnp.stack(centres + widths + [1.0 / x for x in widths])
    thin = w_first.shape[1]
    first_pad = jnp.pad(w_first, ((0, 0), (0, PADDED - thin)))
    last_pad = jnp.pad(w_last, ((0, PADDED - thin), (0, 0)))

    learned, inner_hidden, inner_inputs = kernel_call(
        inner_kernel, "inner", 0,
        [((tiles, FIELDS * rows, LANES), f32), ((layers + 1, (rows - 2) * cols, hid), bf16),
         ((PADDED, (rows - 2) * cols), bf16)],
        [((3, rows, wide), f32)] * 2
        + [((tiles, FIELDS * rows, LANES), f32), ((layers + 1, (rows - 2) * cols, hid), bf16),
           rows - 2],
        fields, first_pad, w_mid, last_pad, far_outs=(1,),
    )
    learned, distant = lax.optimization_barrier((learned, fields[3:7]))
    fl_up, fl_down = from_both(distant, "patch", 1, 6)
    wide_residual, residual, outer_hidden, outer_inputs = kernel_call(
        outer_kernel, "outer", 1,
        [((3, rows, wide), f32), ((3, rows, cols), f32),
         ((layers + 1, 2 * cols, hid), bf16), ((PADDED, 2 * cols), bf16)],
        [((3, tall, wide), f32)] * 6
        + [((tiles, FIELDS * tall, LANES), f32)] * 2
        + [((len(UPPER), tall, wide), f32), ((layers + 1, 2 * cols, hid), bf16), 2],
        table, fields, up, down, learned, first_pad, w_mid, last_pad, far_outs=(2,),
    )
    stiff, support = kernel_call(
        prepare_kernel, "prepare", 1,
        [((len(UPPER), tall, wide), f32), ((3, tall, wide), f32)], [],
        table, fields, fl_up, fl_down,
    )
    up, down = from_both(wide_residual, "patch", 1, rows)
    basis, sums = kernel_call(
        krylov_kernel, "krylov", 1,
        [((DEGREE + 1, 3, tall, wide), f32), ((devices, 1, LANES), f32)],
        [((3, tall, wide), f32)] * 5,
        numbers, wide_residual, up, down, stiff, support,
    )
    sums = everyone(sums)
    count = layers * hid + 2 * FIELDS
    chunk = -(-count // devices)
    adjoint, packed = kernel_call(
        backward_kernel, "backward", 1,
        [((3, rows, cols), f32), ((devices, chunk, LANES), f32)],
        [((9, tall, wide), f32), ((tiles - 1, FIELDS * rows, LANES), f32),
         ((devices * chunk, LANES), f32), ((layers + 1, (rows - 2) * cols, hid), bf16),
         ((layers + 1, 2 * cols, hid), bf16), rows - 2, 2],
        numbers, sums, basis, inner_hidden, inner_inputs, outer_hidden, outer_inputs,
        w_mid, last_pad, far=(3, 5),
    )
    (total,) = kernel_call(
        gather_kernel, "gather", 0, [(packed.shape, f32)], [], everyone(packed)
    )
    grad_first, grad_mid, grad_last = kernel_call(
        deliver_kernel, "deliver", 0,
        [(w_first.shape, f32), (w_mid.shape, f32), (w_last.shape, f32)],
        [((devices * chunk, LANES), f32)],
        everyone(total),
    )
    return residual, adjoint, grad_first, grad_mid, grad_last


def solution(mesh):
    field = P(None, "patch", "sub")
    return jax.shard_map(
        per_device,
        mesh=mesh,
        in_specs=(field, field, field, P("patch", "sub"), P(), P(), P(), P()),
        out_specs=(field, field, P(), P(), P()),
        check_vma=False,
    )
```

```python
import jax
import jax.numpy as jnp
from jax import lax
from jax.experimental import pallas as pl
from jax.experimental.pallas import tpu as pltpu
from jax.sharding import PartitionSpec as P

HY = 16
LANES = 128
AXES = ("patch", "sub")


def ring(axis, step):
    count = lax.axis_size(axis)
    return [(i, (i + step) % count) for i in range(count)]


def from_both(array, axis, dim, width):
    size = array.shape[dim]
    tail = lax.slice_in_dim(array, size - width, size, axis=dim)
    head = lax.slice_in_dim(array, 0, width, axis=dim)
    before = lax.ppermute(tail, axis, ring(axis, 1))
    after = lax.ppermute(head, axis, ring(axis, -1))
    return before, after


def everyone(rows):
    return lax.all_to_all(rows, AXES, 0, 0, tiled=True)


def galerkin(matrix, target):
    size = len(target)
    matrix = [list(row) for row in matrix]
    target = list(target)
    scale = [matrix[i][i] for i in range(size)]
    inverse = []
    for i in range(size):
        pivot = matrix[i][i]
        usable = pivot > 1e-6 * scale[i]
        inverse.append(jnp.where(usable, 1.0 / jnp.where(usable, pivot, 1.0), 0.0))
        for j in range(i + 1, size):
            factor = matrix[i][j] * inverse[i]
            for k in range(j, size):
                matrix[j][k] = matrix[j][k] - factor * matrix[i][k]
            target[j] = target[j] - factor * target[i]
    answer = [None] * size
    for i in reversed(range(size)):
        running = target[i]
        for j in range(i + 1, size):
            running = running - matrix[i][j] * answer[j]
        answer[i] = running * inverse[i]
    return answer


DEGREE = 3
UPPER = [(a, b) for a in range(6) for b in range(a, 6)]
HALVING = (0.0625, 0.0625, 0.0625, -0.125, -0.125, -0.5)
SUMS = 14


def lanes_of(tile):
    if isinstance(tile, int):
        return pl.ds(tile * LANES, LANES)
    return pl.ds(pl.multiple_of(tile * LANES, LANES), LANES)


def beside(tile, tiles):
    if isinstance(tile, int):
        return (tile - 1) % tiles, (tile + 1) % tiles
    return jnp.where(tile == 0, tiles - 1, tile - 1), jnp.where(tile == tiles - 1, 0, tile + 1)


def x_pair(f):
    return pltpu.roll(f, 1, 0), pltpu.roll(f, f.shape[0] - 1, 0)


def spread_strains(u, v, w):
    value_u, slope_u = u[0] + u[1] + 6.0 * u[2], u[1] - u[0]
    value_v, slope_v = v[0] + v[1] + 6.0 * v[2], v[1] - v[0]
    both_w = w[0] + w[1]
    value_w, slope_w, curve_w = both_w + 6.0 * w[2], w[1] - w[0], both_w - 2.0 * w[2]
    b, a = x_pair(value_u)
    e0 = a - b
    hoop = slope_v + 0.0625 * value_w
    b, a = x_pair(hoop)
    e1 = b + a + 6.0 * hoop
    b = pltpu.roll(slope_u - value_v, 1, 0)
    a = pltpu.roll(slope_u + value_v, slope_u.shape[0] - 1, 0)
    e2 = b + a + 6.0 * slope_u
    b, a = x_pair(value_w)
    e3 = b + a - 2.0 * value_w
    b, a = x_pair(curve_w)
    e4 = b + a + 6.0 * curve_w
    b, a = x_pair(slope_w)
    e5 = a - b
    return e0, e1, e2, e3, e4, e5


def spread_forces(s):
    b, a = x_pair(s[0])
    lean_u = b - a
    b, a = x_pair(s[2])
    lean_v = b - a
    turn_u = b + a + 6.0 * s[2]
    b, a = x_pair(s[1])
    turn_v = b + a + 6.0 * s[1]
    b, a = x_pair(s[3])
    lean_w = 0.0625 * turn_v + (b + a - 2.0 * s[3])
    b, a = x_pair(s[4])
    bent_w = b + a + 6.0 * s[4]
    b, a = x_pair(s[5])
    turn_w = a - b
    sum_w = lean_w + bent_w
    return (
        (lean_u + turn_u, lean_u - turn_u, 6.0 * lean_u),
        (lean_v + turn_v, lean_v - turn_v, 6.0 * lean_v),
        (sum_w - turn_w, sum_w + turn_w, 6.0 * lean_w - 2.0 * bent_w),
    )


def chosen(layers, bits):
    if len(layers) == 1:
        return layers[0]
    half = len(layers) // 2
    return jnp.where(bits[-1], chosen(layers[half:], bits[:-1]), chosen(layers[:half], bits[:-1]))


MARGIN = 2
FIELDS = 8
PADDED = 16


def triples_of(centre, before, after, tile, tiles, first, final):
    at = lanes_of(tile)
    left, right = beside(tile, tiles)
    at_left, at_right = lanes_of(left), lanes_of(right)
    return [
        (
            jnp.where(first, before[c, :, at_left], before[c, :, at]),
            jnp.where(final, after[c, :, at_right], after[c, :, at]),
            centre[c, :, at],
        )
        for c in range(3)
    ]


def mixed(values, e):
    s = [None] * 6
    for n, (a, b) in enumerate(UPPER):
        for p, q in ((a, b), (b, a))[: 1 if a == b else 2]:
            term = values[n] * e[q]
            s[p] = term if s[p] is None else s[p] + term
    return s


def contract(left, right, left_dim, right_dim):
    return lax.dot_general(
        left, right, (((left_dim,), (right_dim,)), ((), ())), preferred_element_type=jnp.float32
    )


def widened(x):
    return jnp.concatenate([x, jnp.zeros_like(x)], axis=0).astype(jnp.bfloat16)


def learn(x, w_first, w_mid, w_last, keep=None):
    h = jnp.tanh(contract(x, w_first[...], 0, 0)).astype(jnp.bfloat16)
    if keep is not None:
        keep(0, h)
    for k in range(w_mid.shape[0]):
        h = jnp.tanh(contract(h, w_mid[k], 1, 1)).astype(jnp.bfloat16)
        if keep is not None:
            keep(k + 1, h)
    return contract(w_last[...], h, 1, 1)[:FIELDS]


def pieces_of(cols):
    step = cols
    while step > 2048 and step % 256 == 0:
        step //= 2
    return [(at, step) for at in range(0, cols, step)]


def gathered(array, row, spread, at, size):
    tiles = range(at // LANES, (at + size) // LANES)
    return jnp.concatenate(
        [array[t, pl.ds(row, FIELDS, stride=spread), :] for t in tiles], axis=1
    )


def learn_line(row, line, strain, learned, spread, cols, weights, hidden, inputs):
    for at, size in pieces_of(cols):
        x = widened(gathered(strain, row, spread, at, size))
        keep = None
        if line is not None:
            where = line * cols + at
            if not isinstance(where, int):
                where = pl.multiple_of(where, LANES)
            inputs[:, pl.ds(where, size)] = x

            def keep(k, h, where=where, size=size):
                hidden[k, pl.ds(where, size), :] = h

        out = learn(x, *weights, keep)
        for n in range(size // LANES):
            piece = out[:, n * LANES : (n + 1) * LANES]
            learned[at // LANES + n, pl.ds(row, FIELDS, stride=spread), :] = piece


def learn_rims(rows, strain, learned, spread, cols, weights):
    rim = cols // LANES
    x = [strain[rim, pl.ds(row, FIELDS, stride=spread), :] for row in rows]
    out = learn(widened(jnp.concatenate(x, axis=1)), *weights)
    for n, row in enumerate(rows):
        learned[rim, pl.ds(row, FIELDS, stride=spread), :] = out[:, n * LANES : (n + 1) * LANES]


def line_copy(line, cols, source, target, flags):
    where = line * cols
    if not isinstance(where, int):
        where = pl.multiple_of(where, LANES)
    here = pl.ds(where, cols)
    return pltpu.make_async_copy(source.at[:, here, :], target.at[:, here, :], flags.at[line])


def inner_kernel(
    fields, w_first, w_mid, w_last, learned, stored, inputs, before, after, strain, hidden, flags
):
    rows, wide = fields.shape[1], fields.shape[2]
    tiles = wide // LANES
    cols = wide - LANES
    lane = lax.broadcasted_iota(jnp.int32, (rows, LANES), 1)
    first, final = lane == 0, lane == LANES - 1

    def set_up(tile, carry):
        at = lanes_of(tile)
        for c in range(3):
            value = fields[c, :, at]
            before[c, :, at] = pltpu.roll(value, 1, 1)
            after[c, :, at] = pltpu.roll(value, LANES - 1, 1)
        return carry

    lax.fori_loop(0, tiles, set_up, 0)

    def strains(tile, carry):
        at = lanes_of(tile)
        e = spread_strains(*triples_of(fields.at[0:3], before, after, tile, tiles, first, final))
        for n in range(FIELDS):
            value = HALVING[n] * e[n] if n < 6 else jnp.zeros((rows, LANES), jnp.float32)
            strain[tile, n * rows : (n + 1) * rows] = value
        return carry

    lax.fori_loop(0, tiles, strains, 0)
    weights = (w_first, w_mid, w_last)

    def line(row, carry):
        learn_line(row, row - 1, strain, learned, rows, cols, weights, hidden, inputs)
        line_copy(row - 1, cols, hidden, stored, flags).start()
        return carry

    lax.fori_loop(1, rows - 1, line, 0)
    learn_rims(range(1, rows - 1), strain, learned, rows, cols, weights)
    for n in range(rows - 2):
        line_copy(n, cols, hidden, stored, flags).wait()


def stiffness_of(table, ids, depth, target, at):
    layups = table.shape[0] // 36
    bits = [(ids & (1 << k)) != 0 for k in range(depth)]
    for n, (a, b) in enumerate(UPPER):
        layers = [table[min(l, layups - 1) * 36 + a * 6 + b] for l in range(1 << depth)]
        target[n, :, at] = jnp.broadcast_to(chosen(layers, bits), ids.shape)


def depth_of(table):
    depth = 1
    while (1 << depth) < table.shape[0] // 36:
        depth += 1
    return depth


def prepare_kernel(table, fields, fl_up, fl_down, stiff, support):
    rows, wide = fields.shape[1], fields.shape[2]
    halo = fl_up.shape[1]
    edge = jnp.zeros((rows - halo, LANES), jnp.float32)

    def fill(tile, carry):
        at = lanes_of(tile)
        around = [
            jnp.concatenate(
                [edge, fl_up[c, :, at], fields[3 + c, :, at], fl_down[c, :, at], edge], axis=0
            )
            for c in range(4)
        ]
        for c in range(3):
            support[c, :, at] = around[c]
        stiffness_of(table, around[3].astype(jnp.int32), depth_of(table), stiff, at)
        return carry

    lax.fori_loop(0, wide // LANES, fill, 0)


def outer_kernel(
    table, fields, up, down, inner, w_first, w_mid, w_last,
    residual, own_residual, stored, inputs,
    centre, before, after, ahead, behind, middle, strain, learned, stiff, hidden, flags,
):
    rows, wide = fields.shape[1], fields.shape[2]
    tiles = wide // LANES
    cols = wide - LANES
    tall = 3 * rows
    lane = lax.broadcasted_iota(jnp.int32, (tall, LANES), 1)
    first, final = lane == 0, lane == LANES - 1
    rim = jnp.zeros((rows - MARGIN, LANES), jnp.float32)
    last = 3 * MARGIN

    def set_up(tile, carry):
        at = lanes_of(tile)
        for c in range(3):
            above, below = up[MARGIN * c : MARGIN * (c + 1), at], down[MARGIN * c : MARGIN * (c + 1), at]
            value = jnp.concatenate([rim, above, fields[c, :, at], below, rim], axis=0)
            centre[c, :, at] = value
            before[c, :, at] = pltpu.roll(value, 1, 1)
            after[c, :, at] = pltpu.roll(value, LANES - 1, 1)
        wall = jnp.zeros((rows - 1, LANES), jnp.float32)
        ids = jnp.concatenate(
            [wall, up[last : last + 1, at], fields[6, :, at], down[last : last + 1, at], wall],
            axis=0,
        ).astype(jnp.int32)
        stiffness_of(table, ids, depth_of(table), stiff, at)
        return carry

    lax.fori_loop(0, tiles, set_up, 0)

    def strains(tile, carry):
        at = lanes_of(tile)
        e = spread_strains(*triples_of(centre, before, after, tile, tiles, first, final))
        for n in range(FIELDS):
            value = HALVING[n] * e[n] if n < 6 else jnp.zeros((tall, LANES), jnp.float32)
            strain[tile, n * tall : (n + 1) * tall] = value
        for n in range(6):
            learned[tile, n * tall + rows + 1 : n * tall + 2 * rows - 1] = inner[
                tile, n * rows + 1 : (n + 1) * rows - 1
            ]
        return carry

    lax.fori_loop(0, tiles, strains, 0)
    weights = (w_first, w_mid, w_last)
    rim_rows = (rows - 1, rows, 2 * rows - 1, 2 * rows)
    for row, line in zip(rim_rows, (None, 0, 1, None)):
        learn_line(row, line, strain, learned, tall, cols, weights, hidden, inputs)
        if line is not None:
            line_copy(line, cols, hidden, stored, flags).start()
    learn_rims(rim_rows, strain, learned, tall, cols, weights)

    def push(tile, carry):
        at = lanes_of(tile)
        e = [strain[tile, n * tall : (n + 1) * tall] * (1.0 / HALVING[n]) for n in range(6)]
        s = mixed([stiff[n, :, at] for n in range(len(UPPER))], e)
        s = [s[n] + HALVING[n] * learned[tile, n * tall : (n + 1) * tall] for n in range(6)]
        for c, (alpha, beta, gamma) in enumerate(spread_forces(s)):
            ahead[c, :, at] = pltpu.roll(alpha, 1, 1)
            behind[c, :, at] = pltpu.roll(beta, LANES - 1, 1)
            middle[c, :, at] = gamma
        return carry

    lax.fori_loop(0, tiles, push, 0)
    own = slice(rows, 2 * rows)

    def finish(tile, carry):
        at = lanes_of(tile)
        left, right = beside(tile, tiles)
        at_left, at_right = lanes_of(left), lanes_of(right)
        for c in range(3):
            value = (
                middle[c, own, at]
                + jnp.where(first[:rows], ahead[c, own, at_left], ahead[c, own, at])
                + jnp.where(final[:rows], behind[c, own, at_right], behind[c, own, at])
            )
            value = value + fields[3 + c, :, at] * fields[c, :, at] - fields[7 + c, :, at]
            residual[c, :, at] = value
            if carry is not None:
                own_residual[c, :, at] = value
        return carry

    lax.fori_loop(0, tiles - 1, finish, 0)
    finish(tiles - 1, None)
    for n in range(2):
        line_copy(n, cols, hidden, stored, flags).wait()


def solve(numbers, sums, basis, adjoint, upstream, combined):
    rows = adjoint.shape[1]
    wide = basis.shape[3]
    tiles = wide // LANES
    own_tiles = tiles - 1
    tall = 3 * rows
    line = jnp.sum(sums[...], axis=0)
    picks = [jnp.broadcast_to(line[:, n : n + 1], (1, LANES)) for n in range(SUMS)]
    centre = [numbers[k] for k in range(3)]
    width = [numbers[3 + k] for k in range(3)]
    matrix = [[None] * 4 for _ in range(4)]
    for k in range(3):
        for j in range(k + 1):
            matrix[j][k] = picks[4 + k * (k + 1) // 2 + j]
    cross = [picks[3], picks[10], picks[11], picks[12]]
    for j in range(3):
        value = width[j] * cross[j + 1] + centre[j] * cross[j]
        matrix[j][3] = value + width[j - 1] * cross[j - 1] if j else value
    matrix[3][3] = picks[13]
    weights = [jnp.broadcast_to(x, (tall, LANES)) for x in galerkin(matrix, picks[:4])]

    def combine(tile, carry):
        at = lanes_of(tile)
        for c in range(3):
            value = weights[0] * basis[0, c, :, at]
            for k in range(1, DEGREE + 1):
                value = value + weights[k] * basis[k, c, :, at]
            combined[c, :, at] = value
            combined[3 + c, :, at] = pltpu.roll(value, 1, 1)
            combined[6 + c, :, at] = pltpu.roll(value, LANES - 1, 1)
        return carry

    lax.fori_loop(0, tiles, combine, 0)
    lane = lax.broadcasted_iota(jnp.int32, (tall, LANES), 1)
    first, final = lane == 0, lane == LANES - 1

    def strain(tile, carry):
        at = lanes_of(tile)
        triples = triples_of(
            combined.at[0:3], combined.at[3:6], combined.at[6:9], tile, tiles, first, final
        )
        for c in range(3):
            adjoint[c, :, at] = combined[c, rows : 2 * rows, at]
        for n, value in enumerate(spread_strains(*triples)):
            upstream[tile, n * rows : (n + 1) * rows] = HALVING[n] * value[rows : 2 * rows]
        for n in range(6, FIELDS):
            upstream[tile, n * rows : (n + 1) * rows] = jnp.zeros((rows, LANES), jnp.float32)
        return carry

    lax.fori_loop(0, own_tiles, strain, 0)


def slope_of(signal, h):
    h = h.astype(jnp.float32)
    return (signal * (1.0 - h * h)).astype(jnp.bfloat16)


def backward_kernel(
    numbers, sums, basis, inner_hidden, inner_inputs, outer_hidden, outer_inputs, w_mid, w_last,
    adjoint, packed,
    combined, upstream, grads, near_hidden, far_hidden, near_flags, far_flags,
):
    layers = w_mid.shape[0]
    hid = w_mid.shape[1]
    cols = upstream.shape[0] * LANES
    rows = upstream.shape[1] // FIELDS
    last_at = layers * hid
    first_at = last_at + FIELDS
    for n in range(rows - 2):
        line_copy(n, cols, inner_hidden, near_hidden, near_flags).start()
    for n in range(2):
        line_copy(n, cols, outer_hidden, far_hidden, far_flags).start()
    grads[...] = jnp.zeros_like(grads)
    solve(numbers, sums, basis, adjoint, upstream, combined)

    def line(row, at_line, hidden, inputs):
        for at, size in pieces_of(cols):
            where = at_line * cols + at
            if not isinstance(where, int):
                where = pl.multiple_of(where, LANES)
            here = pl.ds(where, size)
            signal = widened(gathered(upstream, row, rows, at, size))
            h = hidden[layers, here, :]
            grads[last_at : last_at + FIELDS] += contract(signal, h, 1, 0)[:FIELDS]
            d = slope_of(contract(signal, w_last[...], 0, 0), h)
            for k in range(layers - 1, -1, -1):
                h = hidden[k, here, :]
                grads[k * hid : (k + 1) * hid] += contract(d, h, 0, 0)
                d = slope_of(contract(d, w_mid[k], 1, 0), h)
            grads[first_at : first_at + FIELDS] += contract(inputs[:, here], d, 1, 0)[:FIELDS]

    def inside(row, carry):
        line_copy(row - 1, cols, inner_hidden, near_hidden, near_flags).wait()
        line(row, row - 1, near_hidden, inner_inputs)
        return carry

    lax.fori_loop(1, rows - 1, inside, 0)
    for n, row in enumerate((0, rows - 1)):
        line_copy(n, cols, outer_hidden, far_hidden, far_flags).wait()
        line(row, n, far_hidden, outer_inputs)
    chunk = packed.shape[1]
    for n in range(packed.shape[0]):
        packed[n] = grads[n * chunk : (n + 1) * chunk]


def gather_kernel(parts, total):
    total[...] = jnp.broadcast_to(jnp.sum(parts[...], axis=0, keepdims=True), total.shape)


def deliver_kernel(parts, grad_first, grad_mid, grad_last, flat):
    chunk = parts.shape[1]
    for n in range(parts.shape[0]):
        flat[n * chunk : (n + 1) * chunk] = parts[n]
    layers, hid = grad_mid.shape[0], grad_mid.shape[1]
    for k in range(layers):
        grad_mid[k] = flat[k * hid : (k + 1) * hid]
    at = layers * hid
    grad_last[...] = flat[at : at + FIELDS][: grad_last.shape[0]]
    grad_first[...] = flat[at + FIELDS : at + 2 * FIELDS][: grad_first.shape[0]]


def krylov_kernel(
    numbers, r_mid, r_up, r_down, stiff, support, basis, sums,
    before, after, ahead, behind, middle,
):
    rows = r_mid.shape[1]
    wide = r_mid.shape[2]
    tiles = wide // LANES
    own_tiles = tiles - 1
    tall = 3 * rows
    lane = lax.broadcasted_iota(jnp.int32, (tall, LANES), 1)
    first, final = lane == 0, lane == LANES - 1
    def place(k, c, at, value):
        basis[k, c, :, at] = value
        before[c, :, at] = pltpu.roll(value, 1, 1)
        after[c, :, at] = pltpu.roll(value, LANES - 1, 1)

    def set_up(tile, carry):
        at = lanes_of(tile)
        for c in range(3):
            value = jnp.concatenate([r_up[c, :, at], r_mid[c, :, at], r_down[c, :, at]], axis=0)
            place(0, c, at, value)
        return carry

    lax.fori_loop(0, tiles, set_up, 0)

    def strain_of(k, tile):
        return spread_strains(*triples_of(basis.at[k], before, after, tile, tiles, first, final))

    def stress_of(e, at):
        return mixed([stiff[n, :, at] for n in range(len(UPPER))], e)

    def mine(value):
        return value[rows : 2 * rows]

    zero = jnp.zeros((rows, LANES), jnp.float32)
    totals = [None] * SUMS

    for k in range(DEGREE):
        def push(tile, carry, k=k):
            at = lanes_of(tile)
            for c, (alpha, beta, gamma) in enumerate(
                spread_forces(stress_of(strain_of(k, tile), at))
            ):
                ahead[c, :, at] = pltpu.roll(alpha, 1, 1)
                behind[c, :, at] = pltpu.roll(beta, LANES - 1, 1)
                middle[c, :, at] = gamma
            return carry

        lax.fori_loop(0, tiles, push, 0)

        centre, width, inverse = numbers[k], numbers[3 + k], numbers[6 + k]
        former = numbers[2 + k]

        def advance(tile, carry, k=k):
            at = lanes_of(tile)
            left, right = beside(tile, tiles)
            at_left, at_right = lanes_of(left), lanes_of(right)
            image, here, following = [], [], []
            for c in range(3):
                vector = basis[k, c, :, at]
                value = (
                    middle[c, :, at]
                    + jnp.where(first, ahead[c, :, at_left], ahead[c, :, at])
                    + jnp.where(final, behind[c, :, at_right], behind[c, :, at])
                    + support[c, :, at] * vector
                )
                step = value - centre * vector
                if k:
                    step = step - former * basis[k - 1, c, :, at]
                step = step * inverse
                place(k + 1, c, at, step)
                image.append(mine(value))
                here.append(mine(vector))
                following.append(mine(step))
            if carry is None:
                return None

            def dot(left_side, right_side):
                return (
                    left_side[0] * right_side[0]
                    + left_side[1] * right_side[1]
                    + left_side[2] * right_side[2]
                )

            def old(m):
                return [basis[m, c, rows : 2 * rows, at] for c in range(3)]

            fresh = []
            origin = here if k == 0 else old(0)
            if k == 0:
                fresh.append(dot(here, here))
            fresh.append(dot(origin, following))
            for j in range(k + 1):
                fresh.append(dot(here if j == k else (origin if j == 0 else old(j)), image))
            if k == DEGREE - 1:
                fresh.append(dot(old(1), following))
                fresh.append(dot(here, following))
                fresh.append(dot(following, following))
            return tuple(p + q for p, q in zip(carry, fresh))

        names = ([0] if k == 0 else []) + [k + 1] + [4 + k * (k + 1) // 2 + j for j in range(k + 1)]
        if k == DEGREE - 1:
            names += [10, 11, 12]
        found = lax.fori_loop(0, own_tiles, advance, (zero,) * len(names))
        advance(own_tiles, None)
        for name, value in zip(names, found):
            totals[name] = value

    def energy(tile, running):
        at = lanes_of(tile)
        e = strain_of(DEGREE, tile)
        e = [mine(value) for value in e]
        for n, (a, b) in enumerate(UPPER):
            term = stiff[n, rows : 2 * rows, at] * e[b] * e[a]
            running = running + (term if a == b else 2.0 * term)
        for c in range(3):
            vector = basis[DEGREE, c, rows : 2 * rows, at]
            running = running + support[c, rows : 2 * rows, at] * vector * vector
        return running

    totals[13] = lax.fori_loop(0, own_tiles, energy, zero)
    place_of = lax.broadcasted_iota(jnp.int32, (1, LANES), 1)
    line = jnp.zeros((1, LANES), jnp.float32)
    for n in range(SUMS):
        total = jnp.sum(jnp.sum(totals[n], axis=0, keepdims=True), axis=1, keepdims=True)
        line = jnp.where(place_of == n, jnp.broadcast_to(total, (1, LANES)), line)
    sums[...] = jnp.broadcast_to(line[None], sums.shape)


def basis_constants(layup_stiffness):
    bending = 0.5 * (jnp.mean(layup_stiffness[:, 3, 3]) + jnp.mean(layup_stiffness[:, 4, 4]))
    centres = [11.5 * bending + 1.1, 9.8 * bending + 1.1, 8.4 * bending + 1.1]
    widths = [3.9 * bending + 0.4, 5.6 * bending + 0.4, 4.8 * bending + 0.4]
    return centres, widths


ON_CHIP = pl.BlockSpec(memory_space=pltpu.VMEM)
SCALARS = pl.BlockSpec(memory_space=pltpu.SMEM)


IN_PLACE = pl.BlockSpec(memory_space=pltpu.HBM)


def kernel_call(body, name, scalars, outs, scratch, *operands, far=(), far_outs=()):
    specs = [SCALARS] * scalars + [ON_CHIP] * (len(operands) - scalars)
    for n in far:
        specs[n] = IN_PLACE
    return pl.pallas_call(
        body,
        name=name,
        in_specs=specs,
        out_specs=[IN_PLACE if n in far_outs else ON_CHIP for n in range(len(outs))],
        out_shape=[
            pltpu.HBM(*out) if n in far_outs else jax.ShapeDtypeStruct(*out)
            for n, out in enumerate(outs)
        ],
        scratch_shapes=[
            pltpu.VMEM(*s) if isinstance(s, tuple) else pltpu.SemaphoreType.DMA((s,))
            for s in scratch
        ],
        compiler_params=pltpu.CompilerParams(vmem_limit_bytes=LIMITS[name] << 20),
    )(*[
        pltpu.with_memory_space_constraint(x, pltpu.HBM) if n in far else x
        for n, x in enumerate(operands)
    ])


LIMITS = {
    "inner": 24, "outer": 24, "prepare": 8, "krylov": 10, "backward": 32, "gather": 4, "deliver": 4,
}


def per_device(displacement, load, foundation, layup, layup_stiffness, w_first, w_mid, w_last):
    f32, bf16 = jnp.float32, jnp.bfloat16
    rows, cols = layup.shape
    layers, hid = w_mid.shape[0], w_mid.shape[1]
    devices = lax.axis_size("patch") * lax.axis_size("sub")
    wide = cols + LANES
    tall = 3 * rows
    tiles = wide // LANES
    fields = jnp.concatenate([displacement, foundation, layup.astype(f32)[None], load])
    before, after = from_both(fields, "sub", 2, HY)
    gap = jnp.zeros(fields.shape[:2] + (LANES - 2 * HY,), f32)
    fields = jnp.concatenate([fields, after, gap, before], axis=2)
    sends = [
        jnp.concatenate([*[fields[c, edge] for c in range(3)], fields[6, edge][near]])
        for edge, near in ((slice(rows - MARGIN, rows), slice(1, 2)), (slice(0, MARGIN), slice(0, 1)))
    ]
    up = lax.ppermute(sends[0], "patch", ring("patch", 1))
    down = lax.ppermute(sends[1], "patch", ring("patch", -1))

    halving = jnp.array(HALVING, f32)
    table = (layup_stiffness * halving[:, None] * halving[None, :]).reshape(-1)
    centres, widths = basis_constants(layup_stiffness)
    numbers = jnp.stack(centres + widths + [1.0 / x for x in widths])
    thin = w_first.shape[1]
    first_pad = jnp.pad(w_first.T, ((0, PADDED - thin), (0, 0)))
    last_pad = jnp.pad(w_last, ((0, PADDED - thin), (0, 0)))

    learned, inner_hidden, inner_inputs = kernel_call(
        inner_kernel, "inner", 0,
        [((tiles, FIELDS * rows, LANES), f32), ((layers + 1, (rows - 2) * cols, hid), bf16),
         ((PADDED, (rows - 2) * cols), bf16)],
        [((3, rows, wide), f32)] * 2
        + [((tiles, FIELDS * rows, LANES), f32), ((layers + 1, (rows - 2) * cols, hid), bf16),
           rows - 2],
        fields, first_pad, w_mid, last_pad, far_outs=(1,),
    )
    learned, distant = lax.optimization_barrier((learned, fields[3:7]))
    fl_up, fl_down = from_both(distant, "patch", 1, 6)
    wide_residual, residual, outer_hidden, outer_inputs = kernel_call(
        outer_kernel, "outer", 1,
        [((3, rows, wide), f32), ((3, rows, cols), f32),
         ((layers + 1, 2 * cols, hid), bf16), ((PADDED, 2 * cols), bf16)],
        [((3, tall, wide), f32)] * 6
        + [((tiles, FIELDS * tall, LANES), f32)] * 2
        + [((len(UPPER), tall, wide), f32), ((layers + 1, 2 * cols, hid), bf16), 2],
        table, fields, up, down, learned, first_pad, w_mid, last_pad, far_outs=(2,),
    )
    stiff, support = kernel_call(
        prepare_kernel, "prepare", 1,
        [((len(UPPER), tall, wide), f32), ((3, tall, wide), f32)], [],
        table, fields, fl_up, fl_down,
    )
    up, down = from_both(wide_residual, "patch", 1, rows)
    basis, sums = kernel_call(
        krylov_kernel, "krylov", 1,
        [((DEGREE + 1, 3, tall, wide), f32), ((devices, 1, LANES), f32)],
        [((3, tall, wide), f32)] * 5,
        numbers, wide_residual, up, down, stiff, support,
    )
    sums = everyone(sums)
    count = layers * hid + 2 * FIELDS
    chunk = -(-count // devices)
    adjoint, packed = kernel_call(
        backward_kernel, "backward", 1,
        [((3, rows, cols), f32), ((devices, chunk, LANES), f32)],
        [((9, tall, wide), f32), ((tiles - 1, FIELDS * rows, LANES), f32),
         ((devices * chunk, LANES), f32), ((layers + 1, (rows - 2) * cols, hid), bf16),
         ((layers + 1, 2 * cols, hid), bf16), rows - 2, 2],
        numbers, sums, basis, inner_hidden, inner_inputs, outer_hidden, outer_inputs,
        w_mid, last_pad, far=(3, 5),
    )
    (total,) = kernel_call(
        gather_kernel, "gather", 0, [(packed.shape, f32)], [], everyone(packed)
    )
    grad_first, grad_mid, grad_last = kernel_call(
        deliver_kernel, "deliver", 0,
        [((thin, hid), f32), (w_mid.shape, f32), (w_last.shape, f32)],
        [((devices * chunk, LANES), f32)],
        everyone(total),
    )
    return residual, adjoint, grad_first.T, grad_mid, grad_last


def solution(mesh):
    field = P(None, "patch", "sub")
    return jax.shard_map(
        per_device,
        mesh=mesh,
        in_specs=(field, field, field, P("patch", "sub"), P(), P(), P(), P()),
        out_specs=(field, field, P(), P(), P()),
        check_vma=False,
    )
```

```python
import jax
import jax.numpy as jnp
from jax import lax
from jax.experimental import pallas as pl
from jax.experimental.pallas import tpu as pltpu
from jax.sharding import PartitionSpec as P


HY = 16
LANES = 128
AXES = ("patch", "sub")


def ring(axis, step):
    count = lax.axis_size(axis)
    return [(i, (i + step) % count) for i in range(count)]


def from_both(array, axis, dim, width):
    size = array.shape[dim]
    tail = lax.slice_in_dim(array, size - width, size, axis=dim)
    head = lax.slice_in_dim(array, 0, width, axis=dim)
    before = lax.ppermute(tail, axis, ring(axis, 1))
    after = lax.ppermute(head, axis, ring(axis, -1))
    return before, after


def everyone(rows):
    return lax.all_to_all(rows, AXES, 0, 0, tiled=True)


def galerkin(matrix, target):
    size = len(target)
    matrix = [list(row) for row in matrix]
    target = list(target)
    scale = [matrix[i][i] for i in range(size)]
    inverse = []
    for i in range(size):
        pivot = matrix[i][i]
        usable = pivot > 1e-6 * scale[i]
        inverse.append(jnp.where(usable, 1.0 / jnp.where(usable, pivot, 1.0), 0.0))
        for j in range(i + 1, size):
            factor = matrix[i][j] * inverse[i]
            for k in range(j, size):
                matrix[j][k] = matrix[j][k] - factor * matrix[i][k]
            target[j] = target[j] - factor * target[i]
    answer = [None] * size
    for i in reversed(range(size)):
        running = target[i]
        for j in range(i + 1, size):
            running = running - matrix[i][j] * answer[j]
        answer[i] = running * inverse[i]
    return answer


DEGREE = 3
UPPER = [(a, b) for a in range(6) for b in range(a, 6)]
HALVING = (0.0625, 0.0625, 0.0625, -0.125, -0.125, -0.5)
SUMS = 14


def lanes_of(tile):
    if isinstance(tile, int):
        return pl.ds(tile * LANES, LANES)
    return pl.ds(pl.multiple_of(tile * LANES, LANES), LANES)


def beside(tile, tiles):
    if isinstance(tile, int):
        return (tile - 1) % tiles, (tile + 1) % tiles
    return jnp.where(tile == 0, tiles - 1, tile - 1), jnp.where(tile == tiles - 1, 0, tile + 1)


def x_pair(f):
    return pltpu.roll(f, 1, 0), pltpu.roll(f, f.shape[0] - 1, 0)


def spread_strains(u, v, w):
    value_u, slope_u = u[0] + u[1] + 6.0 * u[2], u[1] - u[0]
    value_v, slope_v = v[0] + v[1] + 6.0 * v[2], v[1] - v[0]
    both_w = w[0] + w[1]
    value_w, slope_w, curve_w = both_w + 6.0 * w[2], w[1] - w[0], both_w - 2.0 * w[2]
    b, a = x_pair(value_u)
    e0 = a - b
    hoop = slope_v + 0.0625 * value_w
    b, a = x_pair(hoop)
    e1 = b + a + 6.0 * hoop
    b = pltpu.roll(slope_u - value_v, 1, 0)
    a = pltpu.roll(slope_u + value_v, slope_u.shape[0] - 1, 0)
    e2 = b + a + 6.0 * slope_u
    b, a = x_pair(value_w)
    e3 = b + a - 2.0 * value_w
    b, a = x_pair(curve_w)
    e4 = b + a + 6.0 * curve_w
    b, a = x_pair(slope_w)
    e5 = a - b
    return e0, e1, e2, e3, e4, e5


def spread_forces(s):
    b, a = x_pair(s[0])
    lean_u = b - a
    b, a = x_pair(s[2])
    lean_v = b - a
    turn_u = b + a + 6.0 * s[2]
    b, a = x_pair(s[1])
    turn_v = b + a + 6.0 * s[1]
    b, a = x_pair(s[3])
    lean_w = 0.0625 * turn_v + (b + a - 2.0 * s[3])
    b, a = x_pair(s[4])
    bent_w = b + a + 6.0 * s[4]
    b, a = x_pair(s[5])
    turn_w = a - b
    sum_w = lean_w + bent_w
    return (
        (lean_u + turn_u, lean_u - turn_u, 6.0 * lean_u),
        (lean_v + turn_v, lean_v - turn_v, 6.0 * lean_v),
        (sum_w - turn_w, sum_w + turn_w, 6.0 * lean_w - 2.0 * bent_w),
    )


def chosen(layers, bits):
    if len(layers) == 1:
        return layers[0]
    half = len(layers) // 2
    return jnp.where(bits[-1], chosen(layers[half:], bits[:-1]), chosen(layers[:half], bits[:-1]))


MARGIN = 2
FIELDS = 8
PADDED = 16


def triples_of(centre, before, after, tile, tiles, first, final):
    at = lanes_of(tile)
    left, right = beside(tile, tiles)
    at_left, at_right = lanes_of(left), lanes_of(right)
    return [
        (
            jnp.where(first, before[c, :, at_left], before[c, :, at]),
            jnp.where(final, after[c, :, at_right], after[c, :, at]),
            centre[c, :, at],
        )
        for c in range(3)
    ]


def mixed(values, e):
    s = [None] * 6
    for n, (a, b) in enumerate(UPPER):
        for p, q in ((a, b), (b, a))[: 1 if a == b else 2]:
            term = values[n] * e[q]
            s[p] = term if s[p] is None else s[p] + term
    return s


def contract(left, right, left_dim, right_dim):
    return lax.dot_general(
        left, right, (((left_dim,), (right_dim,)), ((), ())), preferred_element_type=jnp.float32
    )


def widened(x):
    return jnp.concatenate([x, jnp.zeros_like(x)], axis=0).astype(jnp.bfloat16)


def learn(x, w_first, w_mid, w_last, keep=None):
    h = jnp.tanh(contract(x, w_first[...], 0, 0)).astype(jnp.bfloat16)
    if keep is not None:
        keep(0, h)
    for k in range(w_mid.shape[0]):
        h = jnp.tanh(contract(h, w_mid[k], 1, 1)).astype(jnp.bfloat16)
        if keep is not None:
            keep(k + 1, h)
    return contract(w_last[...], h, 1, 1)[:FIELDS]


def pieces_of(cols):
    step = cols
    while step > 2048 and step % 256 == 0:
        step //= 2
    return [(at, step) for at in range(0, cols, step)]


def gathered(array, row, spread, at, size):
    tiles = range(at // LANES, (at + size) // LANES)
    return jnp.concatenate(
        [array[t, pl.ds(row, FIELDS, stride=spread), :] for t in tiles], axis=1
    )


def learn_line(row, line, strain, learned, spread, cols, weights, hidden, inputs):
    for at, size in pieces_of(cols):
        x = widened(gathered(strain, row, spread, at, size))
        keep = None
        if line is not None:
            where = line * cols + at
            if not isinstance(where, int):
                where = pl.multiple_of(where, LANES)
            inputs[:, pl.ds(where, size)] = x

            def keep(k, h, where=where, size=size):
                hidden[k, pl.ds(where, size), :] = h

        out = learn(x, *weights, keep)
        for n in range(size // LANES):
            piece = out[:, n * LANES : (n + 1) * LANES]
            learned[at // LANES + n, pl.ds(row, FIELDS, stride=spread), :] = piece


def learn_rims(rows, strain, learned, spread, cols, weights):
    rim = cols // LANES
    x = [strain[rim, pl.ds(row, FIELDS, stride=spread), :] for row in rows]
    out = learn(widened(jnp.concatenate(x, axis=1)), *weights)
    for n, row in enumerate(rows):
        learned[rim, pl.ds(row, FIELDS, stride=spread), :] = out[:, n * LANES : (n + 1) * LANES]


def line_copy(line, cols, source, target, flags):
    where = line * cols
    if not isinstance(where, int):
        where = pl.multiple_of(where, LANES)
    here = pl.ds(where, cols)
    return pltpu.make_async_copy(source.at[:, here, :], target.at[:, here, :], flags.at[line])


def inner_kernel(
    fields, ends, w_mid, learned, stored, inputs, before, after, strain, hidden, flags
):
    rows, wide = fields.shape[1], fields.shape[2]
    tiles = wide // LANES
    cols = wide - LANES
    lane = lax.broadcasted_iota(jnp.int32, (rows, LANES), 1)
    first, final = lane == 0, lane == LANES - 1

    def set_up(tile, carry):
        at = lanes_of(tile)
        for c in range(3):
            value = fields[c, :, at]
            before[c, :, at] = pltpu.roll(value, 1, 1)
            after[c, :, at] = pltpu.roll(value, LANES - 1, 1)
        return carry

    lax.fori_loop(0, tiles, set_up, 0)

    def strains(tile, carry):
        at = lanes_of(tile)
        e = spread_strains(*triples_of(fields.at[0:3], before, after, tile, tiles, first, final))
        for n in range(FIELDS):
            value = HALVING[n] * e[n] if n < 6 else jnp.zeros((rows, LANES), jnp.float32)
            strain[tile, n * rows : (n + 1) * rows] = value
        return carry

    lax.fori_loop(0, tiles, strains, 0)
    weights = (ends.at[0:PADDED], w_mid, ends.at[PADDED : 2 * PADDED])

    def line(row, carry):
        learn_line(row, row - 1, strain, learned, rows, cols, weights, hidden, inputs)
        line_copy(row - 1, cols, hidden, stored, flags).start()
        return carry

    lax.fori_loop(1, rows - 1, line, 0)
    learn_rims(range(1, rows - 1), strain, learned, rows, cols, weights)
    for n in range(rows - 2):
        line_copy(n, cols, hidden, stored, flags).wait()


def stiffness_of(table, ids, depth, target, at):
    layups = table.shape[0] // 36
    bits = [(ids & (1 << k)) != 0 for k in range(depth)]
    for n, (a, b) in enumerate(UPPER):
        layers = [table[min(l, layups - 1) * 36 + a * 6 + b] for l in range(1 << depth)]
        target[n, :, at] = jnp.broadcast_to(chosen(layers, bits), ids.shape)


def depth_of(table):
    depth = 1
    while (1 << depth) < table.shape[0] // 36:
        depth += 1
    return depth


def prepare_kernel(table, fields, fl_up, fl_down, stiff, support):
    rows, wide = fields.shape[1], fields.shape[2]
    halo = fl_up.shape[1]
    edge = jnp.zeros((rows - halo, LANES), jnp.float32)

    def fill(tile, carry):
        at = lanes_of(tile)
        around = [
            jnp.concatenate(
                [edge, fl_up[c, :, at], fields[3 + c, :, at], fl_down[c, :, at], edge], axis=0
            )
            for c in range(4)
        ]
        for c in range(3):
            support[c, :, at] = around[c]
        stiffness_of(table, around[3].astype(jnp.int32), depth_of(table), stiff, at)
        return carry

    lax.fori_loop(0, wide // LANES, fill, 0)


def outer_kernel(
    table, fields, up, down, inner, ends, w_mid,
    residual, own_residual, stored, inputs,
    centre, before, after, ahead, behind, middle, strain, learned, stiff, hidden, flags,
):
    rows, wide = fields.shape[1], fields.shape[2]
    tiles = wide // LANES
    cols = wide - LANES
    tall = 3 * rows
    lane = lax.broadcasted_iota(jnp.int32, (tall, LANES), 1)
    first, final = lane == 0, lane == LANES - 1
    rim = jnp.zeros((rows - MARGIN, LANES), jnp.float32)
    last = 3 * MARGIN

    def set_up(tile, carry):
        at = lanes_of(tile)
        for c in range(3):
            above, below = up[MARGIN * c : MARGIN * (c + 1), at], down[MARGIN * c : MARGIN * (c + 1), at]
            value = jnp.concatenate([rim, above, fields[c, :, at], below, rim], axis=0)
            centre[c, :, at] = value
            before[c, :, at] = pltpu.roll(value, 1, 1)
            after[c, :, at] = pltpu.roll(value, LANES - 1, 1)
        wall = jnp.zeros((rows - 1, LANES), jnp.float32)
        ids = jnp.concatenate(
            [wall, up[last : last + 1, at], fields[6, :, at], down[last : last + 1, at], wall],
            axis=0,
        ).astype(jnp.int32)
        stiffness_of(table, ids, depth_of(table), stiff, at)
        return carry

    lax.fori_loop(0, tiles, set_up, 0)

    def strains(tile, carry):
        at = lanes_of(tile)
        e = spread_strains(*triples_of(centre, before, after, tile, tiles, first, final))
        for n in range(FIELDS):
            value = HALVING[n] * e[n] if n < 6 else jnp.zeros((tall, LANES), jnp.float32)
            strain[tile, n * tall : (n + 1) * tall] = value
        for n in range(6):
            learned[tile, n * tall + rows + 1 : n * tall + 2 * rows - 1] = inner[
                tile, n * rows + 1 : (n + 1) * rows - 1
            ]
        return carry

    lax.fori_loop(0, tiles, strains, 0)
    weights = (ends.at[0:PADDED], w_mid, ends.at[PADDED : 2 * PADDED])
    rim_rows = (rows - 1, rows, 2 * rows - 1, 2 * rows)
    for row, line in zip(rim_rows, (None, 0, 1, None)):
        learn_line(row, line, strain, learned, tall, cols, weights, hidden, inputs)
        if line is not None:
            line_copy(line, cols, hidden, stored, flags).start()
    learn_rims(rim_rows, strain, learned, tall, cols, weights)

    def push(tile, carry):
        at = lanes_of(tile)
        e = [strain[tile, n * tall : (n + 1) * tall] * (1.0 / HALVING[n]) for n in range(6)]
        s = mixed([stiff[n, :, at] for n in range(len(UPPER))], e)
        s = [s[n] + HALVING[n] * learned[tile, n * tall : (n + 1) * tall] for n in range(6)]
        for c, (alpha, beta, gamma) in enumerate(spread_forces(s)):
            ahead[c, :, at] = pltpu.roll(alpha, 1, 1)
            behind[c, :, at] = pltpu.roll(beta, LANES - 1, 1)
            middle[c, :, at] = gamma
        return carry

    lax.fori_loop(0, tiles, push, 0)
    own = slice(rows, 2 * rows)

    def finish(tile, carry):
        at = lanes_of(tile)
        left, right = beside(tile, tiles)
        at_left, at_right = lanes_of(left), lanes_of(right)
        for c in range(3):
            value = (
                middle[c, own, at]
                + jnp.where(first[:rows], ahead[c, own, at_left], ahead[c, own, at])
                + jnp.where(final[:rows], behind[c, own, at_right], behind[c, own, at])
            )
            value = value + fields[3 + c, :, at] * fields[c, :, at] - fields[7 + c, :, at]
            residual[c, :, at] = value
            if carry is not None:
                own_residual[c, :, at] = value
        return carry

    lax.fori_loop(0, tiles - 1, finish, 0)
    finish(tiles - 1, None)
    for n in range(2):
        line_copy(n, cols, hidden, stored, flags).wait()


def solve(numbers, sums, kept, bends, adjoint, upstream):
    rows = adjoint.shape[1]
    own_tiles = upstream.shape[0]
    line = jnp.sum(sums[...], axis=0)
    picks = [jnp.broadcast_to(line[:, n : n + 1], (1, LANES)) for n in range(SUMS)]
    centre = [numbers[k] for k in range(3)]
    width = [numbers[3 + k] for k in range(3)]
    matrix = [[None] * 4 for _ in range(4)]
    for k in range(3):
        for j in range(k + 1):
            matrix[j][k] = picks[4 + k * (k + 1) // 2 + j]
    cross = [picks[3], picks[10], picks[11], picks[12]]
    for j in range(3):
        value = width[j] * cross[j + 1] + centre[j] * cross[j]
        matrix[j][3] = value + width[j - 1] * cross[j - 1] if j else value
    matrix[3][3] = picks[13]
    weights = [jnp.broadcast_to(x, (rows, LANES)) for x in galerkin(matrix, picks[:4])]

    def weighted(parts):
        total = weights[0] * parts[0]
        for weight, part in zip(weights[1:], parts[1:]):
            total = total + weight * part
        return total

    levels = range(DEGREE + 1)

    def combine(tile, carry):
        at = lanes_of(tile)
        for c in range(3):
            adjoint[c, :, at] = weighted([kept[k, c, :, at] for k in levels])
        for n in range(6):
            here = slice(n * rows, (n + 1) * rows)
            upstream[tile, here] = HALVING[n] * weighted([bends[k, tile, here] for k in levels])
        upstream[tile, 6 * rows :] = jnp.zeros(((FIELDS - 6) * rows, LANES), jnp.float32)
        return carry

    lax.fori_loop(0, own_tiles, combine, 0)


def slope_of(signal, h):
    h = h.astype(jnp.float32)
    return (signal * (1.0 - h * h)).astype(jnp.bfloat16)


def backward_kernel(
    numbers, sums, kept, bends, inner_hidden, inner_inputs, outer_hidden, outer_inputs, w_mid,
    ends, adjoint, packed,
    upstream, grads, near_hidden, far_hidden, near_flags, far_flags,
):
    layers = w_mid.shape[0]
    hid = w_mid.shape[1]
    cols = upstream.shape[0] * LANES
    rows = upstream.shape[1] // FIELDS
    last_at = layers * hid
    first_at = last_at + FIELDS
    for n in range(rows - 2):
        line_copy(n, cols, inner_hidden, near_hidden, near_flags).start()
    for n in range(2):
        line_copy(n, cols, outer_hidden, far_hidden, far_flags).start()
    grads[...] = jnp.zeros_like(grads)
    solve(numbers, sums, kept, bends, adjoint, upstream)

    def line(row, at_line, hidden, inputs):
        for at, size in pieces_of(cols):
            where = at_line * cols + at
            if not isinstance(where, int):
                where = pl.multiple_of(where, LANES)
            here = pl.ds(where, size)
            signal = widened(gathered(upstream, row, rows, at, size))
            h = hidden[layers, here, :]
            grads[last_at : last_at + FIELDS] += contract(signal, h, 1, 0)[:FIELDS]
            d = slope_of(contract(signal, ends[PADDED : 2 * PADDED], 0, 0), h)
            for k in range(layers - 1, -1, -1):
                h = hidden[k, here, :]
                grads[k * hid : (k + 1) * hid] += contract(d, h, 0, 0)
                d = slope_of(contract(d, w_mid[k], 1, 0), h)
            grads[first_at : first_at + FIELDS] += contract(inputs[:, here], d, 1, 0)[:FIELDS]

    def inside(row, carry):
        line_copy(row - 1, cols, inner_hidden, near_hidden, near_flags).wait()
        line(row, row - 1, near_hidden, inner_inputs)
        return carry

    lax.fori_loop(1, rows - 1, inside, 0)
    for n, row in enumerate((0, rows - 1)):
        line_copy(n, cols, outer_hidden, far_hidden, far_flags).wait()
        line(row, n, far_hidden, outer_inputs)
    chunk = packed.shape[1]
    for n in range(packed.shape[0]):
        for r in range(chunk):
            packed[n, r] = grads[n * chunk + r : n * chunk + r + 1]


def gather_kernel(parts, total):
    total[...] = jnp.broadcast_to(jnp.sum(parts[...], axis=0, keepdims=True), total.shape)


def deliver_kernel(parts, grad_first, grad_mid, grad_last, flat):
    chunk = parts.shape[1]
    for n in range(parts.shape[0]):
        for r in range(chunk):
            flat[n * chunk + r : n * chunk + r + 1] = parts[n, r]
    layers, hid = grad_mid.shape[0], grad_mid.shape[1]
    for k in range(layers):
        grad_mid[k] = flat[k * hid : (k + 1) * hid]
    at = layers * hid
    grad_last[...] = flat[at : at + FIELDS][: grad_last.shape[0]]
    grad_first[...] = flat[at + FIELDS : at + 2 * FIELDS][: grad_first.shape[0]]


def krylov_kernel(
    numbers, r_mid, r_up, r_down, stiff, support, kept, bends, sums,
    basis, before, after, ahead, behind, middle,
):
    rows = r_mid.shape[1]
    wide = r_mid.shape[2]
    tiles = wide // LANES
    own_tiles = tiles - 1
    tall = 3 * rows
    lane = lax.broadcasted_iota(jnp.int32, (tall, LANES), 1)
    first, final = lane == 0, lane == LANES - 1

    def place(k, c, at, value):
        basis[k, c, :, at] = value
        kept[k, c, :, at] = value[rows : 2 * rows]
        before[c, :, at] = pltpu.roll(value, 1, 1)
        after[c, :, at] = pltpu.roll(value, LANES - 1, 1)

    def set_up(tile, carry):
        at = lanes_of(tile)
        for c in range(3):
            value = jnp.concatenate([r_up[c, :, at], r_mid[c, :, at], r_down[c, :, at]], axis=0)
            place(0, c, at, value)
        return carry

    lax.fori_loop(0, tiles, set_up, 0)

    def strain_of(k, tile):
        e = spread_strains(*triples_of(basis.at[k], before, after, tile, tiles, first, final))
        for n in range(6):
            bends[k, tile, n * rows : (n + 1) * rows] = e[n][rows : 2 * rows]
        return e

    def stress_of(e, at):
        return mixed([stiff[n, :, at] for n in range(len(UPPER))], e)

    def mine(value):
        return value[rows : 2 * rows]

    zero = jnp.zeros((rows, LANES), jnp.float32)
    totals = [None] * SUMS

    for k in range(DEGREE):
        def push(tile, carry, k=k):
            at = lanes_of(tile)
            for c, (alpha, beta, gamma) in enumerate(
                spread_forces(stress_of(strain_of(k, tile), at))
            ):
                ahead[c, :, at] = pltpu.roll(alpha, 1, 1)
                behind[c, :, at] = pltpu.roll(beta, LANES - 1, 1)
                middle[c, :, at] = gamma
            return carry

        lax.fori_loop(0, tiles, push, 0)

        centre, inverse = numbers[k], numbers[6 + k]
        former = numbers[2 + k]

        def advance(tile, carry, k=k):
            at = lanes_of(tile)
            left, right = beside(tile, tiles)
            at_left, at_right = lanes_of(left), lanes_of(right)
            image, here, following = [], [], []
            for c in range(3):
                vector = basis[k, c, :, at]
                value = (
                    middle[c, :, at]
                    + jnp.where(first, ahead[c, :, at_left], ahead[c, :, at])
                    + jnp.where(final, behind[c, :, at_right], behind[c, :, at])
                    + support[c, :, at] * vector
                )
                step = value - centre * vector
                if k:
                    step = step - former * basis[k - 1, c, :, at]
                step = step * inverse
                place(k + 1, c, at, step)
                image.append(mine(value))
                here.append(mine(vector))
                following.append(mine(step))
            if carry is None:
                return None

            def dot(left_side, right_side):
                return (
                    left_side[0] * right_side[0]
                    + left_side[1] * right_side[1]
                    + left_side[2] * right_side[2]
                )

            def old(m):
                return [basis[m, c, rows : 2 * rows, at] for c in range(3)]

            fresh = []
            origin = here if k == 0 else old(0)
            if k == 0:
                fresh.append(dot(here, here))
            fresh.append(dot(origin, following))
            for j in range(k + 1):
                fresh.append(dot(here if j == k else (origin if j == 0 else old(j)), image))
            if k == DEGREE - 1:
                fresh.append(dot(old(1), following))
                fresh.append(dot(here, following))
                fresh.append(dot(following, following))
            return tuple(p + q for p, q in zip(carry, fresh))

        names = ([0] if k == 0 else []) + [k + 1] + [4 + k * (k + 1) // 2 + j for j in range(k + 1)]
        if k == DEGREE - 1:
            names += [10, 11, 12]
        found = lax.fori_loop(0, own_tiles, advance, (zero,) * len(names))
        advance(own_tiles, None)
        for name, value in zip(names, found):
            totals[name] = value

    def energy(tile, running):
        at = lanes_of(tile)
        e = strain_of(DEGREE, tile)
        e = [mine(value) for value in e]
        for n, (a, b) in enumerate(UPPER):
            term = stiff[n, rows : 2 * rows, at] * e[b] * e[a]
            running = running + (term if a == b else 2.0 * term)
        for c in range(3):
            vector = basis[DEGREE, c, rows : 2 * rows, at]
            running = running + support[c, rows : 2 * rows, at] * vector * vector
        return running

    totals[13] = lax.fori_loop(0, own_tiles, energy, zero)
    place_of = lax.broadcasted_iota(jnp.int32, (1, LANES), 1)
    line = jnp.zeros((1, LANES), jnp.float32)
    for n in range(SUMS):
        total = jnp.sum(jnp.sum(totals[n], axis=0, keepdims=True), axis=1, keepdims=True)
        line = jnp.where(place_of == n, jnp.broadcast_to(total, (1, LANES)), line)
    sums[...] = jnp.broadcast_to(line[None], sums.shape)


def basis_constants(layup_stiffness):
    bending = 0.5 * (jnp.mean(layup_stiffness[:, 3, 3]) + jnp.mean(layup_stiffness[:, 4, 4]))
    centres = [11.5 * bending + 1.1, 9.8 * bending + 1.1, 8.4 * bending + 1.1]
    widths = [3.9 * bending + 0.4, 5.6 * bending + 0.4, 4.8 * bending + 0.4]
    return centres, widths


ON_CHIP = pl.BlockSpec(memory_space=pltpu.VMEM)
SCALARS = pl.BlockSpec(memory_space=pltpu.SMEM)


IN_PLACE = pl.BlockSpec(memory_space=pltpu.HBM)


def kernel_call(body, name, scalars, outs, scratch, *operands, far=(), far_outs=()):
    specs = [SCALARS] * scalars + [ON_CHIP] * (len(operands) - scalars)
    for n in far:
        specs[n] = IN_PLACE
    return pl.pallas_call(
        body,
        in_specs=specs,
        out_specs=[IN_PLACE if n in far_outs else ON_CHIP for n in range(len(outs))],
        out_shape=[
            pltpu.HBM(*out) if n in far_outs else jax.ShapeDtypeStruct(*out)
            for n, out in enumerate(outs)
        ],
        scratch_shapes=[
            pltpu.VMEM(*s) if isinstance(s, tuple) else pltpu.SemaphoreType.DMA((s,))
            for s in scratch
        ],
        compiler_params=pltpu.CompilerParams(vmem_limit_bytes=LIMITS[name] << 20),
    )(*[
        pltpu.with_memory_space_constraint(x, pltpu.HBM) if n in far else x
        for n, x in enumerate(operands)
    ])


LIMITS = {
    "inner": 24, "outer": 24, "prepare": 8, "krylov": 10, "backward": 32, "gather": 4, "deliver": 4,
}


def per_device(displacement, load, foundation, layup, layup_stiffness, w_first, w_mid, w_last):
    f32, bf16 = jnp.float32, jnp.bfloat16
    rows, cols = layup.shape
    layers, hid = w_mid.shape[0], w_mid.shape[1]
    devices = lax.axis_size("patch") * lax.axis_size("sub")
    wide = cols + LANES
    tall = 3 * rows
    tiles = wide // LANES
    fields = jnp.concatenate([displacement, foundation, layup.astype(f32)[None], load])
    before, after = from_both(fields, "sub", 2, HY)
    gap = jnp.zeros(fields.shape[:2] + (LANES - 2 * HY,), f32)
    fields = jnp.concatenate([fields, after, gap, before], axis=2)
    sends = [
        jnp.concatenate([*[fields[c, edge] for c in range(3)], fields[6, edge][near]])
        for edge, near in ((slice(rows - MARGIN, rows), slice(1, 2)), (slice(0, MARGIN), slice(0, 1)))
    ]
    up = lax.ppermute(sends[0], "patch", ring("patch", 1))
    down = lax.ppermute(sends[1], "patch", ring("patch", -1))
    fl_up, fl_down = from_both(fields[3:7], "patch", 1, 6)

    halving = jnp.array(HALVING, f32)
    table = (layup_stiffness * halving[:, None] * halving[None, :]).reshape(-1)
    centres, widths = basis_constants(layup_stiffness)
    numbers = jnp.stack(centres + widths + [1.0 / x for x in widths])
    thin = w_first.shape[1]
    blank = jnp.zeros((PADDED - thin, hid), bf16)
    ends = jnp.concatenate([w_first.T, blank, w_last, blank])

    learned, inner_hidden, inner_inputs = kernel_call(
        inner_kernel, "inner", 0,
        [((tiles, FIELDS * rows, LANES), f32), ((layers + 1, (rows - 2) * cols, hid), bf16),
         ((PADDED, (rows - 2) * cols), bf16)],
        [((3, rows, wide), f32)] * 2
        + [((tiles, FIELDS * rows, LANES), f32), ((layers + 1, (rows - 2) * cols, hid), bf16),
           rows - 2],
        fields, ends, w_mid, far_outs=(1,),
    )
    wide_residual, residual, outer_hidden, outer_inputs = kernel_call(
        outer_kernel, "outer", 1,
        [((3, rows, wide), f32), ((3, rows, cols), f32),
         ((layers + 1, 2 * cols, hid), bf16), ((PADDED, 2 * cols), bf16)],
        [((3, tall, wide), f32)] * 6
        + [((tiles, FIELDS * tall, LANES), f32)] * 2
        + [((len(UPPER), tall, wide), f32), ((layers + 1, 2 * cols, hid), bf16), 2],
        table, fields, up, down, learned, ends, w_mid, far_outs=(2,),
    )
    stiff, support = kernel_call(
        prepare_kernel, "prepare", 1,
        [((len(UPPER), tall, wide), f32), ((3, tall, wide), f32)], [],
        table, fields, fl_up, fl_down,
    )
    up, down = from_both(wide_residual, "patch", 1, rows)
    kept, bends, sums = kernel_call(
        krylov_kernel, "krylov", 1,
        [((DEGREE + 1, 3, rows, wide), f32), ((DEGREE + 1, tiles, 6 * rows, LANES), f32),
         ((devices, 1, LANES), f32)],
        [((DEGREE + 1, 3, tall, wide), f32)] + [((3, tall, wide), f32)] * 5,
        numbers, wide_residual, up, down, stiff, support,
    )
    sums = everyone(sums)
    count = layers * hid + 2 * FIELDS
    chunk = -(-count // devices)
    adjoint, packed = kernel_call(
        backward_kernel, "backward", 1,
        [((3, rows, cols), f32), ((devices, chunk, 1, LANES), f32)],
        [((tiles - 1, FIELDS * rows, LANES), f32),
         ((devices * chunk, LANES), f32), ((layers + 1, (rows - 2) * cols, hid), bf16),
         ((layers + 1, 2 * cols, hid), bf16), rows - 2, 2],
        numbers, sums, kept, bends, inner_hidden, inner_inputs, outer_hidden, outer_inputs,
        w_mid, ends, far=(4, 6),
    )
    (total,) = kernel_call(
        gather_kernel, "gather", 0, [(packed.shape, f32)], [], everyone(packed)
    )
    grad_first, grad_mid, grad_last = kernel_call(
        deliver_kernel, "deliver", 0,
        [((thin, hid), f32), (w_mid.shape, f32), (w_last.shape, f32)],
        [((devices * chunk, LANES), f32)],
        everyone(total),
    )
    return residual, adjoint, grad_first.T, grad_mid, grad_last


def solution(mesh):
    field = P(None, "patch", "sub")
    return jax.shard_map(
        per_device,
        mesh=mesh,
        in_specs=(field, field, field, P("patch", "sub"), P(), P(), P(), P()),
        out_specs=(field, field, P(), P(), P()),
        check_vma=False,
    )
```

```python
import jax
import jax.numpy as jnp
from jax import lax
from jax.experimental import pallas as pl
from jax.experimental.pallas import tpu as pltpu
from jax.sharding import PartitionSpec as P


HY = 16
LANES = 128
AXES = ("patch", "sub")


def ring(axis, step):
    count = lax.axis_size(axis)
    return [(i, (i + step) % count) for i in range(count)]


def from_both(array, axis, dim, width):
    size = array.shape[dim]
    tail = lax.slice_in_dim(array, size - width, size, axis=dim)
    head = lax.slice_in_dim(array, 0, width, axis=dim)
    before = lax.ppermute(tail, axis, ring(axis, 1))
    after = lax.ppermute(head, axis, ring(axis, -1))
    return before, after


def everyone(rows):
    return lax.all_to_all(rows, AXES, 0, 0, tiled=True)


def galerkin(matrix, target):
    size = len(target)
    matrix = [list(row) for row in matrix]
    target = list(target)
    scale = [matrix[i][i] for i in range(size)]
    inverse = []
    for i in range(size):
        pivot = matrix[i][i]
        usable = pivot > 1e-6 * scale[i]
        inverse.append(jnp.where(usable, 1.0 / jnp.where(usable, pivot, 1.0), 0.0))
        for j in range(i + 1, size):
            factor = matrix[i][j] * inverse[i]
            for k in range(j, size):
                matrix[j][k] = matrix[j][k] - factor * matrix[i][k]
            target[j] = target[j] - factor * target[i]
    answer = [None] * size
    for i in reversed(range(size)):
        running = target[i]
        for j in range(i + 1, size):
            running = running - matrix[i][j] * answer[j]
        answer[i] = running * inverse[i]
    return answer


DEGREE = 3
UPPER = [(a, b) for a in range(6) for b in range(a, 6)]
HALVING = (0.0625, 0.0625, 0.0625, -0.125, -0.125, -0.5)
SUMS = 14


def lanes_of(tile):
    if isinstance(tile, int):
        return pl.ds(tile * LANES, LANES)
    return pl.ds(pl.multiple_of(tile * LANES, LANES), LANES)


def beside(tile, tiles):
    if isinstance(tile, int):
        return (tile - 1) % tiles, (tile + 1) % tiles
    return jnp.where(tile == 0, tiles - 1, tile - 1), jnp.where(tile == tiles - 1, 0, tile + 1)


def x_pair(f):
    return pltpu.roll(f, 1, 0), pltpu.roll(f, f.shape[0] - 1, 0)


def spread_strains(u, v, w):
    value_u, slope_u = u[0] + u[1] + 6.0 * u[2], u[1] - u[0]
    value_v, slope_v = v[0] + v[1] + 6.0 * v[2], v[1] - v[0]
    both_w = w[0] + w[1]
    value_w, slope_w, curve_w = both_w + 6.0 * w[2], w[1] - w[0], both_w - 2.0 * w[2]
    b, a = x_pair(value_u)
    e0 = a - b
    hoop = slope_v + 0.0625 * value_w
    b, a = x_pair(hoop)
    e1 = b + a + 6.0 * hoop
    b = pltpu.roll(slope_u - value_v, 1, 0)
    a = pltpu.roll(slope_u + value_v, slope_u.shape[0] - 1, 0)
    e2 = b + a + 6.0 * slope_u
    b, a = x_pair(value_w)
    e3 = b + a - 2.0 * value_w
    b, a = x_pair(curve_w)
    e4 = b + a + 6.0 * curve_w
    b, a = x_pair(slope_w)
    e5 = a - b
    return e0, e1, e2, e3, e4, e5


def spread_forces(s):
    b, a = x_pair(s[0])
    lean_u = b - a
    b, a = x_pair(s[2])
    lean_v = b - a
    turn_u = b + a + 6.0 * s[2]
    b, a = x_pair(s[1])
    turn_v = b + a + 6.0 * s[1]
    b, a = x_pair(s[3])
    lean_w = 0.0625 * turn_v + (b + a - 2.0 * s[3])
    b, a = x_pair(s[4])
    bent_w = b + a + 6.0 * s[4]
    b, a = x_pair(s[5])
    turn_w = a - b
    sum_w = lean_w + bent_w
    return (
        (lean_u + turn_u, lean_u - turn_u, 6.0 * lean_u),
        (lean_v + turn_v, lean_v - turn_v, 6.0 * lean_v),
        (sum_w - turn_w, sum_w + turn_w, 6.0 * lean_w - 2.0 * bent_w),
    )


def chosen(layers, bits):
    if len(layers) == 1:
        return layers[0]
    half = len(layers) // 2
    return jnp.where(bits[-1], chosen(layers[half:], bits[:-1]), chosen(layers[:half], bits[:-1]))


MARGIN = 2
FIELDS = 8
PADDED = 16
PIECES = 3
GROUP = 9


def triples_of(centre, before, after, tile, tiles, first, final):
    at = lanes_of(tile)
    left, right = beside(tile, tiles)
    at_left, at_right = lanes_of(left), lanes_of(right)
    return [
        (
            jnp.where(first, before[c, :, at_left], before[c, :, at]),
            jnp.where(final, after[c, :, at_right], after[c, :, at]),
            centre[c, :, at],
        )
        for c in range(3)
    ]


def mixed(values, e):
    s = [None] * 6
    for n, (a, b) in enumerate(UPPER):
        for p, q in ((a, b), (b, a))[: 1 if a == b else 2]:
            term = values[n] * e[q]
            s[p] = term if s[p] is None else s[p] + term
    return s


def contract(left, right, left_dim, right_dim):
    return lax.dot_general(
        left, right, (((left_dim,), (right_dim,)), ((), ())), preferred_element_type=jnp.float32
    )


def widened(x):
    return jnp.concatenate([x, jnp.zeros_like(x)], axis=0).astype(jnp.bfloat16)


def learn(x, w_first, w_mid, w_last, keep=None):
    h = jnp.tanh(contract(x, w_first[...], 0, 0)).astype(jnp.bfloat16)
    if keep is not None:
        keep(0, h)
    for k in range(w_mid.shape[0]):
        h = jnp.tanh(contract(h, w_mid[k], 1, 1)).astype(jnp.bfloat16)
        if keep is not None:
            keep(k + 1, h)
    return contract(w_last[...], h, 1, 1)[:FIELDS]


def pieces_of(cols):
    step = cols
    while step > 2048 and step % 256 == 0:
        step //= 2
    return [(at, step) for at in range(0, cols, step)]


def gathered(array, row, spread, at, size):
    tiles = range(at // LANES, (at + size) // LANES)
    return jnp.concatenate(
        [array[t, pl.ds(row, FIELDS, stride=spread), :] for t in tiles], axis=1
    )


def learn_line(row, line, strain, learned, spread, cols, weights, hidden, inputs):
    for at, size in pieces_of(cols):
        x = widened(gathered(strain, row, spread, at, size))
        keep = None
        if line is not None:
            where = line * cols + at
            if not isinstance(where, int):
                where = pl.multiple_of(where, LANES)
            inputs[:, pl.ds(where, size)] = x

            def keep(k, h, where=where, size=size):
                hidden[k, pl.ds(where, size), :] = h

        out = learn(x, *weights, keep)
        for n in range(size // LANES):
            piece = out[:, n * LANES : (n + 1) * LANES]
            learned[at // LANES + n, pl.ds(row, FIELDS, stride=spread), :] = piece


def learn_rims(rows, strain, learned, spread, cols, weights):
    rim = cols // LANES
    x = [strain[rim, pl.ds(row, FIELDS, stride=spread), :] for row in rows]
    out = learn(widened(jnp.concatenate(x, axis=1)), *weights)
    for n, row in enumerate(rows):
        learned[rim, pl.ds(row, FIELDS, stride=spread), :] = out[:, n * LANES : (n + 1) * LANES]


def line_copy(line, cols, source, target, flags):
    where = line * cols
    if not isinstance(where, int):
        where = pl.multiple_of(where, LANES)
    here = pl.ds(where, cols)
    return pltpu.make_async_copy(source.at[:, here, :], target.at[:, here, :], flags.at[line])


def inner_kernel(
    fields, ends, w_mid, learned, stored, inputs, before, after, strain, hidden, flags
):
    rows, wide = fields.shape[1], fields.shape[2]
    tiles = wide // LANES
    cols = wide - LANES
    lane = lax.broadcasted_iota(jnp.int32, (rows, LANES), 1)
    first, final = lane == 0, lane == LANES - 1

    def set_up(tile, carry):
        at = lanes_of(tile)
        for c in range(3):
            value = fields[c, :, at]
            before[c, :, at] = pltpu.roll(value, 1, 1)
            after[c, :, at] = pltpu.roll(value, LANES - 1, 1)
        return carry

    lax.fori_loop(0, tiles, set_up, 0)

    def strains(tile, carry):
        at = lanes_of(tile)
        e = spread_strains(*triples_of(fields.at[0:3], before, after, tile, tiles, first, final))
        for n in range(FIELDS):
            value = HALVING[n] * e[n] if n < 6 else jnp.zeros((rows, LANES), jnp.float32)
            strain[tile, n * rows : (n + 1) * rows] = value
        return carry

    lax.fori_loop(0, tiles, strains, 0)
    weights = (ends.at[0:PADDED], w_mid, ends.at[PADDED : 2 * PADDED])

    def line(row, carry):
        learn_line(row, row - 1, strain, learned, rows, cols, weights, hidden, inputs)
        line_copy(row - 1, cols, hidden, stored, flags).start()
        return carry

    lax.fori_loop(1, rows - 1, line, 0)
    learn_rims(range(1, rows - 1), strain, learned, rows, cols, weights)
    for n in range(rows - 2):
        line_copy(n, cols, hidden, stored, flags).wait()


def stiffness_of(table, ids, depth, target, at):
    layups = table.shape[0] // 36
    bits = [(ids & (1 << k)) != 0 for k in range(depth)]
    for n, (a, b) in enumerate(UPPER):
        layers = [table[min(l, layups - 1) * 36 + a * 6 + b] for l in range(1 << depth)]
        target[n, :, at] = jnp.broadcast_to(chosen(layers, bits), ids.shape)


def depth_of(table):
    depth = 1
    while (1 << depth) < table.shape[0] // 36:
        depth += 1
    return depth


def prepare_kernel(table, fields, fl_up, fl_down, stiff, support):
    rows, wide = fields.shape[1], fields.shape[2]
    halo = fl_up.shape[1]
    edge = jnp.zeros((rows - halo, LANES), jnp.float32)

    def fill(tile, carry):
        at = lanes_of(tile)
        around = [
            jnp.concatenate(
                [edge, fl_up[c, :, at], fields[3 + c, :, at], fl_down[c, :, at], edge], axis=0
            )
            for c in range(4)
        ]
        for c in range(3):
            support[c, :, at] = around[c]
        stiffness_of(table, around[3].astype(jnp.int32), depth_of(table), stiff, at)
        return carry

    lax.fori_loop(0, wide // LANES, fill, 0)


def outer_kernel(
    table, fields, up, down, inner, ends, w_mid,
    residual, own_residual, stored, inputs,
    centre, before, after, ahead, behind, middle, strain, learned, stiff, shifts, hidden, flags,
):
    rows, wide = fields.shape[1], fields.shape[2]
    tiles = wide // LANES
    cols = wide - LANES
    tall = 3 * rows
    lane = lax.broadcasted_iota(jnp.int32, (tall, LANES), 1)
    first, final = lane == 0, lane == LANES - 1
    rim = jnp.zeros((rows - MARGIN, LANES), jnp.float32)
    last = 3 * MARGIN

    def set_up(tile, carry):
        at = lanes_of(tile)
        for c in range(3):
            above, below = up[MARGIN * c : MARGIN * (c + 1), at], down[MARGIN * c : MARGIN * (c + 1), at]
            value = jnp.concatenate([rim, above, fields[c, :, at], below, rim], axis=0)
            centre[c, :, at] = value
        wall = jnp.zeros((rows - 1, LANES), jnp.float32)
        ids = jnp.concatenate(
            [wall, up[last : last + 1, at], fields[6, :, at], down[last : last + 1, at], wall],
            axis=0,
        ).astype(jnp.int32)
        stiffness_of(table, ids, depth_of(table), stiff, at)
        return carry

    fill_shifts(shifts)
    lax.fori_loop(0, tiles, set_up, 0)
    shift_both(centre, before, after, shifts)

    def strains(tile, carry):
        at = lanes_of(tile)
        e = spread_strains(*triples_of(centre, before, after, tile, tiles, first, final))
        for n in range(FIELDS):
            value = HALVING[n] * e[n] if n < 6 else jnp.zeros((tall, LANES), jnp.float32)
            strain[tile, n * tall : (n + 1) * tall] = value
        for n in range(6):
            learned[tile, n * tall + rows + 1 : n * tall + 2 * rows - 1] = inner[
                tile, n * rows + 1 : (n + 1) * rows - 1
            ]
        return carry

    lax.fori_loop(0, tiles, strains, 0)
    weights = (ends.at[0:PADDED], w_mid, ends.at[PADDED : 2 * PADDED])
    rim_rows = (rows - 1, rows, 2 * rows - 1, 2 * rows)
    for row, line in zip(rim_rows, (None, 0, 1, None)):
        learn_line(row, line, strain, learned, tall, cols, weights, hidden, inputs)
        if line is not None:
            line_copy(line, cols, hidden, stored, flags).start()
    learn_rims(rim_rows, strain, learned, tall, cols, weights)

    def push(tile, carry):
        at = lanes_of(tile)
        e = [strain[tile, n * tall : (n + 1) * tall] * (1.0 / HALVING[n]) for n in range(6)]
        s = mixed([stiff[n, :, at] for n in range(len(UPPER))], e)
        s = [s[n] + HALVING[n] * learned[tile, n * tall : (n + 1) * tall] for n in range(6)]
        for c, (alpha, beta, gamma) in enumerate(spread_forces(s)):
            ahead[c, :, at] = alpha
            behind[c, :, at] = beta
            middle[c, :, at] = gamma
        return carry

    lax.fori_loop(0, tiles, push, 0)
    shift_in_place(ahead, 0, shifts)
    shift_in_place(behind, 1, shifts)
    own = slice(rows, 2 * rows)

    def finish(tile, carry):
        at = lanes_of(tile)
        left, right = beside(tile, tiles)
        at_left, at_right = lanes_of(left), lanes_of(right)
        for c in range(3):
            value = (
                middle[c, own, at]
                + jnp.where(first[:rows], ahead[c, own, at_left], ahead[c, own, at])
                + jnp.where(final[:rows], behind[c, own, at_right], behind[c, own, at])
            )
            value = value + fields[3 + c, :, at] * fields[c, :, at] - fields[7 + c, :, at]
            residual[c, :, at] = value
            if carry is not None:
                own_residual[c, :, at] = value
        return carry

    lax.fori_loop(0, tiles - 1, finish, 0)
    finish(tiles - 1, None)
    for n in range(2):
        line_copy(n, cols, hidden, stored, flags).wait()


def solve(numbers, sums, kept, bends, adjoint, upstream):
    rows = adjoint.shape[1]
    own_tiles = upstream.shape[0]
    line = jnp.sum(sums[...], axis=0)
    picks = [jnp.broadcast_to(line[:, n : n + 1], (1, LANES)) for n in range(SUMS)]
    centre = [numbers[k] for k in range(3)]
    width = [numbers[3 + k] for k in range(3)]
    matrix = [[None] * 4 for _ in range(4)]
    for k in range(3):
        for j in range(k + 1):
            matrix[j][k] = picks[4 + k * (k + 1) // 2 + j]
    cross = [picks[3], picks[10], picks[11], picks[12]]
    for j in range(3):
        value = width[j] * cross[j + 1] + centre[j] * cross[j]
        matrix[j][3] = value + width[j - 1] * cross[j - 1] if j else value
    matrix[3][3] = picks[13]
    weights = [jnp.broadcast_to(x, (rows, LANES)) for x in galerkin(matrix, picks[:4])]

    def weighted(parts):
        total = weights[0] * parts[0]
        for weight, part in zip(weights[1:], parts[1:]):
            total = total + weight * part
        return total

    levels = range(DEGREE + 1)

    def combine(tile, carry):
        at = lanes_of(tile)
        for c in range(3):
            adjoint[c, :, at] = weighted([kept[k, c, :, at] for k in levels])
        for n in range(6):
            here = slice(n * rows, (n + 1) * rows)
            upstream[tile, here] = HALVING[n] * weighted([bends[k, tile, here] for k in levels])
        upstream[tile, 6 * rows :] = jnp.zeros(((FIELDS - 6) * rows, LANES), jnp.float32)
        return carry

    lax.fori_loop(0, own_tiles, combine, 0)


def slope_of(signal, h):
    h = h.astype(jnp.float32)
    return (signal * (1.0 - h * h)).astype(jnp.bfloat16)


def backward_kernel(
    numbers, sums, kept, bends, inner_hidden, inner_inputs, outer_hidden, outer_inputs, w_mid,
    ends, adjoint, packed,
    upstream, grads, near_hidden, far_hidden, near_flags, far_flags,
):
    layers = w_mid.shape[0]
    hid = w_mid.shape[1]
    cols = upstream.shape[0] * LANES
    rows = upstream.shape[1] // FIELDS
    last_at = layers * hid
    first_at = last_at + FIELDS
    for n in range(rows - 2):
        line_copy(n, cols, inner_hidden, near_hidden, near_flags).start()
    for n in range(2):
        line_copy(n, cols, outer_hidden, far_hidden, far_flags).start()
    grads[...] = jnp.zeros_like(grads)
    solve(numbers, sums, kept, bends, adjoint, upstream)

    def line(row, at_line, hidden, inputs):
        for at, size in pieces_of(cols):
            where = at_line * cols + at
            if not isinstance(where, int):
                where = pl.multiple_of(where, LANES)
            here = pl.ds(where, size)
            signal = widened(gathered(upstream, row, rows, at, size))
            h = hidden[layers, here, :]
            grads[last_at : last_at + FIELDS] += contract(signal, h, 1, 0)[:FIELDS]
            d = slope_of(contract(signal, ends[PADDED : 2 * PADDED], 0, 0), h)
            for k in range(layers - 1, -1, -1):
                h = hidden[k, here, :]
                grads[k * hid : (k + 1) * hid] += contract(d, h, 0, 0)
                d = slope_of(contract(d, w_mid[k], 1, 0), h)
            grads[first_at : first_at + FIELDS] += contract(inputs[:, here], d, 1, 0)[:FIELDS]

    def inside(row, carry):
        line_copy(row - 1, cols, inner_hidden, near_hidden, near_flags).wait()
        line(row, row - 1, near_hidden, inner_inputs)
        return carry

    lax.fori_loop(1, rows - 1, inside, 0)
    for n, row in enumerate((0, rows - 1)):
        line_copy(n, cols, outer_hidden, far_hidden, far_flags).wait()
        line(row, n, far_hidden, outer_inputs)
    chunk = packed.shape[1]
    for n in range(packed.shape[0]):
        for r in range(chunk):
            packed[n, r] = grads[n * chunk + r : n * chunk + r + 1]


def gather_kernel(parts, total):
    total[...] = jnp.broadcast_to(jnp.sum(parts[...], axis=0, keepdims=True), total.shape)


def deliver_kernel(parts, grad_first, grad_mid, grad_last, flat):
    chunk = parts.shape[1]
    for n in range(parts.shape[0]):
        for r in range(chunk):
            flat[n * chunk + r : n * chunk + r + 1] = parts[n, r]
    layers, hid = grad_mid.shape[0], grad_mid.shape[1]
    for k in range(layers):
        grad_mid[k] = flat[k * hid : (k + 1) * hid]
    at = layers * hid
    grad_last[...] = flat[at : at + FIELDS][: grad_last.shape[0]]
    grad_first[...] = flat[at + FIELDS : at + 2 * FIELDS][: grad_first.shape[0]]


def fill_shifts(shifts):
    shape = (PIECES * LANES, LANES)
    source = lax.broadcasted_iota(jnp.int32, shape, 0) % LANES
    target = lax.broadcasted_iota(jnp.int32, shape, 1)
    for n, step in enumerate((1, LANES - 1)):
        hit = (source + step) % LANES == target
        shifts[:, n * LANES : (n + 1) * LANES] = jnp.where(hit, 1.0, 0.0).astype(jnp.bfloat16)


def pieces(x):
    parts = []
    for n in range(PIECES):
        part = x.astype(jnp.bfloat16)
        parts.append(part)
        if n + 1 < PIECES:
            x = x - part.astype(jnp.float32)
    return jnp.concatenate(parts, axis=1)


def groups_of(array):
    tiles = array.shape[2] // LANES
    return [range(t, min(t + GROUP, tiles)) for t in range(0, tiles, GROUP)]


def stacked(source, group):
    return pieces(
        jnp.concatenate([source[c, :, lanes_of(t)] for t in group for c in range(3)], axis=0)
    )


def shift_both(source, before, after, shifts):
    tall = source.shape[1]
    for group in groups_of(source):
        moved = contract(stacked(source, group), shifts[...], 1, 0)
        for n, tile in enumerate(group):
            for c in range(3):
                at = (3 * n + c) * tall
                before[c, :, lanes_of(tile)] = moved[at : at + tall, :LANES]
                after[c, :, lanes_of(tile)] = moved[at : at + tall, LANES:]


def shift_in_place(array, side, shifts):
    tall = array.shape[1]
    for group in groups_of(array):
        moved = contract(stacked(array, group), shifts[:, side * LANES : (side + 1) * LANES], 1, 0)
        for n, tile in enumerate(group):
            for c in range(3):
                at = (3 * n + c) * tall
                array[c, :, lanes_of(tile)] = moved[at : at + tall]


def krylov_kernel(
    numbers, r_mid, r_up, r_down, stiff, support, kept, bends, sums,
    basis, before, after, ahead, behind, middle, shifts,
):
    rows = r_mid.shape[1]
    wide = r_mid.shape[2]
    tiles = wide // LANES
    own_tiles = tiles - 1
    tall = 3 * rows
    lane = lax.broadcasted_iota(jnp.int32, (tall, LANES), 1)
    first, final = lane == 0, lane == LANES - 1

    def place(k, c, at, value):
        basis[k, c, :, at] = value
        kept[k, c, :, at] = value[rows : 2 * rows]

    def set_up(tile, carry):
        at = lanes_of(tile)
        for c in range(3):
            value = jnp.concatenate([r_up[c, :, at], r_mid[c, :, at], r_down[c, :, at]], axis=0)
            place(0, c, at, value)
        return carry

    fill_shifts(shifts)
    lax.fori_loop(0, tiles, set_up, 0)
    shift_both(basis.at[0], before, after, shifts)

    def strain_of(k, tile):
        e = spread_strains(*triples_of(basis.at[k], before, after, tile, tiles, first, final))
        for n in range(6):
            bends[k, tile, n * rows : (n + 1) * rows] = e[n][rows : 2 * rows]
        return e

    def stress_of(e, at):
        return mixed([stiff[n, :, at] for n in range(len(UPPER))], e)

    def mine(value):
        return value[rows : 2 * rows]

    zero = jnp.zeros((rows, LANES), jnp.float32)
    totals = [None] * SUMS

    for k in range(DEGREE):
        def push(tile, carry, k=k):
            at = lanes_of(tile)
            for c, (alpha, beta, gamma) in enumerate(
                spread_forces(stress_of(strain_of(k, tile), at))
            ):
                ahead[c, :, at] = alpha
                behind[c, :, at] = beta
                middle[c, :, at] = gamma
            return carry

        lax.fori_loop(0, tiles, push, 0)
        shift_in_place(ahead, 0, shifts)
        shift_in_place(behind, 1, shifts)

        centre, inverse = numbers[k], numbers[6 + k]
        former = numbers[2 + k]

        def advance(tile, carry, k=k):
            at = lanes_of(tile)
            left, right = beside(tile, tiles)
            at_left, at_right = lanes_of(left), lanes_of(right)
            image, here, following = [], [], []
            for c in range(3):
                vector = basis[k, c, :, at]
                value = (
                    middle[c, :, at]
                    + jnp.where(first, ahead[c, :, at_left], ahead[c, :, at])
                    + jnp.where(final, behind[c, :, at_right], behind[c, :, at])
                    + support[c, :, at] * vector
                )
                step = value - centre * vector
                if k:
                    step = step - former * basis[k - 1, c, :, at]
                step = step * inverse
                place(k + 1, c, at, step)
                image.append(mine(value))
                here.append(mine(vector))
                following.append(mine(step))
            if carry is None:
                return None

            def dot(left_side, right_side):
                return (
                    left_side[0] * right_side[0]
                    + left_side[1] * right_side[1]
                    + left_side[2] * right_side[2]
                )

            def old(m):
                return [basis[m, c, rows : 2 * rows, at] for c in range(3)]

            fresh = []
            origin = here if k == 0 else old(0)
            if k == 0:
                fresh.append(dot(here, here))
            fresh.append(dot(origin, following))
            for j in range(k + 1):
                fresh.append(dot(here if j == k else (origin if j == 0 else old(j)), image))
            if k == DEGREE - 1:
                fresh.append(dot(old(1), following))
                fresh.append(dot(here, following))
                fresh.append(dot(following, following))
            return tuple(p + q for p, q in zip(carry, fresh))

        names = ([0] if k == 0 else []) + [k + 1] + [4 + k * (k + 1) // 2 + j for j in range(k + 1)]
        if k == DEGREE - 1:
            names += [10, 11, 12]
        found = lax.fori_loop(0, own_tiles, advance, (zero,) * len(names))
        advance(own_tiles, None)
        shift_both(basis.at[k + 1], before, after, shifts)
        for name, value in zip(names, found):
            totals[name] = value

    def energy(tile, running):
        at = lanes_of(tile)
        e = strain_of(DEGREE, tile)
        e = [mine(value) for value in e]
        for n, (a, b) in enumerate(UPPER):
            term = stiff[n, rows : 2 * rows, at] * e[b] * e[a]
            running = running + (term if a == b else 2.0 * term)
        for c in range(3):
            vector = basis[DEGREE, c, rows : 2 * rows, at]
            running = running + support[c, rows : 2 * rows, at] * vector * vector
        return running

    totals[13] = lax.fori_loop(0, own_tiles, energy, zero)
    place_of = lax.broadcasted_iota(jnp.int32, (1, LANES), 1)
    line = jnp.zeros((1, LANES), jnp.float32)
    for n in range(SUMS):
        total = jnp.sum(jnp.sum(totals[n], axis=0, keepdims=True), axis=1, keepdims=True)
        line = jnp.where(place_of == n, jnp.broadcast_to(total, (1, LANES)), line)
    sums[...] = jnp.broadcast_to(line[None], sums.shape)


def basis_constants(layup_stiffness):
    bending = 0.5 * (jnp.mean(layup_stiffness[:, 3, 3]) + jnp.mean(layup_stiffness[:, 4, 4]))
    centres = [11.5 * bending + 1.1, 9.8 * bending + 1.1, 8.4 * bending + 1.1]
    widths = [3.9 * bending + 0.4, 5.6 * bending + 0.4, 4.8 * bending + 0.4]
    return centres, widths


ON_CHIP = pl.BlockSpec(memory_space=pltpu.VMEM)
SCALARS = pl.BlockSpec(memory_space=pltpu.SMEM)


IN_PLACE = pl.BlockSpec(memory_space=pltpu.HBM)


def kernel_call(body, name, scalars, outs, scratch, *operands, far=(), far_outs=()):
    specs = [SCALARS] * scalars + [ON_CHIP] * (len(operands) - scalars)
    for n in far:
        specs[n] = IN_PLACE
    return pl.pallas_call(
        body,
        in_specs=specs,
        out_specs=[IN_PLACE if n in far_outs else ON_CHIP for n in range(len(outs))],
        out_shape=[
            pltpu.HBM(*out) if n in far_outs else jax.ShapeDtypeStruct(*out)
            for n, out in enumerate(outs)
        ],
        scratch_shapes=[
            pltpu.VMEM(*s) if isinstance(s, tuple) else pltpu.SemaphoreType.DMA((s,))
            for s in scratch
        ],
        compiler_params=pltpu.CompilerParams(vmem_limit_bytes=LIMITS[name] << 20),
    )(*[
        pltpu.with_memory_space_constraint(x, pltpu.HBM) if n in far else x
        for n, x in enumerate(operands)
    ])


LIMITS = {
    "inner": 24, "outer": 24, "prepare": 8, "krylov": 10, "backward": 32, "gather": 4, "deliver": 4,
}


def per_device(displacement, load, foundation, layup, layup_stiffness, w_first, w_mid, w_last):
    f32, bf16 = jnp.float32, jnp.bfloat16
    rows, cols = layup.shape
    layers, hid = w_mid.shape[0], w_mid.shape[1]
    devices = lax.axis_size("patch") * lax.axis_size("sub")
    wide = cols + LANES
    tall = 3 * rows
    tiles = wide // LANES
    fields = jnp.concatenate([displacement, foundation, layup.astype(f32)[None], load])
    before, after = from_both(fields, "sub", 2, HY)
    gap = jnp.zeros(fields.shape[:2] + (LANES - 2 * HY,), f32)
    fields = jnp.concatenate([fields, after, gap, before], axis=2)
    sends = [
        jnp.concatenate([*[fields[c, edge] for c in range(3)], fields[6, edge][near]])
        for edge, near in ((slice(rows - MARGIN, rows), slice(1, 2)), (slice(0, MARGIN), slice(0, 1)))
    ]
    up = lax.ppermute(sends[0], "patch", ring("patch", 1))
    down = lax.ppermute(sends[1], "patch", ring("patch", -1))
    fl_up, fl_down = from_both(fields[3:7], "patch", 1, 6)

    halving = jnp.array(HALVING, f32)
    table = (layup_stiffness * halving[:, None] * halving[None, :]).reshape(-1)
    centres, widths = basis_constants(layup_stiffness)
    numbers = jnp.stack(centres + widths + [1.0 / x for x in widths])
    thin = w_first.shape[1]
    blank = jnp.zeros((PADDED - thin, hid), bf16)
    ends = jnp.concatenate([w_first.T, blank, w_last, blank])

    learned, inner_hidden, inner_inputs = kernel_call(
        inner_kernel, "inner", 0,
        [((tiles, FIELDS * rows, LANES), f32), ((layers + 1, (rows - 2) * cols, hid), bf16),
         ((PADDED, (rows - 2) * cols), bf16)],
        [((3, rows, wide), f32)] * 2
        + [((tiles, FIELDS * rows, LANES), f32), ((layers + 1, (rows - 2) * cols, hid), bf16),
           rows - 2],
        fields, ends, w_mid, far_outs=(1,),
    )
    wide_residual, residual, outer_hidden, outer_inputs = kernel_call(
        outer_kernel, "outer", 1,
        [((3, rows, wide), f32), ((3, rows, cols), f32),
         ((layers + 1, 2 * cols, hid), bf16), ((PADDED, 2 * cols), bf16)],
        [((3, tall, wide), f32)] * 6
        + [((tiles, FIELDS * tall, LANES), f32)] * 2
        + [((len(UPPER), tall, wide), f32), ((PIECES * LANES, 2 * LANES), bf16),
           ((layers + 1, 2 * cols, hid), bf16), 2],
        table, fields, up, down, learned, ends, w_mid, far_outs=(2,),
    )
    stiff, support = kernel_call(
        prepare_kernel, "prepare", 1,
        [((len(UPPER), tall, wide), f32), ((3, tall, wide), f32)], [],
        table, fields, fl_up, fl_down,
    )
    up, down = from_both(wide_residual, "patch", 1, rows)
    kept, bends, sums = kernel_call(
        krylov_kernel, "krylov", 1,
        [((DEGREE + 1, 3, rows, wide), f32), ((DEGREE + 1, tiles, 6 * rows, LANES), f32),
         ((devices, 1, LANES), f32)],
        [((DEGREE + 1, 3, tall, wide), f32)] + [((3, tall, wide), f32)] * 5
        + [((PIECES * LANES, 2 * LANES), bf16)],
        numbers, wide_residual, up, down, stiff, support,
    )
    sums = everyone(sums)
    count = layers * hid + 2 * FIELDS
    chunk = -(-count // devices)
    adjoint, packed = kernel_call(
        backward_kernel, "backward", 1,
        [((3, rows, cols), f32), ((devices, chunk, 1, LANES), f32)],
        [((tiles - 1, FIELDS * rows, LANES), f32),
         ((devices * chunk, LANES), f32), ((layers + 1, (rows - 2) * cols, hid), bf16),
         ((layers + 1, 2 * cols, hid), bf16), rows - 2, 2],
        numbers, sums, kept, bends, inner_hidden, inner_inputs, outer_hidden, outer_inputs,
        w_mid, ends, far=(4, 6),
    )
    (total,) = kernel_call(
        gather_kernel, "gather", 0, [(packed.shape, f32)], [], everyone(packed)
    )
    grad_first, grad_mid, grad_last = kernel_call(
        deliver_kernel, "deliver", 0,
        [((thin, hid), f32), (w_mid.shape, f32), (w_last.shape, f32)],
        [((devices * chunk, LANES), f32)],
        everyone(total),
    )
    return residual, adjoint, grad_first.T, grad_mid, grad_last


def solution(mesh):
    field = P(None, "patch", "sub")
    return jax.shard_map(
        per_device,
        mesh=mesh,
        in_specs=(field, field, field, P("patch", "sub"), P(), P(), P(), P()),
        out_specs=(field, field, P(), P(), P()),
        check_vma=False,
    )
```

```python
import jax
import jax.numpy as jnp
from jax import lax
from jax.experimental import pallas as pl
from jax.experimental.pallas import tpu as pltpu
from jax.sharding import PartitionSpec as P


HY = 16
LANES = 128
AXES = ("patch", "sub")


def ring(axis, step):
    count = lax.axis_size(axis)
    return [(i, (i + step) % count) for i in range(count)]


def from_both(array, axis, dim, width):
    size = array.shape[dim]
    tail = lax.slice_in_dim(array, size - width, size, axis=dim)
    head = lax.slice_in_dim(array, 0, width, axis=dim)
    before = lax.ppermute(tail, axis, ring(axis, 1))
    after = lax.ppermute(head, axis, ring(axis, -1))
    return before, after


def everyone(rows):
    return lax.all_to_all(rows, AXES, 0, 0, tiled=True)


def galerkin(matrix, target):
    size = len(target)
    matrix = [list(row) for row in matrix]
    target = list(target)
    scale = [matrix[i][i] for i in range(size)]
    inverse = []
    for i in range(size):
        pivot = matrix[i][i]
        usable = pivot > 1e-6 * scale[i]
        inverse.append(jnp.where(usable, 1.0 / jnp.where(usable, pivot, 1.0), 0.0))
        for j in range(i + 1, size):
            factor = matrix[i][j] * inverse[i]
            for k in range(j, size):
                matrix[j][k] = matrix[j][k] - factor * matrix[i][k]
            target[j] = target[j] - factor * target[i]
    answer = [None] * size
    for i in reversed(range(size)):
        running = target[i]
        for j in range(i + 1, size):
            running = running - matrix[i][j] * answer[j]
        answer[i] = running * inverse[i]
    return answer


DEGREE = 3
UPPER = [(a, b) for a in range(6) for b in range(a, 6)]
HALVING = (0.0625, 0.0625, 0.0625, -0.125, -0.125, -0.5)
SUMS = 14


def lanes_of(tile):
    if isinstance(tile, int):
        return pl.ds(tile * LANES, LANES)
    return pl.ds(pl.multiple_of(tile * LANES, LANES), LANES)


def beside(tile, tiles):
    if isinstance(tile, int):
        return (tile - 1) % tiles, (tile + 1) % tiles
    return jnp.where(tile == 0, tiles - 1, tile - 1), jnp.where(tile == tiles - 1, 0, tile + 1)


def x_pair(f):
    return pltpu.roll(f, 1, 0), pltpu.roll(f, f.shape[0] - 1, 0)


def spread_strains(u, v, w):
    value_u, slope_u = u[0] + u[1] + 6.0 * u[2], u[1] - u[0]
    value_v, slope_v = v[0] + v[1] + 6.0 * v[2], v[1] - v[0]
    both_w = w[0] + w[1]
    value_w, slope_w, curve_w = both_w + 6.0 * w[2], w[1] - w[0], both_w - 2.0 * w[2]
    b, a = x_pair(value_u)
    e0 = a - b
    hoop = slope_v + 0.0625 * value_w
    b, a = x_pair(hoop)
    e1 = b + a + 6.0 * hoop
    b = pltpu.roll(slope_u - value_v, 1, 0)
    a = pltpu.roll(slope_u + value_v, slope_u.shape[0] - 1, 0)
    e2 = b + a + 6.0 * slope_u
    b, a = x_pair(value_w)
    e3 = b + a - 2.0 * value_w
    b, a = x_pair(curve_w)
    e4 = b + a + 6.0 * curve_w
    b, a = x_pair(slope_w)
    e5 = a - b
    return e0, e1, e2, e3, e4, e5


def spread_forces(s):
    b, a = x_pair(s[0])
    lean_u = b - a
    b, a = x_pair(s[2])
    lean_v = b - a
    turn_u = b + a + 6.0 * s[2]
    b, a = x_pair(s[1])
    turn_v = b + a + 6.0 * s[1]
    b, a = x_pair(s[3])
    lean_w = 0.0625 * turn_v + (b + a - 2.0 * s[3])
    b, a = x_pair(s[4])
    bent_w = b + a + 6.0 * s[4]
    b, a = x_pair(s[5])
    turn_w = a - b
    sum_w = lean_w + bent_w
    return (
        (lean_u + turn_u, lean_u - turn_u, 6.0 * lean_u),
        (lean_v + turn_v, lean_v - turn_v, 6.0 * lean_v),
        (sum_w - turn_w, sum_w + turn_w, 6.0 * lean_w - 2.0 * bent_w),
    )


def chosen(layers, bits):
    if len(layers) == 1:
        return layers[0]
    half = len(layers) // 2
    return jnp.where(bits[-1], chosen(layers[half:], bits[:-1]), chosen(layers[:half], bits[:-1]))


MARGIN = 2
FIELDS = 8
PADDED = 16
PIECES = 3
GROUP = 9
PARTS = 3


def triples_of(centre, before, after, tile, tiles, first, final):
    at = lanes_of(tile)
    left, right = beside(tile, tiles)
    at_left, at_right = lanes_of(left), lanes_of(right)
    return [
        (
            jnp.where(first, before[c, :, at_left], before[c, :, at]),
            jnp.where(final, after[c, :, at_right], after[c, :, at]),
            centre[c, :, at],
        )
        for c in range(3)
    ]


def mixed(values, e):
    s = [None] * 6
    for n, (a, b) in enumerate(UPPER):
        for p, q in ((a, b), (b, a))[: 1 if a == b else 2]:
            term = values[n] * e[q]
            s[p] = term if s[p] is None else s[p] + term
    return s


def contract(left, right, left_dim, right_dim):
    return lax.dot_general(
        left, right, (((left_dim,), (right_dim,)), ((), ())), preferred_element_type=jnp.float32
    )


def widened(x):
    return jnp.concatenate([x, jnp.zeros_like(x)], axis=0).astype(jnp.bfloat16)


def learn(x, w_first, w_mid, w_last, keep=None):
    h = jnp.tanh(contract(x, w_first[...], 0, 0)).astype(jnp.bfloat16)
    if keep is not None:
        keep(0, h)
    for k in range(w_mid.shape[0]):
        h = jnp.tanh(contract(h, w_mid[k], 1, 1)).astype(jnp.bfloat16)
        if keep is not None:
            keep(k + 1, h)
    return contract(w_last[...], h, 1, 1)[:FIELDS]


def pieces_of(cols):
    step = cols
    while step > 2048 and step % 256 == 0:
        step //= 2
    return [(at, step) for at in range(0, cols, step)]


def gathered(array, row, spread, at, size):
    tiles = range(at // LANES, (at + size) // LANES)
    return jnp.concatenate(
        [array[t, pl.ds(row, FIELDS, stride=spread), :] for t in tiles], axis=1
    )


def layer_copy(k, base, span, source, target, flag):
    here = pl.ds(base, span)
    return pltpu.make_async_copy(source.at[k, here, :], target.at[k, here, :], flag)


def learn_lines(
    rows, rims, kept, base, strain, learned, spread, cols, weights, hidden, stored, inputs, flags
):
    rim = cols // LANES
    parts = [gathered(strain, row, spread, 0, cols) for row in rows]
    parts += [strain[rim, pl.ds(row, FIELDS, stride=spread), :] for row in rims]
    x = widened(jnp.concatenate(parts, axis=1))
    start, span = base * cols, kept * cols
    inputs[:, pl.ds(start, span)] = x[:, :span]
    copies = []

    def keep(k, h):
        hidden[k, pl.ds(start, span), :] = h[:span]
        copies.append(layer_copy(k, start, span, hidden, stored, flags[k]))
        copies[-1].start()

    out = learn(x, *weights, keep)
    for n, row in enumerate(rows):
        for t in range(rim):
            at = n * cols + t * LANES
            learned[t, pl.ds(row, FIELDS, stride=spread), :] = out[:, at : at + LANES]
    for n, row in enumerate(rims):
        at = len(rows) * cols + n * LANES
        learned[rim, pl.ds(row, FIELDS, stride=spread), :] = out[:, at : at + LANES]
    return copies


def line_copy(line, cols, source, target, flags):
    where = line * cols
    if not isinstance(where, int):
        where = pl.multiple_of(where, LANES)
    here = pl.ds(where, cols)
    return pltpu.make_async_copy(source.at[:, here, :], target.at[:, here, :], flags.at[line])


def inner_kernel(
    fields, ends, w_mid, learned, stored, inputs, before, after, strain, hidden, flags
):
    rows, wide = fields.shape[1], fields.shape[2]
    tiles = wide // LANES
    cols = wide - LANES
    lane = lax.broadcasted_iota(jnp.int32, (rows, LANES), 1)
    first, final = lane == 0, lane == LANES - 1

    def set_up(tile, carry):
        at = lanes_of(tile)
        for c in range(3):
            value = fields[c, :, at]
            before[c, :, at] = pltpu.roll(value, 1, 1)
            after[c, :, at] = pltpu.roll(value, LANES - 1, 1)
        return carry

    lax.fori_loop(0, tiles, set_up, 0)

    def strains(tile, carry):
        at = lanes_of(tile)
        e = spread_strains(*triples_of(fields.at[0:3], before, after, tile, tiles, first, final))
        for n in range(FIELDS):
            value = HALVING[n] * e[n] if n < 6 else jnp.zeros((rows, LANES), jnp.float32)
            strain[tile, n * rows : (n + 1) * rows] = value
        return carry

    lax.fori_loop(0, tiles, strains, 0)
    weights = (ends.at[0:PADDED], w_mid, ends.at[PADDED : 2 * PADDED])
    inside = list(range(1, rows - 1))
    share = -(-len(inside) // PARTS)
    levels = w_mid.shape[0] + 1
    copies = []
    for n in range(PARTS):
        mine = inside[n * share : (n + 1) * share]
        copies += learn_lines(
            mine, inside if n == PARTS - 1 else [], len(mine), n * share,
            strain, learned, rows, cols, weights, hidden, stored, inputs,
            [flags.at[n * levels + k] for k in range(levels)],
        )
    for copy in copies:
        copy.wait()


def stiffness_of(table, ids, depth, target, at):
    layups = table.shape[0] // 36
    bits = [(ids & (1 << k)) != 0 for k in range(depth)]
    for n, (a, b) in enumerate(UPPER):
        layers = [table[min(l, layups - 1) * 36 + a * 6 + b] for l in range(1 << depth)]
        target[n, :, at] = jnp.broadcast_to(chosen(layers, bits), ids.shape)


def depth_of(table):
    depth = 1
    while (1 << depth) < table.shape[0] // 36:
        depth += 1
    return depth


def prepare_kernel(table, fields, fl_up, fl_down, stiff, support):
    rows, wide = fields.shape[1], fields.shape[2]
    halo = fl_up.shape[1]
    edge = jnp.zeros((rows - halo, LANES), jnp.float32)

    def fill(tile, carry):
        at = lanes_of(tile)
        around = [
            jnp.concatenate(
                [edge, fl_up[c, :, at], fields[3 + c, :, at], fl_down[c, :, at], edge], axis=0
            )
            for c in range(4)
        ]
        for c in range(3):
            support[c, :, at] = around[c]
        stiffness_of(table, around[3].astype(jnp.int32), depth_of(table), stiff, at)
        return carry

    lax.fori_loop(0, wide // LANES, fill, 0)


def outer_kernel(
    table, fields, up, down, inner, ends, w_mid,
    residual, own_residual, stored, inputs,
    centre, before, after, ahead, behind, middle, strain, learned, stiff, shifts, hidden, flags,
):
    rows, wide = fields.shape[1], fields.shape[2]
    tiles = wide // LANES
    cols = wide - LANES
    tall = 3 * rows
    lane = lax.broadcasted_iota(jnp.int32, (tall, LANES), 1)
    first, final = lane == 0, lane == LANES - 1
    rim = jnp.zeros((rows - MARGIN, LANES), jnp.float32)
    last = 3 * MARGIN

    def set_up(tile, carry):
        at = lanes_of(tile)
        for c in range(3):
            above, below = up[MARGIN * c : MARGIN * (c + 1), at], down[MARGIN * c : MARGIN * (c + 1), at]
            value = jnp.concatenate([rim, above, fields[c, :, at], below, rim], axis=0)
            centre[c, :, at] = value
        wall = jnp.zeros((rows - 1, LANES), jnp.float32)
        ids = jnp.concatenate(
            [wall, up[last : last + 1, at], fields[6, :, at], down[last : last + 1, at], wall],
            axis=0,
        ).astype(jnp.int32)
        stiffness_of(table, ids, depth_of(table), stiff, at)
        return carry

    fill_shifts(shifts)
    lax.fori_loop(0, tiles, set_up, 0)
    shift_both(centre, before, after, shifts)

    def strains(tile, carry):
        at = lanes_of(tile)
        e = spread_strains(*triples_of(centre, before, after, tile, tiles, first, final))
        for n in range(FIELDS):
            value = HALVING[n] * e[n] if n < 6 else jnp.zeros((tall, LANES), jnp.float32)
            strain[tile, n * tall : (n + 1) * tall] = value
        for n in range(6):
            learned[tile, n * tall + rows + 1 : n * tall + 2 * rows - 1] = inner[
                tile, n * rows + 1 : (n + 1) * rows - 1
            ]
        return carry

    lax.fori_loop(0, tiles, strains, 0)
    weights = (ends.at[0:PADDED], w_mid, ends.at[PADDED : 2 * PADDED])
    lines = (rows, 2 * rows - 1, rows - 1, 2 * rows)
    copies = learn_lines(
        lines, lines, 2, 0, strain, learned, tall, cols, weights, hidden, stored, inputs,
        [flags.at[k] for k in range(w_mid.shape[0] + 1)],
    )

    def push(tile, carry):
        at = lanes_of(tile)
        e = [strain[tile, n * tall : (n + 1) * tall] * (1.0 / HALVING[n]) for n in range(6)]
        s = mixed([stiff[n, :, at] for n in range(len(UPPER))], e)
        s = [s[n] + HALVING[n] * learned[tile, n * tall : (n + 1) * tall] for n in range(6)]
        for c, (alpha, beta, gamma) in enumerate(spread_forces(s)):
            ahead[c, :, at] = alpha
            behind[c, :, at] = beta
            middle[c, :, at] = gamma
        return carry

    lax.fori_loop(0, tiles, push, 0)
    shift_in_place(ahead, 0, shifts)
    shift_in_place(behind, 1, shifts)
    own = slice(rows, 2 * rows)

    def finish(tile, carry):
        at = lanes_of(tile)
        left, right = beside(tile, tiles)
        at_left, at_right = lanes_of(left), lanes_of(right)
        for c in range(3):
            value = (
                middle[c, own, at]
                + jnp.where(first[:rows], ahead[c, own, at_left], ahead[c, own, at])
                + jnp.where(final[:rows], behind[c, own, at_right], behind[c, own, at])
            )
            value = value + fields[3 + c, :, at] * fields[c, :, at] - fields[7 + c, :, at]
            residual[c, :, at] = value
            if carry is not None:
                own_residual[c, :, at] = value
        return carry

    lax.fori_loop(0, tiles - 1, finish, 0)
    finish(tiles - 1, None)
    for copy in copies:
        copy.wait()


def solve(numbers, sums, kept, bends, adjoint, upstream):
    rows = adjoint.shape[1]
    own_tiles = upstream.shape[0]
    line = jnp.sum(sums[...], axis=0)
    picks = [jnp.broadcast_to(line[:, n : n + 1], (1, LANES)) for n in range(SUMS)]
    centre = [numbers[k] for k in range(3)]
    width = [numbers[3 + k] for k in range(3)]
    matrix = [[None] * 4 for _ in range(4)]
    for k in range(3):
        for j in range(k + 1):
            matrix[j][k] = picks[4 + k * (k + 1) // 2 + j]
    cross = [picks[3], picks[10], picks[11], picks[12]]
    for j in range(3):
        value = width[j] * cross[j + 1] + centre[j] * cross[j]
        matrix[j][3] = value + width[j - 1] * cross[j - 1] if j else value
    matrix[3][3] = picks[13]
    weights = [jnp.broadcast_to(x, (rows, LANES)) for x in galerkin(matrix, picks[:4])]

    def weighted(parts):
        total = weights[0] * parts[0]
        for weight, part in zip(weights[1:], parts[1:]):
            total = total + weight * part
        return total

    levels = range(DEGREE + 1)

    def combine(tile, carry):
        at = lanes_of(tile)
        for c in range(3):
            adjoint[c, :, at] = weighted([kept[k, c, :, at] for k in levels])
        for n in range(6):
            here = slice(n * rows, (n + 1) * rows)
            upstream[tile, here] = HALVING[n] * weighted([bends[k, tile, here] for k in levels])
        upstream[tile, 6 * rows :] = jnp.zeros(((FIELDS - 6) * rows, LANES), jnp.float32)
        return carry

    lax.fori_loop(0, own_tiles, combine, 0)


def slope_of(signal, h):
    h = h.astype(jnp.float32)
    return (signal * (1.0 - h * h)).astype(jnp.bfloat16)


def backward_kernel(
    numbers, sums, kept, bends, inner_hidden, inner_inputs, outer_hidden, outer_inputs, w_mid,
    ends, adjoint, packed,
    upstream, grads, near_hidden, far_hidden, near_flags, far_flags,
):
    layers = w_mid.shape[0]
    hid = w_mid.shape[1]
    cols = upstream.shape[0] * LANES
    rows = upstream.shape[1] // FIELDS
    last_at = layers * hid
    first_at = last_at + FIELDS
    for n in range(rows - 2):
        line_copy(n, cols, inner_hidden, near_hidden, near_flags).start()
    for n in range(2):
        line_copy(n, cols, outer_hidden, far_hidden, far_flags).start()
    grads[...] = jnp.zeros_like(grads)
    solve(numbers, sums, kept, bends, adjoint, upstream)

    def line(row, at_line, hidden, inputs):
        for at, size in pieces_of(cols):
            where = at_line * cols + at
            if not isinstance(where, int):
                where = pl.multiple_of(where, LANES)
            here = pl.ds(where, size)
            signal = widened(gathered(upstream, row, rows, at, size))
            h = hidden[layers, here, :]
            grads[last_at : last_at + FIELDS] += contract(signal, h, 1, 0)[:FIELDS]
            d = slope_of(contract(signal, ends[PADDED : 2 * PADDED], 0, 0), h)
            for k in range(layers - 1, -1, -1):
                h = hidden[k, here, :]
                grads[k * hid : (k + 1) * hid] += contract(d, h, 0, 0)
                d = slope_of(contract(d, w_mid[k], 1, 0), h)
            grads[first_at : first_at + FIELDS] += contract(inputs[:, here], d, 1, 0)[:FIELDS]

    def inside(row, carry):
        line_copy(row - 1, cols, inner_hidden, near_hidden, near_flags).wait()
        line(row, row - 1, near_hidden, inner_inputs)
        return carry

    lax.fori_loop(1, rows - 1, inside, 0)
    for n, row in enumerate((0, rows - 1)):
        line_copy(n, cols, outer_hidden, far_hidden, far_flags).wait()
        line(row, n, far_hidden, outer_inputs)
    chunk = packed.shape[1]
    for n in range(packed.shape[0]):
        for r in range(chunk):
            packed[n, r] = grads[n * chunk + r : n * chunk + r + 1]


def gather_kernel(parts, total):
    total[...] = jnp.broadcast_to(jnp.sum(parts[...], axis=0, keepdims=True), total.shape)


def deliver_kernel(parts, grad_first, grad_mid, grad_last, flat):
    chunk = parts.shape[1]
    for n in range(parts.shape[0]):
        for r in range(chunk):
            flat[n * chunk + r : n * chunk + r + 1] = parts[n, r]
    layers, hid = grad_mid.shape[0], grad_mid.shape[1]
    for k in range(layers):
        grad_mid[k] = flat[k * hid : (k + 1) * hid]
    at = layers * hid
    grad_last[...] = flat[at : at + FIELDS][: grad_last.shape[0]]
    grad_first[...] = flat[at + FIELDS : at + 2 * FIELDS][: grad_first.shape[0]]


def fill_shifts(shifts):
    shape = (PIECES * LANES, LANES)
    source = lax.broadcasted_iota(jnp.int32, shape, 0) % LANES
    target = lax.broadcasted_iota(jnp.int32, shape, 1)
    for n, step in enumerate((1, LANES - 1)):
        hit = (source + step) % LANES == target
        shifts[:, n * LANES : (n + 1) * LANES] = jnp.where(hit, 1.0, 0.0).astype(jnp.bfloat16)


def pieces(x):
    parts = []
    for n in range(PIECES):
        part = x.astype(jnp.bfloat16)
        parts.append(part)
        if n + 1 < PIECES:
            x = x - part.astype(jnp.float32)
    return jnp.concatenate(parts, axis=1)


def groups_of(array):
    tiles = array.shape[2] // LANES
    return [range(t, min(t + GROUP, tiles)) for t in range(0, tiles, GROUP)]


def stacked(source, group):
    return pieces(
        jnp.concatenate([source[c, :, lanes_of(t)] for t in group for c in range(3)], axis=0)
    )


def shift_both(source, before, after, shifts):
    tall = source.shape[1]
    for group in groups_of(source):
        moved = contract(stacked(source, group), shifts[...], 1, 0)
        for n, tile in enumerate(group):
            for c in range(3):
                at = (3 * n + c) * tall
                before[c, :, lanes_of(tile)] = moved[at : at + tall, :LANES]
                after[c, :, lanes_of(tile)] = moved[at : at + tall, LANES:]


def shift_in_place(array, side, shifts):
    tall = array.shape[1]
    for group in groups_of(array):
        moved = contract(stacked(array, group), shifts[:, side * LANES : (side + 1) * LANES], 1, 0)
        for n, tile in enumerate(group):
            for c in range(3):
                at = (3 * n + c) * tall
                array[c, :, lanes_of(tile)] = moved[at : at + tall]


def krylov_kernel(
    numbers, r_mid, r_up, r_down, stiff, support, kept, bends, sums,
    basis, before, after, ahead, behind, middle, shifts,
):
    rows = r_mid.shape[1]
    wide = r_mid.shape[2]
    tiles = wide // LANES
    own_tiles = tiles - 1
    tall = 3 * rows
    lane = lax.broadcasted_iota(jnp.int32, (tall, LANES), 1)
    first, final = lane == 0, lane == LANES - 1

    def place(k, c, at, value):
        basis[k, c, :, at] = value
        kept[k, c, :, at] = value[rows : 2 * rows]

    def set_up(tile, carry):
        at = lanes_of(tile)
        for c in range(3):
            value = jnp.concatenate([r_up[c, :, at], r_mid[c, :, at], r_down[c, :, at]], axis=0)
            place(0, c, at, value)
        return carry

    fill_shifts(shifts)
    lax.fori_loop(0, tiles, set_up, 0)
    shift_both(basis.at[0], before, after, shifts)

    def strain_of(k, tile):
        e = spread_strains(*triples_of(basis.at[k], before, after, tile, tiles, first, final))
        for n in range(6):
            bends[k, tile, n * rows : (n + 1) * rows] = e[n][rows : 2 * rows]
        return e

    def stress_of(e, at):
        return mixed([stiff[n, :, at] for n in range(len(UPPER))], e)

    def mine(value):
        return value[rows : 2 * rows]

    zero = jnp.zeros((rows, LANES), jnp.float32)
    totals = [None] * SUMS

    for k in range(DEGREE):
        def push(tile, carry, k=k):
            at = lanes_of(tile)
            for c, (alpha, beta, gamma) in enumerate(
                spread_forces(stress_of(strain_of(k, tile), at))
            ):
                ahead[c, :, at] = alpha
                behind[c, :, at] = beta
                middle[c, :, at] = gamma
            return carry

        lax.fori_loop(0, tiles, push, 0)
        shift_in_place(ahead, 0, shifts)
        shift_in_place(behind, 1, shifts)

        centre, inverse = numbers[k], numbers[6 + k]
        former = numbers[2 + k]

        def advance(tile, carry, k=k):
            at = lanes_of(tile)
            left, right = beside(tile, tiles)
            at_left, at_right = lanes_of(left), lanes_of(right)
            image, here, following = [], [], []
            for c in range(3):
                vector = basis[k, c, :, at]
                value = (
                    middle[c, :, at]
                    + jnp.where(first, ahead[c, :, at_left], ahead[c, :, at])
                    + jnp.where(final, behind[c, :, at_right], behind[c, :, at])
                    + support[c, :, at] * vector
                )
                step = value - centre * vector
                if k:
                    step = step - former * basis[k - 1, c, :, at]
                step = step * inverse
                place(k + 1, c, at, step)
                image.append(mine(value))
                here.append(mine(vector))
                following.append(mine(step))
            if carry is None:
                return None

            def dot(left_side, right_side):
                return (
                    left_side[0] * right_side[0]
                    + left_side[1] * right_side[1]
                    + left_side[2] * right_side[2]
                )

            def old(m):
                return [basis[m, c, rows : 2 * rows, at] for c in range(3)]

            fresh = []
            origin = here if k == 0 else old(0)
            if k == 0:
                fresh.append(dot(here, here))
            fresh.append(dot(origin, following))
            for j in range(k + 1):
                fresh.append(dot(here if j == k else (origin if j == 0 else old(j)), image))
            if k == DEGREE - 1:
                fresh.append(dot(old(1), following))
                fresh.append(dot(here, following))
                fresh.append(dot(following, following))
            return tuple(p + q for p, q in zip(carry, fresh))

        names = ([0] if k == 0 else []) + [k + 1] + [4 + k * (k + 1) // 2 + j for j in range(k + 1)]
        if k == DEGREE - 1:
            names += [10, 11, 12]
        found = lax.fori_loop(0, own_tiles, advance, (zero,) * len(names))
        advance(own_tiles, None)
        shift_both(basis.at[k + 1], before, after, shifts)
        for name, value in zip(names, found):
            totals[name] = value

    def energy(tile, running):
        at = lanes_of(tile)
        e = strain_of(DEGREE, tile)
        e = [mine(value) for value in e]
        for n, (a, b) in enumerate(UPPER):
            term = stiff[n, rows : 2 * rows, at] * e[b] * e[a]
            running = running + (term if a == b else 2.0 * term)
        for c in range(3):
            vector = basis[DEGREE, c, rows : 2 * rows, at]
            running = running + support[c, rows : 2 * rows, at] * vector * vector
        return running

    totals[13] = lax.fori_loop(0, own_tiles, energy, zero)
    place_of = lax.broadcasted_iota(jnp.int32, (1, LANES), 1)
    line = jnp.zeros((1, LANES), jnp.float32)
    for n in range(SUMS):
        total = jnp.sum(jnp.sum(totals[n], axis=0, keepdims=True), axis=1, keepdims=True)
        line = jnp.where(place_of == n, jnp.broadcast_to(total, (1, LANES)), line)
    sums[...] = jnp.broadcast_to(line[None], sums.shape)


def basis_constants(layup_stiffness):
    bending = 0.5 * (jnp.mean(layup_stiffness[:, 3, 3]) + jnp.mean(layup_stiffness[:, 4, 4]))
    centres = [11.5 * bending + 1.1, 9.8 * bending + 1.1, 8.4 * bending + 1.1]
    widths = [3.9 * bending + 0.4, 5.6 * bending + 0.4, 4.8 * bending + 0.4]
    return centres, widths


ON_CHIP = pl.BlockSpec(memory_space=pltpu.VMEM)
SCALARS = pl.BlockSpec(memory_space=pltpu.SMEM)


IN_PLACE = pl.BlockSpec(memory_space=pltpu.HBM)


def kernel_call(body, name, scalars, outs, scratch, *operands, far=(), far_outs=()):
    specs = [SCALARS] * scalars + [ON_CHIP] * (len(operands) - scalars)
    for n in far:
        specs[n] = IN_PLACE
    return pl.pallas_call(
        body,
        in_specs=specs,
        out_specs=[IN_PLACE if n in far_outs else ON_CHIP for n in range(len(outs))],
        out_shape=[
            pltpu.HBM(*out) if n in far_outs else jax.ShapeDtypeStruct(*out)
            for n, out in enumerate(outs)
        ],
        scratch_shapes=[
            pltpu.VMEM(*s) if isinstance(s, tuple) else pltpu.SemaphoreType.DMA((s,))
            for s in scratch
        ],
        compiler_params=pltpu.CompilerParams(vmem_limit_bytes=LIMITS[name] << 20),
    )(*[
        pltpu.with_memory_space_constraint(x, pltpu.HBM) if n in far else x
        for n, x in enumerate(operands)
    ])


LIMITS = {
    "inner": 40, "outer": 40, "prepare": 8, "krylov": 10, "backward": 32, "gather": 4, "deliver": 4,
}


def per_device(displacement, load, foundation, layup, layup_stiffness, w_first, w_mid, w_last):
    f32, bf16 = jnp.float32, jnp.bfloat16
    rows, cols = layup.shape
    layers, hid = w_mid.shape[0], w_mid.shape[1]
    devices = lax.axis_size("patch") * lax.axis_size("sub")
    wide = cols + LANES
    tall = 3 * rows
    tiles = wide // LANES
    fields = jnp.concatenate([displacement, foundation, layup.astype(f32)[None], load])
    before, after = from_both(fields, "sub", 2, HY)
    gap = jnp.zeros(fields.shape[:2] + (LANES - 2 * HY,), f32)
    fields = jnp.concatenate([fields, after, gap, before], axis=2)
    sends = [
        jnp.concatenate([*[fields[c, edge] for c in range(3)], fields[6, edge][near]])
        for edge, near in ((slice(rows - MARGIN, rows), slice(1, 2)), (slice(0, MARGIN), slice(0, 1)))
    ]
    up = lax.ppermute(sends[0], "patch", ring("patch", 1))
    down = lax.ppermute(sends[1], "patch", ring("patch", -1))
    fl_up, fl_down = from_both(fields[3:7], "patch", 1, 6)

    halving = jnp.array(HALVING, f32)
    table = (layup_stiffness * halving[:, None] * halving[None, :]).reshape(-1)
    centres, widths = basis_constants(layup_stiffness)
    numbers = jnp.stack(centres + widths + [1.0 / x for x in widths])
    thin = w_first.shape[1]
    blank = jnp.zeros((PADDED - thin, hid), bf16)
    ends = jnp.concatenate([w_first.T, blank, w_last, blank])

    learned, inner_hidden, inner_inputs = kernel_call(
        inner_kernel, "inner", 0,
        [((tiles, FIELDS * rows, LANES), f32), ((layers + 1, (rows - 2) * cols, hid), bf16),
         ((PADDED, (rows - 2) * cols), bf16)],
        [((3, rows, wide), f32)] * 2
        + [((tiles, FIELDS * rows, LANES), f32), ((layers + 1, (rows - 2) * cols, hid), bf16),
           PARTS * (layers + 1)],
        fields, ends, w_mid, far_outs=(1,),
    )
    wide_residual, residual, outer_hidden, outer_inputs = kernel_call(
        outer_kernel, "outer", 1,
        [((3, rows, wide), f32), ((3, rows, cols), f32),
         ((layers + 1, 2 * cols, hid), bf16), ((PADDED, 2 * cols), bf16)],
        [((3, tall, wide), f32)] * 6
        + [((tiles, FIELDS * tall, LANES), f32)] * 2
        + [((len(UPPER), tall, wide), f32), ((PIECES * LANES, 2 * LANES), bf16),
           ((layers + 1, 2 * cols, hid), bf16), layers + 1],
        table, fields, up, down, learned, ends, w_mid, far_outs=(2,),
    )
    stiff, support = kernel_call(
        prepare_kernel, "prepare", 1,
        [((len(UPPER), tall, wide), f32), ((3, tall, wide), f32)], [],
        table, fields, fl_up, fl_down,
    )
    up, down = from_both(wide_residual, "patch", 1, rows)
    kept, bends, sums = kernel_call(
        krylov_kernel, "krylov", 1,
        [((DEGREE + 1, 3, rows, wide), f32), ((DEGREE + 1, tiles, 6 * rows, LANES), f32),
         ((devices, 1, LANES), f32)],
        [((DEGREE + 1, 3, tall, wide), f32)] + [((3, tall, wide), f32)] * 5
        + [((PIECES * LANES, 2 * LANES), bf16)],
        numbers, wide_residual, up, down, stiff, support,
    )
    sums = everyone(sums)
    count = layers * hid + 2 * FIELDS
    chunk = -(-count // devices)
    adjoint, packed = kernel_call(
        backward_kernel, "backward", 1,
        [((3, rows, cols), f32), ((devices, chunk, 1, LANES), f32)],
        [((tiles - 1, FIELDS * rows, LANES), f32),
         ((devices * chunk, LANES), f32), ((layers + 1, (rows - 2) * cols, hid), bf16),
         ((layers + 1, 2 * cols, hid), bf16), rows - 2, 2],
        numbers, sums, kept, bends, inner_hidden, inner_inputs, outer_hidden, outer_inputs,
        w_mid, ends, far=(4, 6),
    )
    (total,) = kernel_call(
        gather_kernel, "gather", 0, [(packed.shape, f32)], [], everyone(packed)
    )
    grad_first, grad_mid, grad_last = kernel_call(
        deliver_kernel, "deliver", 0,
        [((thin, hid), f32), (w_mid.shape, f32), (w_last.shape, f32)],
        [((devices * chunk, LANES), f32)],
        everyone(total),
    )
    return residual, adjoint, grad_first.T, grad_mid, grad_last


def solution(mesh):
    field = P(None, "patch", "sub")
    return jax.shard_map(
        per_device,
        mesh=mesh,
        in_specs=(field, field, field, P("patch", "sub"), P(), P(), P(), P()),
        out_specs=(field, field, P(), P(), P()),
        check_vma=False,
    )
```

```python
import jax
import jax.numpy as jnp
from jax import lax
from jax.experimental import pallas as pl
from jax.experimental.pallas import tpu as pltpu
from jax.sharding import PartitionSpec as P


HY = 16
LANES = 128
AXES = ("patch", "sub")


def ring(axis, step):
    count = lax.axis_size(axis)
    return [(i, (i + step) % count) for i in range(count)]


def from_both(array, axis, dim, width):
    size = array.shape[dim]
    tail = lax.slice_in_dim(array, size - width, size, axis=dim)
    head = lax.slice_in_dim(array, 0, width, axis=dim)
    before = lax.ppermute(tail, axis, ring(axis, 1))
    after = lax.ppermute(head, axis, ring(axis, -1))
    return before, after


def everyone(rows):
    return lax.all_to_all(rows, AXES, 0, 0, tiled=True)


def galerkin(matrix, target):
    size = len(target)
    matrix = [list(row) for row in matrix]
    target = list(target)
    scale = [matrix[i][i] for i in range(size)]
    inverse = []
    for i in range(size):
        pivot = matrix[i][i]
        usable = pivot > 1e-6 * scale[i]
        inverse.append(jnp.where(usable, 1.0 / jnp.where(usable, pivot, 1.0), 0.0))
        for j in range(i + 1, size):
            factor = matrix[i][j] * inverse[i]
            for k in range(j, size):
                matrix[j][k] = matrix[j][k] - factor * matrix[i][k]
            target[j] = target[j] - factor * target[i]
    answer = [None] * size
    for i in reversed(range(size)):
        running = target[i]
        for j in range(i + 1, size):
            running = running - matrix[i][j] * answer[j]
        answer[i] = running * inverse[i]
    return answer


DEGREE = 3
UPPER = [(a, b) for a in range(6) for b in range(a, 6)]
HALVING = (0.0625, 0.0625, 0.0625, -0.125, -0.125, -0.5)
SUMS = 14


def lanes_of(tile):
    if isinstance(tile, int):
        return pl.ds(tile * LANES, LANES)
    return pl.ds(pl.multiple_of(tile * LANES, LANES), LANES)


def beside(tile, tiles):
    if isinstance(tile, int):
        return (tile - 1) % tiles, (tile + 1) % tiles
    return jnp.where(tile == 0, tiles - 1, tile - 1), jnp.where(tile == tiles - 1, 0, tile + 1)


def x_pair(f):
    return pltpu.roll(f, 1, 0), pltpu.roll(f, f.shape[0] - 1, 0)


def spread_strains(u, v, w):
    value_u, slope_u = u[0] + u[1] + 6.0 * u[2], u[1] - u[0]
    value_v, slope_v = v[0] + v[1] + 6.0 * v[2], v[1] - v[0]
    both_w = w[0] + w[1]
    value_w, slope_w, curve_w = both_w + 6.0 * w[2], w[1] - w[0], both_w - 2.0 * w[2]
    b, a = x_pair(value_u)
    e0 = a - b
    hoop = slope_v + 0.0625 * value_w
    b, a = x_pair(hoop)
    e1 = b + a + 6.0 * hoop
    b = pltpu.roll(slope_u - value_v, 1, 0)
    a = pltpu.roll(slope_u + value_v, slope_u.shape[0] - 1, 0)
    e2 = b + a + 6.0 * slope_u
    b, a = x_pair(value_w)
    e3 = b + a - 2.0 * value_w
    b, a = x_pair(curve_w)
    e4 = b + a + 6.0 * curve_w
    b, a = x_pair(slope_w)
    e5 = a - b
    return e0, e1, e2, e3, e4, e5


def spread_forces(s):
    b, a = x_pair(s[0])
    lean_u = b - a
    b, a = x_pair(s[2])
    lean_v = b - a
    turn_u = b + a + 6.0 * s[2]
    b, a = x_pair(s[1])
    turn_v = b + a + 6.0 * s[1]
    b, a = x_pair(s[3])
    lean_w = 0.0625 * turn_v + (b + a - 2.0 * s[3])
    b, a = x_pair(s[4])
    bent_w = b + a + 6.0 * s[4]
    b, a = x_pair(s[5])
    turn_w = a - b
    sum_w = lean_w + bent_w
    return (
        (lean_u + turn_u, lean_u - turn_u, 6.0 * lean_u),
        (lean_v + turn_v, lean_v - turn_v, 6.0 * lean_v),
        (sum_w - turn_w, sum_w + turn_w, 6.0 * lean_w - 2.0 * bent_w),
    )


def chosen(layers, bits):
    if len(layers) == 1:
        return layers[0]
    half = len(layers) // 2
    return jnp.where(bits[-1], chosen(layers[half:], bits[:-1]), chosen(layers[:half], bits[:-1]))


MARGIN = 2
FIELDS = 8
PADDED = 16
PIECES = 3
GROUP = 9
PARTS = 3


def triples_of(centre, before, after, tile, tiles, first, final):
    at = lanes_of(tile)
    left, right = beside(tile, tiles)
    at_left, at_right = lanes_of(left), lanes_of(right)
    return [
        (
            jnp.where(first, before[c, :, at_left], before[c, :, at]),
            jnp.where(final, after[c, :, at_right], after[c, :, at]),
            centre[c, :, at],
        )
        for c in range(3)
    ]


def mixed(values, e):
    s = [None] * 6
    for n, (a, b) in enumerate(UPPER):
        for p, q in ((a, b), (b, a))[: 1 if a == b else 2]:
            term = values[n] * e[q]
            s[p] = term if s[p] is None else s[p] + term
    return s


def contract(left, right, left_dim, right_dim):
    return lax.dot_general(
        left, right, (((left_dim,), (right_dim,)), ((), ())), preferred_element_type=jnp.float32
    )


def widened(x):
    return jnp.concatenate([x, jnp.zeros_like(x)], axis=0).astype(jnp.bfloat16)


def learn(x, w_first, w_mid, w_last, keep=None):
    h = jnp.tanh(contract(x, w_first[...], 0, 0)).astype(jnp.bfloat16)
    if keep is not None:
        keep(0, h)
    for k in range(w_mid.shape[0]):
        h = jnp.tanh(contract(h, w_mid[k], 1, 1)).astype(jnp.bfloat16)
        if keep is not None:
            keep(k + 1, h)
    return contract(w_last[...], h, 1, 1)[:FIELDS]


def pieces_of(cols):
    step = cols
    while step > 2048 and step % 256 == 0:
        step //= 2
    return [(at, step) for at in range(0, cols, step)]


def gathered(array, row, spread, at, size):
    tiles = range(at // LANES, (at + size) // LANES)
    return jnp.concatenate(
        [array[t, pl.ds(row, FIELDS, stride=spread), :] for t in tiles], axis=1
    )


def layer_copy(k, base, span, source, target, flag):
    here = pl.ds(base, span)
    return pltpu.make_async_copy(source.at[k, here, :], target.at[k, here, :], flag)


def learn_lines(
    rows, rims, kept, base, strain, learned, spread, cols, weights, hidden, stored, inputs, flags
):
    rim = cols // LANES
    parts = [gathered(strain, row, spread, 0, cols) for row in rows]
    parts += [strain[rim, pl.ds(row, FIELDS, stride=spread), :] for row in rims]
    x = widened(jnp.concatenate(parts, axis=1))
    start, span = base * cols, kept * cols
    inputs[:, pl.ds(start, span)] = x[:, :span]
    copies = []

    def keep(k, h):
        hidden[k, pl.ds(start, span), :] = h[:span]
        copies.append(layer_copy(k, start, span, hidden, stored, flags[k]))
        copies[-1].start()

    out = learn(x, *weights, keep)
    for n, row in enumerate(rows):
        for t in range(rim):
            at = n * cols + t * LANES
            learned[t, pl.ds(row, FIELDS, stride=spread), :] = out[:, at : at + LANES]
    for n, row in enumerate(rims):
        at = len(rows) * cols + n * LANES
        learned[rim, pl.ds(row, FIELDS, stride=spread), :] = out[:, at : at + LANES]
    return copies


def line_copy(line, cols, source, target, flags):
    where = line * cols
    if not isinstance(where, int):
        where = pl.multiple_of(where, LANES)
    here = pl.ds(where, cols)
    return pltpu.make_async_copy(source.at[:, here, :], target.at[:, here, :], flags.at[line])


def assemble_kernel(displacement, foundation, layup, load, fields, ids, flags):
    moves = ((layup, ids), (displacement, fields.at[0:3]), (foundation, fields.at[3:6]),
             (load, fields.at[7:10]))
    copies = [pltpu.make_async_copy(a, b, flags.at[n]) for n, (a, b) in enumerate(moves)]
    for copy in copies:
        copy.start()
    copies[0].wait()
    fields[6] = ids[...].astype(jnp.float32)
    for copy in copies[1:]:
        copy.wait()


def inner_kernel(
    fields, ends, w_mid, learned, stored, inputs, before, after, strain, hidden, flags
):
    rows, wide = fields.shape[1], fields.shape[2]
    tiles = wide // LANES
    cols = wide - LANES
    lane = lax.broadcasted_iota(jnp.int32, (rows, LANES), 1)
    first, final = lane == 0, lane == LANES - 1

    def set_up(tile, carry):
        at = lanes_of(tile)
        for c in range(3):
            value = fields[c, :, at]
            before[c, :, at] = pltpu.roll(value, 1, 1)
            after[c, :, at] = pltpu.roll(value, LANES - 1, 1)
        return carry

    lax.fori_loop(0, tiles, set_up, 0)

    def strains(tile, carry):
        at = lanes_of(tile)
        e = spread_strains(*triples_of(fields.at[0:3], before, after, tile, tiles, first, final))
        for n in range(FIELDS):
            value = HALVING[n] * e[n] if n < 6 else jnp.zeros((rows, LANES), jnp.float32)
            strain[tile, n * rows : (n + 1) * rows] = value
        return carry

    lax.fori_loop(0, tiles, strains, 0)
    weights = (ends.at[0:PADDED], w_mid, ends.at[PADDED : 2 * PADDED])
    inside = list(range(1, rows - 1))
    share = -(-len(inside) // PARTS)
    levels = w_mid.shape[0] + 1
    copies = []
    for n in range(PARTS):
        mine = inside[n * share : (n + 1) * share]
        copies += learn_lines(
            mine, inside if n == PARTS - 1 else [], len(mine), n * share,
            strain, learned, rows, cols, weights, hidden, stored, inputs,
            [flags.at[n * levels + k] for k in range(levels)],
        )
    for copy in copies:
        copy.wait()


def stiffness_of(table, ids, depth, target, at):
    layups = table.shape[0] // 36
    bits = [(ids & (1 << k)) != 0 for k in range(depth)]
    for n, (a, b) in enumerate(UPPER):
        layers = [table[min(l, layups - 1) * 36 + a * 6 + b] for l in range(1 << depth)]
        target[n, :, at] = jnp.broadcast_to(chosen(layers, bits), ids.shape)


def depth_of(table):
    depth = 1
    while (1 << depth) < table.shape[0] // 36:
        depth += 1
    return depth


def prepare_kernel(table, fields, fl_up, fl_down, stiff, support):
    rows, wide = fields.shape[1], fields.shape[2]
    halo = fl_up.shape[1]
    edge = jnp.zeros((rows - halo, LANES), jnp.float32)

    def fill(tile, carry):
        at = lanes_of(tile)
        around = [
            jnp.concatenate(
                [edge, fl_up[c, :, at], fields[3 + c, :, at], fl_down[c, :, at], edge], axis=0
            )
            for c in range(4)
        ]
        for c in range(3):
            support[c, :, at] = around[c]
        stiffness_of(table, around[3].astype(jnp.int32), depth_of(table), stiff, at)
        return carry

    lax.fori_loop(0, wide // LANES, fill, 0)


def outer_kernel(
    table, fields, up, down, inner, ends, w_mid,
    residual, own_residual, stored, inputs,
    centre, before, after, ahead, behind, middle, strain, learned, stiff, shifts, hidden, flags,
):
    rows, wide = fields.shape[1], fields.shape[2]
    tiles = wide // LANES
    cols = wide - LANES
    tall = 3 * rows
    lane = lax.broadcasted_iota(jnp.int32, (tall, LANES), 1)
    first, final = lane == 0, lane == LANES - 1
    rim = jnp.zeros((rows - MARGIN, LANES), jnp.float32)
    last = 3 * MARGIN

    def set_up(tile, carry):
        at = lanes_of(tile)
        for c in range(3):
            above, below = up[MARGIN * c : MARGIN * (c + 1), at], down[MARGIN * c : MARGIN * (c + 1), at]
            value = jnp.concatenate([rim, above, fields[c, :, at], below, rim], axis=0)
            centre[c, :, at] = value
        wall = jnp.zeros((rows - 1, LANES), jnp.float32)
        ids = jnp.concatenate(
            [wall, up[last : last + 1, at], fields[6, :, at], down[last : last + 1, at], wall],
            axis=0,
        ).astype(jnp.int32)
        stiffness_of(table, ids, depth_of(table), stiff, at)
        return carry

    fill_shifts(shifts)
    lax.fori_loop(0, tiles, set_up, 0)
    shift_both(centre, before, after, shifts)

    def strains(tile, carry):
        at = lanes_of(tile)
        e = spread_strains(*triples_of(centre, before, after, tile, tiles, first, final))
        for n in range(FIELDS):
            value = HALVING[n] * e[n] if n < 6 else jnp.zeros((tall, LANES), jnp.float32)
            strain[tile, n * tall : (n + 1) * tall] = value
        for n in range(6):
            learned[tile, n * tall + rows + 1 : n * tall + 2 * rows - 1] = inner[
                tile, n * rows + 1 : (n + 1) * rows - 1
            ]
        return carry

    lax.fori_loop(0, tiles, strains, 0)
    weights = (ends.at[0:PADDED], w_mid, ends.at[PADDED : 2 * PADDED])
    lines = (rows, 2 * rows - 1, rows - 1, 2 * rows)
    copies = learn_lines(
        lines, lines, 2, 0, strain, learned, tall, cols, weights, hidden, stored, inputs,
        [flags.at[k] for k in range(w_mid.shape[0] + 1)],
    )

    def push(tile, carry):
        at = lanes_of(tile)
        e = [strain[tile, n * tall : (n + 1) * tall] * (1.0 / HALVING[n]) for n in range(6)]
        s = mixed([stiff[n, :, at] for n in range(len(UPPER))], e)
        s = [s[n] + HALVING[n] * learned[tile, n * tall : (n + 1) * tall] for n in range(6)]
        for c, (alpha, beta, gamma) in enumerate(spread_forces(s)):
            ahead[c, :, at] = alpha
            behind[c, :, at] = beta
            middle[c, :, at] = gamma
        return carry

    lax.fori_loop(0, tiles, push, 0)
    shift_in_place(ahead, 0, shifts)
    shift_in_place(behind, 1, shifts)
    own = slice(rows, 2 * rows)

    def finish(tile, carry):
        at = lanes_of(tile)
        left, right = beside(tile, tiles)
        at_left, at_right = lanes_of(left), lanes_of(right)
        for c in range(3):
            value = (
                middle[c, own, at]
                + jnp.where(first[:rows], ahead[c, own, at_left], ahead[c, own, at])
                + jnp.where(final[:rows], behind[c, own, at_right], behind[c, own, at])
            )
            value = value + fields[3 + c, :, at] * fields[c, :, at] - fields[7 + c, :, at]
            residual[c, :, at] = value
            if carry is not None:
                own_residual[c, :, at] = value
        return carry

    lax.fori_loop(0, tiles - 1, finish, 0)
    finish(tiles - 1, None)
    for copy in copies:
        copy.wait()


def solve(numbers, sums, kept, bends, adjoint, upstream):
    rows = adjoint.shape[1]
    own_tiles = upstream.shape[0]
    line = jnp.sum(sums[...], axis=0)
    picks = [jnp.broadcast_to(line[:, n : n + 1], (1, LANES)) for n in range(SUMS)]
    centre = [numbers[k] for k in range(3)]
    width = [numbers[3 + k] for k in range(3)]
    matrix = [[None] * 4 for _ in range(4)]
    for k in range(3):
        for j in range(k + 1):
            matrix[j][k] = picks[4 + k * (k + 1) // 2 + j]
    cross = [picks[3], picks[10], picks[11], picks[12]]
    for j in range(3):
        value = width[j] * cross[j + 1] + centre[j] * cross[j]
        matrix[j][3] = value + width[j - 1] * cross[j - 1] if j else value
    matrix[3][3] = picks[13]
    weights = [jnp.broadcast_to(x, (rows, LANES)) for x in galerkin(matrix, picks[:4])]

    def weighted(parts):
        total = weights[0] * parts[0]
        for weight, part in zip(weights[1:], parts[1:]):
            total = total + weight * part
        return total

    levels = range(DEGREE + 1)

    def combine(tile, carry):
        at = lanes_of(tile)
        for c in range(3):
            adjoint[c, :, at] = weighted([kept[k, c, :, at] for k in levels])
        for n in range(6):
            here = slice(n * rows, (n + 1) * rows)
            upstream[tile, here] = HALVING[n] * weighted([bends[k, tile, here] for k in levels])
        upstream[tile, 6 * rows :] = jnp.zeros(((FIELDS - 6) * rows, LANES), jnp.float32)
        return carry

    lax.fori_loop(0, own_tiles, combine, 0)


def slope_of(signal, h):
    h = h.astype(jnp.float32)
    return (signal * (1.0 - h * h)).astype(jnp.bfloat16)


def backward_kernel(
    numbers, sums, kept, bends, inner_hidden, inner_inputs, outer_hidden, outer_inputs, w_mid,
    ends, adjoint, packed,
    upstream, grads, near_hidden, far_hidden, near_flags, far_flags,
):
    layers = w_mid.shape[0]
    hid = w_mid.shape[1]
    cols = upstream.shape[0] * LANES
    rows = upstream.shape[1] // FIELDS
    last_at = layers * hid
    first_at = last_at + FIELDS
    for n in range(rows - 2):
        line_copy(n, cols, inner_hidden, near_hidden, near_flags).start()
    for n in range(2):
        line_copy(n, cols, outer_hidden, far_hidden, far_flags).start()
    grads[...] = jnp.zeros_like(grads)
    solve(numbers, sums, kept, bends, adjoint, upstream)

    def line(row, at_line, hidden, inputs):
        for at, size in pieces_of(cols):
            where = at_line * cols + at
            if not isinstance(where, int):
                where = pl.multiple_of(where, LANES)
            here = pl.ds(where, size)
            signal = widened(gathered(upstream, row, rows, at, size))
            h = hidden[layers, here, :]
            grads[last_at : last_at + FIELDS] += contract(signal, h, 1, 0)[:FIELDS]
            d = slope_of(contract(signal, ends[PADDED : 2 * PADDED], 0, 0), h)
            for k in range(layers - 1, -1, -1):
                h = hidden[k, here, :]
                grads[k * hid : (k + 1) * hid] += contract(d, h, 0, 0)
                d = slope_of(contract(d, w_mid[k], 1, 0), h)
            grads[first_at : first_at + FIELDS] += contract(inputs[:, here], d, 1, 0)[:FIELDS]

    def inside(row, carry):
        line_copy(row - 1, cols, inner_hidden, near_hidden, near_flags).wait()
        line(row, row - 1, near_hidden, inner_inputs)
        return carry

    lax.fori_loop(1, rows - 1, inside, 0)
    for n, row in enumerate((0, rows - 1)):
        line_copy(n, cols, outer_hidden, far_hidden, far_flags).wait()
        line(row, n, far_hidden, outer_inputs)
    chunk = packed.shape[1]
    for n in range(packed.shape[0]):
        for r in range(chunk):
            packed[n, r] = grads[n * chunk + r : n * chunk + r + 1]


def gather_kernel(parts, total):
    total[...] = jnp.broadcast_to(jnp.sum(parts[...], axis=0, keepdims=True), total.shape)


def deliver_kernel(parts, grad_first, grad_mid, grad_last, flat):
    chunk = parts.shape[1]
    for n in range(parts.shape[0]):
        for r in range(chunk):
            flat[n * chunk + r : n * chunk + r + 1] = parts[n, r]
    layers, hid = grad_mid.shape[0], grad_mid.shape[1]
    for k in range(layers):
        grad_mid[k] = flat[k * hid : (k + 1) * hid]
    at = layers * hid
    grad_last[...] = flat[at : at + FIELDS][: grad_last.shape[0]]
    grad_first[...] = flat[at + FIELDS : at + 2 * FIELDS][: grad_first.shape[0]]


def fill_shifts(shifts):
    shape = (PIECES * LANES, LANES)
    source = lax.broadcasted_iota(jnp.int32, shape, 0) % LANES
    target = lax.broadcasted_iota(jnp.int32, shape, 1)
    for n, step in enumerate((1, LANES - 1)):
        hit = (source + step) % LANES == target
        shifts[:, n * LANES : (n + 1) * LANES] = jnp.where(hit, 1.0, 0.0).astype(jnp.bfloat16)


def pieces(x):
    parts = []
    for n in range(PIECES):
        part = x.astype(jnp.bfloat16)
        parts.append(part)
        if n + 1 < PIECES:
            x = x - part.astype(jnp.float32)
    return jnp.concatenate(parts, axis=1)


def groups_of(array):
    tiles = array.shape[2] // LANES
    return [range(t, min(t + GROUP, tiles)) for t in range(0, tiles, GROUP)]


def stacked(source, group):
    return pieces(
        jnp.concatenate([source[c, :, lanes_of(t)] for t in group for c in range(3)], axis=0)
    )


def shift_both(source, before, after, shifts):
    tall = source.shape[1]
    for group in groups_of(source):
        moved = contract(stacked(source, group), shifts[...], 1, 0)
        for n, tile in enumerate(group):
            for c in range(3):
                at = (3 * n + c) * tall
                before[c, :, lanes_of(tile)] = moved[at : at + tall, :LANES]
                after[c, :, lanes_of(tile)] = moved[at : at + tall, LANES:]


def shift_in_place(array, side, shifts):
    tall = array.shape[1]
    for group in groups_of(array):
        moved = contract(stacked(array, group), shifts[:, side * LANES : (side + 1) * LANES], 1, 0)
        for n, tile in enumerate(group):
            for c in range(3):
                at = (3 * n + c) * tall
                array[c, :, lanes_of(tile)] = moved[at : at + tall]


def krylov_kernel(
    numbers, r_mid, r_up, r_down, stiff, support, kept, bends, sums,
    basis, before, after, ahead, behind, middle, shifts,
):
    rows = r_mid.shape[1]
    wide = r_mid.shape[2]
    tiles = wide // LANES
    own_tiles = tiles - 1
    tall = 3 * rows
    lane = lax.broadcasted_iota(jnp.int32, (tall, LANES), 1)
    first, final = lane == 0, lane == LANES - 1

    def place(k, c, at, value):
        basis[k, c, :, at] = value
        kept[k, c, :, at] = value[rows : 2 * rows]

    def set_up(tile, carry):
        at = lanes_of(tile)
        for c in range(3):
            value = jnp.concatenate([r_up[c, :, at], r_mid[c, :, at], r_down[c, :, at]], axis=0)
            place(0, c, at, value)
        return carry

    fill_shifts(shifts)
    lax.fori_loop(0, tiles, set_up, 0)
    shift_both(basis.at[0], before, after, shifts)

    def strain_of(k, tile):
        e = spread_strains(*triples_of(basis.at[k], before, after, tile, tiles, first, final))
        for n in range(6):
            bends[k, tile, n * rows : (n + 1) * rows] = e[n][rows : 2 * rows]
        return e

    def stress_of(e, at):
        return mixed([stiff[n, :, at] for n in range(len(UPPER))], e)

    def mine(value):
        return value[rows : 2 * rows]

    zero = jnp.zeros((rows, LANES), jnp.float32)
    totals = [None] * SUMS

    for k in range(DEGREE):
        def push(tile, carry, k=k):
            at = lanes_of(tile)
            for c, (alpha, beta, gamma) in enumerate(
                spread_forces(stress_of(strain_of(k, tile), at))
            ):
                ahead[c, :, at] = alpha
                behind[c, :, at] = beta
                middle[c, :, at] = gamma
            return carry

        lax.fori_loop(0, tiles, push, 0)
        shift_in_place(ahead, 0, shifts)
        shift_in_place(behind, 1, shifts)

        centre, inverse = numbers[k], numbers[6 + k]
        former = numbers[2 + k]

        def advance(tile, carry, k=k):
            at = lanes_of(tile)
            left, right = beside(tile, tiles)
            at_left, at_right = lanes_of(left), lanes_of(right)
            image, here, following = [], [], []
            for c in range(3):
                vector = basis[k, c, :, at]
                value = (
                    middle[c, :, at]
                    + jnp.where(first, ahead[c, :, at_left], ahead[c, :, at])
                    + jnp.where(final, behind[c, :, at_right], behind[c, :, at])
                    + support[c, :, at] * vector
                )
                step = value - centre * vector
                if k:
                    step = step - former * basis[k - 1, c, :, at]
                step = step * inverse
                place(k + 1, c, at, step)
                image.append(mine(value))
                here.append(mine(vector))
                following.append(mine(step))
            if carry is None:
                return None

            def dot(left_side, right_side):
                return (
                    left_side[0] * right_side[0]
                    + left_side[1] * right_side[1]
                    + left_side[2] * right_side[2]
                )

            def old(m):
                return [basis[m, c, rows : 2 * rows, at] for c in range(3)]

            fresh = []
            origin = here if k == 0 else old(0)
            if k == 0:
                fresh.append(dot(here, here))
            fresh.append(dot(origin, following))
            for j in range(k + 1):
                fresh.append(dot(here if j == k else (origin if j == 0 else old(j)), image))
            if k == DEGREE - 1:
                fresh.append(dot(old(1), following))
                fresh.append(dot(here, following))
                fresh.append(dot(following, following))
            return tuple(p + q for p, q in zip(carry, fresh))

        names = ([0] if k == 0 else []) + [k + 1] + [4 + k * (k + 1) // 2 + j for j in range(k + 1)]
        if k == DEGREE - 1:
            names += [10, 11, 12]
        found = lax.fori_loop(0, own_tiles, advance, (zero,) * len(names))
        advance(own_tiles, None)
        shift_both(basis.at[k + 1], before, after, shifts)
        for name, value in zip(names, found):
            totals[name] = value

    def energy(tile, running):
        at = lanes_of(tile)
        e = strain_of(DEGREE, tile)
        e = [mine(value) for value in e]
        for n, (a, b) in enumerate(UPPER):
            term = stiff[n, rows : 2 * rows, at] * e[b] * e[a]
            running = running + (term if a == b else 2.0 * term)
        for c in range(3):
            vector = basis[DEGREE, c, rows : 2 * rows, at]
            running = running + support[c, rows : 2 * rows, at] * vector * vector
        return running

    totals[13] = lax.fori_loop(0, own_tiles, energy, zero)
    place_of = lax.broadcasted_iota(jnp.int32, (1, LANES), 1)
    line = jnp.zeros((1, LANES), jnp.float32)
    for n in range(SUMS):
        total = jnp.sum(jnp.sum(totals[n], axis=0, keepdims=True), axis=1, keepdims=True)
        line = jnp.where(place_of == n, jnp.broadcast_to(total, (1, LANES)), line)
    sums[...] = jnp.broadcast_to(line[None], sums.shape)


def basis_constants(layup_stiffness):
    bending = 0.5 * (jnp.mean(layup_stiffness[:, 3, 3]) + jnp.mean(layup_stiffness[:, 4, 4]))
    centres = [11.5 * bending + 1.1, 9.8 * bending + 1.1, 8.4 * bending + 1.1]
    widths = [3.9 * bending + 0.4, 5.6 * bending + 0.4, 4.8 * bending + 0.4]
    return centres, widths


ON_CHIP = pl.BlockSpec(memory_space=pltpu.VMEM)
SCALARS = pl.BlockSpec(memory_space=pltpu.SMEM)


IN_PLACE = pl.BlockSpec(memory_space=pltpu.HBM)


def kernel_call(body, name, scalars, outs, scratch, *operands, far=(), far_outs=()):
    specs = [SCALARS] * scalars + [ON_CHIP] * (len(operands) - scalars)
    for n in far:
        specs[n] = IN_PLACE
    return pl.pallas_call(
        body,
        in_specs=specs,
        out_specs=[IN_PLACE if n in far_outs else ON_CHIP for n in range(len(outs))],
        out_shape=[
            pltpu.HBM(*out) if n in far_outs else jax.ShapeDtypeStruct(*out)
            for n, out in enumerate(outs)
        ],
        scratch_shapes=[
            pltpu.VMEM(*s) if isinstance(s, tuple) else pltpu.SemaphoreType.DMA((s,))
            for s in scratch
        ],
        compiler_params=pltpu.CompilerParams(vmem_limit_bytes=LIMITS[name] << 20),
    )(*[
        pltpu.with_memory_space_constraint(x, pltpu.HBM) if n in far else x
        for n, x in enumerate(operands)
    ])


LIMITS = {
    "assemble": 4,
    "inner": 40, "outer": 40, "prepare": 8, "krylov": 10, "backward": 32, "gather": 4, "deliver": 4,
}


def per_device(displacement, load, foundation, layup, layup_stiffness, w_first, w_mid, w_last):
    f32, bf16 = jnp.float32, jnp.bfloat16
    rows, cols = layup.shape
    layers, hid = w_mid.shape[0], w_mid.shape[1]
    devices = lax.axis_size("patch") * lax.axis_size("sub")
    wide = cols + LANES
    tall = 3 * rows
    tiles = wide // LANES
    (fields,) = kernel_call(
        assemble_kernel, "assemble", 0,
        [((10, rows, cols), f32)], [((rows, cols), jnp.int32), 4],
        displacement, foundation, layup, load, far=(0, 1, 2, 3),
    )
    before, after = from_both(fields, "sub", 2, HY)
    gap = jnp.zeros(fields.shape[:2] + (LANES - 2 * HY,), f32)
    fields = jnp.concatenate([fields, after, gap, before], axis=2)
    sends = [
        jnp.concatenate([*[fields[c, edge] for c in range(3)], fields[6, edge][near]])
        for edge, near in ((slice(rows - MARGIN, rows), slice(1, 2)), (slice(0, MARGIN), slice(0, 1)))
    ]
    up = lax.ppermute(sends[0], "patch", ring("patch", 1))
    down = lax.ppermute(sends[1], "patch", ring("patch", -1))
    fl_up, fl_down = from_both(fields[3:7], "patch", 1, 6)

    halving = jnp.array(HALVING, f32)
    table = (layup_stiffness * halving[:, None] * halving[None, :]).reshape(-1)
    centres, widths = basis_constants(layup_stiffness)
    numbers = jnp.stack(centres + widths + [1.0 / x for x in widths])
    thin = w_first.shape[1]
    blank = jnp.zeros((PADDED - thin, hid), bf16)
    ends = jnp.concatenate([w_first.T, blank, w_last, blank])

    learned, inner_hidden, inner_inputs = kernel_call(
        inner_kernel, "inner", 0,
        [((tiles, FIELDS * rows, LANES), f32), ((layers + 1, (rows - 2) * cols, hid), bf16),
         ((PADDED, (rows - 2) * cols), bf16)],
        [((3, rows, wide), f32)] * 2
        + [((tiles, FIELDS * rows, LANES), f32), ((layers + 1, (rows - 2) * cols, hid), bf16),
           PARTS * (layers + 1)],
        fields, ends, w_mid, far_outs=(1,),
    )
    wide_residual, residual, outer_hidden, outer_inputs = kernel_call(
        outer_kernel, "outer", 1,
        [((3, rows, wide), f32), ((3, rows, cols), f32),
         ((layers + 1, 2 * cols, hid), bf16), ((PADDED, 2 * cols), bf16)],
        [((3, tall, wide), f32)] * 6
        + [((tiles, FIELDS * tall, LANES), f32)] * 2
        + [((len(UPPER), tall, wide), f32), ((PIECES * LANES, 2 * LANES), bf16),
           ((layers + 1, 2 * cols, hid), bf16), layers + 1],
        table, fields, up, down, learned, ends, w_mid, far_outs=(2,),
    )
    stiff, support = kernel_call(
        prepare_kernel, "prepare", 1,
        [((len(UPPER), tall, wide), f32), ((3, tall, wide), f32)], [],
        table, fields, fl_up, fl_down,
    )
    up, down = from_both(wide_residual, "patch", 1, rows)
    kept, bends, sums = kernel_call(
        krylov_kernel, "krylov", 1,
        [((DEGREE + 1, 3, rows, wide), f32), ((DEGREE + 1, tiles, 6 * rows, LANES), f32),
         ((devices, 1, LANES), f32)],
        [((DEGREE + 1, 3, tall, wide), f32)] + [((3, tall, wide), f32)] * 5
        + [((PIECES * LANES, 2 * LANES), bf16)],
        numbers, wide_residual, up, down, stiff, support,
    )
    sums = everyone(sums)
    count = layers * hid + 2 * FIELDS
    chunk = -(-count // devices)
    adjoint, packed = kernel_call(
        backward_kernel, "backward", 1,
        [((3, rows, cols), f32), ((devices, chunk, 1, LANES), f32)],
        [((tiles - 1, FIELDS * rows, LANES), f32),
         ((devices * chunk, LANES), f32), ((layers + 1, (rows - 2) * cols, hid), bf16),
         ((layers + 1, 2 * cols, hid), bf16), rows - 2, 2],
        numbers, sums, kept, bends, inner_hidden, inner_inputs, outer_hidden, outer_inputs,
        w_mid, ends, far=(4, 6),
    )
    (total,) = kernel_call(
        gather_kernel, "gather", 0, [(packed.shape, f32)], [], everyone(packed)
    )
    grad_first, grad_mid, grad_last = kernel_call(
        deliver_kernel, "deliver", 0,
        [((thin, hid), f32), (w_mid.shape, f32), (w_last.shape, f32)],
        [((devices * chunk, LANES), f32)],
        everyone(total),
    )
    return residual, adjoint, grad_first.T, grad_mid, grad_last


def solution(mesh):
    field = P(None, "patch", "sub")
    return jax.shard_map(
        per_device,
        mesh=mesh,
        in_specs=(field, field, field, P("patch", "sub"), P(), P(), P(), P()),
        out_specs=(field, field, P(), P(), P()),
        check_vma=False,
    )
```

```python
import jax
import jax.numpy as jnp
from jax import lax
from jax.experimental import pallas as pl
from jax.experimental.pallas import tpu as pltpu
from jax.sharding import PartitionSpec as P


HY = 16
LANES = 128
AXES = ("patch", "sub")


def ring(axis, step):
    count = lax.axis_size(axis)
    return [(i, (i + step) % count) for i in range(count)]


def from_both(array, axis, dim, width):
    size = array.shape[dim]
    tail = lax.slice_in_dim(array, size - width, size, axis=dim)
    head = lax.slice_in_dim(array, 0, width, axis=dim)
    before = lax.ppermute(tail, axis, ring(axis, 1))
    after = lax.ppermute(head, axis, ring(axis, -1))
    return before, after


def everyone(rows):
    return lax.all_to_all(rows, AXES, 0, 0, tiled=True)


def galerkin(matrix, target):
    size = len(target)
    matrix = [list(row) for row in matrix]
    target = list(target)
    scale = [matrix[i][i] for i in range(size)]
    inverse = []
    for i in range(size):
        pivot = matrix[i][i]
        usable = pivot > 1e-6 * scale[i]
        inverse.append(jnp.where(usable, 1.0 / jnp.where(usable, pivot, 1.0), 0.0))
        for j in range(i + 1, size):
            factor = matrix[i][j] * inverse[i]
            for k in range(j, size):
                matrix[j][k] = matrix[j][k] - factor * matrix[i][k]
            target[j] = target[j] - factor * target[i]
    answer = [None] * size
    for i in reversed(range(size)):
        running = target[i]
        for j in range(i + 1, size):
            running = running - matrix[i][j] * answer[j]
        answer[i] = running * inverse[i]
    return answer


DEGREE = 3
UPPER = [(a, b) for a in range(6) for b in range(a, 6)]
HALVING = (0.0625, 0.0625, 0.0625, -0.125, -0.125, -0.5)
SUMS = 14


def lanes_of(tile):
    if isinstance(tile, int):
        return pl.ds(tile * LANES, LANES)
    return pl.ds(pl.multiple_of(tile * LANES, LANES), LANES)


def beside(tile, tiles):
    if isinstance(tile, int):
        return (tile - 1) % tiles, (tile + 1) % tiles
    return jnp.where(tile == 0, tiles - 1, tile - 1), jnp.where(tile == tiles - 1, 0, tile + 1)


def x_pair(f):
    return pltpu.roll(f, 1, 0), pltpu.roll(f, f.shape[0] - 1, 0)


def spread_strains(u, v, w):
    value_u, slope_u = u[0] + u[1] + 6.0 * u[2], u[1] - u[0]
    value_v, slope_v = v[0] + v[1] + 6.0 * v[2], v[1] - v[0]
    both_w = w[0] + w[1]
    value_w, slope_w, curve_w = both_w + 6.0 * w[2], w[1] - w[0], both_w - 2.0 * w[2]
    b, a = x_pair(value_u)
    e0 = a - b
    hoop = slope_v + 0.0625 * value_w
    b, a = x_pair(hoop)
    e1 = b + a + 6.0 * hoop
    b = pltpu.roll(slope_u - value_v, 1, 0)
    a = pltpu.roll(slope_u + value_v, slope_u.shape[0] - 1, 0)
    e2 = b + a + 6.0 * slope_u
    b, a = x_pair(value_w)
    e3 = b + a - 2.0 * value_w
    b, a = x_pair(curve_w)
    e4 = b + a + 6.0 * curve_w
    b, a = x_pair(slope_w)
    e5 = a - b
    return e0, e1, e2, e3, e4, e5


def spread_forces(s):
    b, a = x_pair(s[0])
    lean_u = b - a
    b, a = x_pair(s[2])
    lean_v = b - a
    turn_u = b + a + 6.0 * s[2]
    b, a = x_pair(s[1])
    turn_v = b + a + 6.0 * s[1]
    b, a = x_pair(s[3])
    lean_w = 0.0625 * turn_v + (b + a - 2.0 * s[3])
    b, a = x_pair(s[4])
    bent_w = b + a + 6.0 * s[4]
    b, a = x_pair(s[5])
    turn_w = a - b
    sum_w = lean_w + bent_w
    return (
        (lean_u + turn_u, lean_u - turn_u, 6.0 * lean_u),
        (lean_v + turn_v, lean_v - turn_v, 6.0 * lean_v),
        (sum_w - turn_w, sum_w + turn_w, 6.0 * lean_w - 2.0 * bent_w),
    )


def chosen(layers, bits):
    if len(layers) == 1:
        return layers[0]
    half = len(layers) // 2
    return jnp.where(bits[-1], chosen(layers[half:], bits[:-1]), chosen(layers[:half], bits[:-1]))


MARGIN = 2
FIELDS = 8
PADDED = 16
PIECES = 3
GROUP = 9
PARTS = 3


def triples_of(centre, before, after, tile, tiles, first, final):
    at = lanes_of(tile)
    left, right = beside(tile, tiles)
    at_left, at_right = lanes_of(left), lanes_of(right)
    return [
        (
            jnp.where(first, before[c, :, at_left], before[c, :, at]),
            jnp.where(final, after[c, :, at_right], after[c, :, at]),
            centre[c, :, at],
        )
        for c in range(3)
    ]


def mixed(values, e):
    s = [None] * 6
    for n, (a, b) in enumerate(UPPER):
        for p, q in ((a, b), (b, a))[: 1 if a == b else 2]:
            term = values[n] * e[q]
            s[p] = term if s[p] is None else s[p] + term
    return s


def contract(left, right, left_dim, right_dim):
    return lax.dot_general(
        left, right, (((left_dim,), (right_dim,)), ((), ())), preferred_element_type=jnp.float32
    )


def widened(x):
    return jnp.concatenate([x, jnp.zeros_like(x)], axis=0).astype(jnp.bfloat16)


def learn(x, w_first, w_mid, w_last, keep=None):
    h = jnp.tanh(contract(x, w_first[...], 0, 0)).astype(jnp.bfloat16)
    if keep is not None:
        keep(0, h)
    for k in range(w_mid.shape[0]):
        h = jnp.tanh(contract(h, w_mid[k], 1, 1)).astype(jnp.bfloat16)
        if keep is not None:
            keep(k + 1, h)
    return contract(w_last[...], h, 1, 1)[:FIELDS]


def pieces_of(cols):
    step = cols
    while step > 2048 and step % 256 == 0:
        step //= 2
    return [(at, step) for at in range(0, cols, step)]


def gathered(array, row, spread, at, size):
    tiles = range(at // LANES, (at + size) // LANES)
    return jnp.concatenate(
        [array[t, pl.ds(row, FIELDS, stride=spread), :] for t in tiles], axis=1
    )


def layer_copy(k, base, span, source, target, flag):
    here = pl.ds(base, span)
    return pltpu.make_async_copy(source.at[k, here, :], target.at[k, here, :], flag)


def learn_lines(
    rows, rims, kept, base, strain, learned, spread, cols, weights, hidden, stored, inputs, flags
):
    rim = cols // LANES
    parts = [gathered(strain, row, spread, 0, cols) for row in rows]
    parts += [strain[rim, pl.ds(row, FIELDS, stride=spread), :] for row in rims]
    x = widened(jnp.concatenate(parts, axis=1))
    start, span = base * cols, kept * cols
    copies = []
    if kept:
        inputs[:, pl.ds(start, span)] = x[:, :span]

    def keep(k, h):
        hidden[k, pl.ds(start, span), :] = h[:span]
        copies.append(layer_copy(k, start, span, hidden, stored, flags[k]))
        copies[-1].start()

    out = learn(x, *weights, keep if kept else None)
    for n, row in enumerate(rows):
        for t in range(rim):
            at = n * cols + t * LANES
            learned[t, pl.ds(row, FIELDS, stride=spread), :] = out[:, at : at + LANES]
    for n, row in enumerate(rims):
        at = len(rows) * cols + n * LANES
        learned[rim, pl.ds(row, FIELDS, stride=spread), :] = out[:, at : at + LANES]
    return copies


def line_copy(line, cols, source, target, flags):
    where = line * cols
    if not isinstance(where, int):
        where = pl.multiple_of(where, LANES)
    here = pl.ds(where, cols)
    return pltpu.make_async_copy(source.at[:, here, :], target.at[:, here, :], flags.at[line])


def assemble_kernel(displacement, foundation, layup, load, fields, ids, flags):
    moves = ((layup, ids), (displacement, fields.at[0:3]), (foundation, fields.at[3:6]),
             (load, fields.at[7:10]))
    copies = [pltpu.make_async_copy(a, b, flags.at[n]) for n, (a, b) in enumerate(moves)]
    for copy in copies:
        copy.start()
    copies[0].wait()
    fields[6] = ids[...].astype(jnp.float32)
    for copy in copies[1:]:
        copy.wait()


def inner_kernel(
    fields, ends, w_mid, learned, stored, inputs, before, after, strain, hidden, flags
):
    rows, wide = fields.shape[1], fields.shape[2]
    tiles = wide // LANES
    cols = wide - LANES
    lane = lax.broadcasted_iota(jnp.int32, (rows, LANES), 1)
    first, final = lane == 0, lane == LANES - 1

    def set_up(tile, carry):
        at = lanes_of(tile)
        for c in range(3):
            value = fields[c, :, at]
            before[c, :, at] = pltpu.roll(value, 1, 1)
            after[c, :, at] = pltpu.roll(value, LANES - 1, 1)
        return carry

    lax.fori_loop(0, tiles, set_up, 0)

    def strains(tile, carry):
        at = lanes_of(tile)
        e = spread_strains(*triples_of(fields.at[0:3], before, after, tile, tiles, first, final))
        for n in range(FIELDS):
            value = HALVING[n] * e[n] if n < 6 else jnp.zeros((rows, LANES), jnp.float32)
            strain[tile, n * rows : (n + 1) * rows] = value
        return carry

    lax.fori_loop(0, tiles, strains, 0)
    weights = (ends.at[0:PADDED], w_mid, ends.at[PADDED : 2 * PADDED])
    inside = list(range(1, rows - 1))
    share = -(-len(inside) // PARTS)
    levels = w_mid.shape[0] + 1
    copies = []
    for n in range(PARTS):
        mine = inside[n * share : (n + 1) * share]
        copies += learn_lines(
            mine, inside if n == PARTS - 1 else [], len(mine), n * share,
            strain, learned, rows, cols, weights, hidden, stored, inputs,
            [flags.at[n * levels + k] for k in range(levels)],
        )
    for copy in copies:
        copy.wait()


def stiffness_of(table, ids, depth, target, at):
    layups = table.shape[0] // 36
    bits = [(ids & (1 << k)) != 0 for k in range(depth)]
    for n, (a, b) in enumerate(UPPER):
        layers = [table[min(l, layups - 1) * 36 + a * 6 + b] for l in range(1 << depth)]
        target[n, :, at] = jnp.broadcast_to(chosen(layers, bits), ids.shape)


def depth_of(table):
    depth = 1
    while (1 << depth) < table.shape[0] // 36:
        depth += 1
    return depth


def prepare_kernel(table, fields, fl_up, fl_down, stiff, support):
    rows, wide = fields.shape[1], fields.shape[2]
    halo = fl_up.shape[1]
    edge = jnp.zeros((rows - halo, LANES), jnp.float32)

    def fill(tile, carry):
        at = lanes_of(tile)
        around = [
            jnp.concatenate(
                [edge, fl_up[c, :, at], fields[3 + c, :, at], fl_down[c, :, at], edge], axis=0
            )
            for c in range(4)
        ]
        for c in range(3):
            support[c, :, at] = around[c]
        stiffness_of(table, around[3].astype(jnp.int32), depth_of(table), stiff, at)
        return carry

    lax.fori_loop(0, wide // LANES, fill, 0)


def outer_kernel(
    table, fields, up, down, inner, ends, w_mid,
    residual, own_residual, stored, inputs,
    centre, before, after, ahead, behind, middle, strain, learned, stiff, shifts, hidden, flags,
):
    rows, wide = fields.shape[1], fields.shape[2]
    tiles = wide // LANES
    cols = wide - LANES
    tall = 3 * rows
    lane = lax.broadcasted_iota(jnp.int32, (tall, LANES), 1)
    first, final = lane == 0, lane == LANES - 1
    rim = jnp.zeros((rows - MARGIN, LANES), jnp.float32)
    last = 3 * MARGIN

    def set_up(tile, carry):
        at = lanes_of(tile)
        for c in range(3):
            above, below = up[MARGIN * c : MARGIN * (c + 1), at], down[MARGIN * c : MARGIN * (c + 1), at]
            value = jnp.concatenate([rim, above, fields[c, :, at], below, rim], axis=0)
            centre[c, :, at] = value
        wall = jnp.zeros((rows - 1, LANES), jnp.float32)
        ids = jnp.concatenate(
            [wall, up[last : last + 1, at], fields[6, :, at], down[last : last + 1, at], wall],
            axis=0,
        ).astype(jnp.int32)
        stiffness_of(table, ids, depth_of(table), stiff, at)
        return carry

    fill_shifts(shifts)
    lax.fori_loop(0, tiles, set_up, 0)
    shift_both(centre, before, after, shifts)

    def strains(tile, carry):
        at = lanes_of(tile)
        e = spread_strains(*triples_of(centre, before, after, tile, tiles, first, final))
        for n in range(FIELDS):
            value = HALVING[n] * e[n] if n < 6 else jnp.zeros((tall, LANES), jnp.float32)
            strain[tile, n * tall : (n + 1) * tall] = value
        for n in range(6):
            learned[tile, n * tall + rows + 1 : n * tall + 2 * rows - 1] = inner[
                tile, n * rows + 1 : (n + 1) * rows - 1
            ]
        return carry

    lax.fori_loop(0, tiles, strains, 0)
    weights = (ends.at[0:PADDED], w_mid, ends.at[PADDED : 2 * PADDED])
    own_lines, far_lines = (rows, 2 * rows - 1), (rows - 1, 2 * rows)
    copies = learn_lines(
        own_lines, (), 2, 0, strain, learned, tall, cols, weights, hidden, stored, inputs,
        [flags.at[k] for k in range(w_mid.shape[0] + 1)],
    )
    learn_lines(
        far_lines, own_lines + far_lines, 0, 0, strain, learned, tall, cols, weights, hidden,
        stored, inputs, (),
    )

    def push(tile, carry):
        at = lanes_of(tile)
        e = [strain[tile, n * tall : (n + 1) * tall] * (1.0 / HALVING[n]) for n in range(6)]
        s = mixed([stiff[n, :, at] for n in range(len(UPPER))], e)
        s = [s[n] + HALVING[n] * learned[tile, n * tall : (n + 1) * tall] for n in range(6)]
        for c, (alpha, beta, gamma) in enumerate(spread_forces(s)):
            ahead[c, :, at] = alpha
            behind[c, :, at] = beta
            middle[c, :, at] = gamma
        return carry

    lax.fori_loop(0, tiles, push, 0)
    shift_in_place(ahead, 0, shifts)
    shift_in_place(behind, 1, shifts)
    own = slice(rows, 2 * rows)

    def finish(tile, carry):
        at = lanes_of(tile)
        left, right = beside(tile, tiles)
        at_left, at_right = lanes_of(left), lanes_of(right)
        for c in range(3):
            value = (
                middle[c, own, at]
                + jnp.where(first[:rows], ahead[c, own, at_left], ahead[c, own, at])
                + jnp.where(final[:rows], behind[c, own, at_right], behind[c, own, at])
            )
            value = value + fields[3 + c, :, at] * fields[c, :, at] - fields[7 + c, :, at]
            residual[c, :, at] = value
            if carry is not None:
                own_residual[c, :, at] = value
        return carry

    lax.fori_loop(0, tiles - 1, finish, 0)
    finish(tiles - 1, None)
    for copy in copies:
        copy.wait()


def solve(numbers, sums, kept, bends, adjoint, upstream):
    rows = adjoint.shape[1]
    own_tiles = upstream.shape[0]
    line = jnp.sum(sums[...], axis=0)
    picks = [jnp.broadcast_to(line[:, n : n + 1], (1, LANES)) for n in range(SUMS)]
    centre = [numbers[k] for k in range(3)]
    width = [numbers[3 + k] for k in range(3)]
    matrix = [[None] * 4 for _ in range(4)]
    for k in range(3):
        for j in range(k + 1):
            matrix[j][k] = picks[4 + k * (k + 1) // 2 + j]
    cross = [picks[3], picks[10], picks[11], picks[12]]
    for j in range(3):
        value = width[j] * cross[j + 1] + centre[j] * cross[j]
        matrix[j][3] = value + width[j - 1] * cross[j - 1] if j else value
    matrix[3][3] = picks[13]
    weights = [jnp.broadcast_to(x, (rows, LANES)) for x in galerkin(matrix, picks[:4])]

    def weighted(parts):
        total = weights[0] * parts[0]
        for weight, part in zip(weights[1:], parts[1:]):
            total = total + weight * part
        return total

    levels = range(DEGREE + 1)

    def combine(tile, carry):
        at = lanes_of(tile)
        for c in range(3):
            adjoint[c, :, at] = weighted([kept[k, c, :, at] for k in levels])
        for n in range(6):
            here = slice(n * rows, (n + 1) * rows)
            upstream[tile, here] = HALVING[n] * weighted([bends[k, tile, here] for k in levels])
        upstream[tile, 6 * rows :] = jnp.zeros(((FIELDS - 6) * rows, LANES), jnp.float32)
        return carry

    lax.fori_loop(0, own_tiles, combine, 0)


def slope_of(signal, h):
    h = h.astype(jnp.float32)
    return (signal * (1.0 - h * h)).astype(jnp.bfloat16)


def backward_kernel(
    numbers, sums, kept, bends, inner_hidden, inner_inputs, outer_hidden, outer_inputs, w_mid,
    ends, adjoint, packed,
    upstream, grads, near_hidden, far_hidden, near_flags, far_flags,
):
    layers = w_mid.shape[0]
    hid = w_mid.shape[1]
    cols = upstream.shape[0] * LANES
    rows = upstream.shape[1] // FIELDS
    last_at = layers * hid
    first_at = last_at + FIELDS
    for n in range(rows - 2):
        line_copy(n, cols, inner_hidden, near_hidden, near_flags).start()
    for n in range(2):
        line_copy(n, cols, outer_hidden, far_hidden, far_flags).start()
    grads[...] = jnp.zeros_like(grads)
    solve(numbers, sums, kept, bends, adjoint, upstream)

    def line(row, at_line, hidden, inputs):
        for at, size in pieces_of(cols):
            where = at_line * cols + at
            if not isinstance(where, int):
                where = pl.multiple_of(where, LANES)
            here = pl.ds(where, size)
            signal = widened(gathered(upstream, row, rows, at, size))
            h = hidden[layers, here, :]
            grads[last_at : last_at + FIELDS] += contract(signal, h, 1, 0)[:FIELDS]
            d = slope_of(contract(signal, ends[PADDED : 2 * PADDED], 0, 0), h)
            for k in range(layers - 1, -1, -1):
                h = hidden[k, here, :]
                grads[k * hid : (k + 1) * hid] += contract(d, h, 0, 0)
                d = slope_of(contract(d, w_mid[k], 1, 0), h)
            grads[first_at : first_at + FIELDS] += contract(inputs[:, here], d, 1, 0)[:FIELDS]

    def inside(row, carry):
        line_copy(row - 1, cols, inner_hidden, near_hidden, near_flags).wait()
        line(row, row - 1, near_hidden, inner_inputs)
        return carry

    lax.fori_loop(1, rows - 1, inside, 0)
    for n, row in enumerate((0, rows - 1)):
        line_copy(n, cols, outer_hidden, far_hidden, far_flags).wait()
        line(row, n, far_hidden, outer_inputs)
    chunk = packed.shape[1]
    for n in range(packed.shape[0]):
        for r in range(chunk):
            packed[n, r] = grads[n * chunk + r : n * chunk + r + 1]


def gather_kernel(parts, total):
    total[...] = jnp.broadcast_to(jnp.sum(parts[...], axis=0, keepdims=True), total.shape)


def deliver_kernel(parts, grad_first, grad_mid, grad_last, flat):
    chunk = parts.shape[1]
    for n in range(parts.shape[0]):
        for r in range(chunk):
            flat[n * chunk + r : n * chunk + r + 1] = parts[n, r]
    layers, hid = grad_mid.shape[0], grad_mid.shape[1]
    for k in range(layers):
        grad_mid[k] = flat[k * hid : (k + 1) * hid]
    at = layers * hid
    grad_last[...] = flat[at : at + FIELDS][: grad_last.shape[0]]
    grad_first[...] = flat[at + FIELDS : at + 2 * FIELDS][: grad_first.shape[0]]


def fill_shifts(shifts):
    shape = (PIECES * LANES, LANES)
    source = lax.broadcasted_iota(jnp.int32, shape, 0) % LANES
    target = lax.broadcasted_iota(jnp.int32, shape, 1)
    for n, step in enumerate((1, LANES - 1)):
        hit = (source + step) % LANES == target
        shifts[:, n * LANES : (n + 1) * LANES] = jnp.where(hit, 1.0, 0.0).astype(jnp.bfloat16)


def pieces(x):
    parts = []
    for n in range(PIECES):
        part = x.astype(jnp.bfloat16)
        parts.append(part)
        if n + 1 < PIECES:
            x = x - part.astype(jnp.float32)
    return jnp.concatenate(parts, axis=1)


def groups_of(array):
    tiles = array.shape[2] // LANES
    return [range(t, min(t + GROUP, tiles)) for t in range(0, tiles, GROUP)]


def stacked(source, group):
    return pieces(
        jnp.concatenate([source[c, :, lanes_of(t)] for t in group for c in range(3)], axis=0)
    )


def shift_both(source, before, after, shifts):
    tall = source.shape[1]
    for group in groups_of(source):
        moved = contract(stacked(source, group), shifts[...], 1, 0)
        for n, tile in enumerate(group):
            for c in range(3):
                at = (3 * n + c) * tall
                before[c, :, lanes_of(tile)] = moved[at : at + tall, :LANES]
                after[c, :, lanes_of(tile)] = moved[at : at + tall, LANES:]


def shift_in_place(array, side, shifts):
    tall = array.shape[1]
    for group in groups_of(array):
        moved = contract(stacked(array, group), shifts[:, side * LANES : (side + 1) * LANES], 1, 0)
        for n, tile in enumerate(group):
            for c in range(3):
                at = (3 * n + c) * tall
                array[c, :, lanes_of(tile)] = moved[at : at + tall]


def krylov_kernel(
    numbers, r_mid, r_up, r_down, stiff, support, kept, bends, sums,
    basis, before, after, ahead, behind, middle, shifts,
):
    rows = r_mid.shape[1]
    wide = r_mid.shape[2]
    tiles = wide // LANES
    own_tiles = tiles - 1
    tall = 3 * rows
    lane = lax.broadcasted_iota(jnp.int32, (tall, LANES), 1)
    first, final = lane == 0, lane == LANES - 1

    def place(k, c, at, value):
        basis[k, c, :, at] = value
        kept[k, c, :, at] = value[rows : 2 * rows]

    def set_up(tile, carry):
        at = lanes_of(tile)
        for c in range(3):
            value = jnp.concatenate([r_up[c, :, at], r_mid[c, :, at], r_down[c, :, at]], axis=0)
            place(0, c, at, value)
        return carry

    fill_shifts(shifts)
    lax.fori_loop(0, tiles, set_up, 0)
    shift_both(basis.at[0], before, after, shifts)

    def strain_of(k, tile):
        e = spread_strains(*triples_of(basis.at[k], before, after, tile, tiles, first, final))
        for n in range(6):
            bends[k, tile, n * rows : (n + 1) * rows] = e[n][rows : 2 * rows]
        return e

    def stress_of(e, at):
        return mixed([stiff[n, :, at] for n in range(len(UPPER))], e)

    def mine(value):
        return value[rows : 2 * rows]

    zero = jnp.zeros((rows, LANES), jnp.float32)
    totals = [None] * SUMS

    for k in range(DEGREE):
        def push(tile, carry, k=k):
            at = lanes_of(tile)
            for c, (alpha, beta, gamma) in enumerate(
                spread_forces(stress_of(strain_of(k, tile), at))
            ):
                ahead[c, :, at] = alpha
                behind[c, :, at] = beta
                middle[c, :, at] = gamma
            return carry

        lax.fori_loop(0, tiles, push, 0)
        shift_in_place(ahead, 0, shifts)
        shift_in_place(behind, 1, shifts)

        centre, inverse = numbers[k], numbers[6 + k]
        former = numbers[2 + k]

        def advance(tile, carry, k=k):
            at = lanes_of(tile)
            left, right = beside(tile, tiles)
            at_left, at_right = lanes_of(left), lanes_of(right)
            image, here, following = [], [], []
            for c in range(3):
                vector = basis[k, c, :, at]
                value = (
                    middle[c, :, at]
                    + jnp.where(first, ahead[c, :, at_left], ahead[c, :, at])
                    + jnp.where(final, behind[c, :, at_right], behind[c, :, at])
                    + support[c, :, at] * vector
                )
                step = value - centre * vector
                if k:
                    step = step - former * basis[k - 1, c, :, at]
                step = step * inverse
                place(k + 1, c, at, step)
                image.append(mine(value))
                here.append(mine(vector))
                following.append(mine(step))
            if carry is None:
                return None

            def dot(left_side, right_side):
                return (
                    left_side[0] * right_side[0]
                    + left_side[1] * right_side[1]
                    + left_side[2] * right_side[2]
                )

            def old(m):
                return [basis[m, c, rows : 2 * rows, at] for c in range(3)]

            fresh = []
            origin = here if k == 0 else old(0)
            if k == 0:
                fresh.append(dot(here, here))
            fresh.append(dot(origin, following))
            for j in range(k + 1):
                fresh.append(dot(here if j == k else (origin if j == 0 else old(j)), image))
            if k == DEGREE - 1:
                fresh.append(dot(old(1), following))
                fresh.append(dot(here, following))
                fresh.append(dot(following, following))
            return tuple(p + q for p, q in zip(carry, fresh))

        names = ([0] if k == 0 else []) + [k + 1] + [4 + k * (k + 1) // 2 + j for j in range(k + 1)]
        if k == DEGREE - 1:
            names += [10, 11, 12]
        found = lax.fori_loop(0, own_tiles, advance, (zero,) * len(names))
        advance(own_tiles, None)
        shift_both(basis.at[k + 1], before, after, shifts)
        for name, value in zip(names, found):
            totals[name] = value

    def energy(tile, running):
        at = lanes_of(tile)
        e = strain_of(DEGREE, tile)
        e = [mine(value) for value in e]
        for n, (a, b) in enumerate(UPPER):
            term = stiff[n, rows : 2 * rows, at] * e[b] * e[a]
            running = running + (term if a == b else 2.0 * term)
        for c in range(3):
            vector = basis[DEGREE, c, rows : 2 * rows, at]
            running = running + support[c, rows : 2 * rows, at] * vector * vector
        return running

    totals[13] = lax.fori_loop(0, own_tiles, energy, zero)
    place_of = lax.broadcasted_iota(jnp.int32, (1, LANES), 1)
    line = jnp.zeros((1, LANES), jnp.float32)
    for n in range(SUMS):
        total = jnp.sum(jnp.sum(totals[n], axis=0, keepdims=True), axis=1, keepdims=True)
        line = jnp.where(place_of == n, jnp.broadcast_to(total, (1, LANES)), line)
    sums[...] = jnp.broadcast_to(line[None], sums.shape)


def basis_constants(layup_stiffness):
    bending = 0.5 * (jnp.mean(layup_stiffness[:, 3, 3]) + jnp.mean(layup_stiffness[:, 4, 4]))
    centres = [11.5 * bending + 1.1, 9.8 * bending + 1.1, 8.4 * bending + 1.1]
    widths = [3.9 * bending + 0.4, 5.6 * bending + 0.4, 4.8 * bending + 0.4]
    return centres, widths


ON_CHIP = pl.BlockSpec(memory_space=pltpu.VMEM)
SCALARS = pl.BlockSpec(memory_space=pltpu.SMEM)


IN_PLACE = pl.BlockSpec(memory_space=pltpu.HBM)


def kernel_call(body, name, scalars, outs, scratch, *operands, far=(), far_outs=()):
    specs = [SCALARS] * scalars + [ON_CHIP] * (len(operands) - scalars)
    for n in far:
        specs[n] = IN_PLACE
    return pl.pallas_call(
        body,
        in_specs=specs,
        out_specs=[IN_PLACE if n in far_outs else ON_CHIP for n in range(len(outs))],
        out_shape=[
            pltpu.HBM(*out) if n in far_outs else jax.ShapeDtypeStruct(*out)
            for n, out in enumerate(outs)
        ],
        scratch_shapes=[
            pltpu.VMEM(*s) if isinstance(s, tuple) else pltpu.SemaphoreType.DMA((s,))
            for s in scratch
        ],
        compiler_params=pltpu.CompilerParams(vmem_limit_bytes=LIMITS[name] << 20),
    )(*[
        pltpu.with_memory_space_constraint(x, pltpu.HBM) if n in far else x
        for n, x in enumerate(operands)
    ])


LIMITS = {
    "assemble": 4,
    "inner": 40, "outer": 40, "prepare": 8, "krylov": 10, "backward": 32, "gather": 4, "deliver": 4,
}


def per_device(displacement, load, foundation, layup, layup_stiffness, w_first, w_mid, w_last):
    f32, bf16 = jnp.float32, jnp.bfloat16
    rows, cols = layup.shape
    layers, hid = w_mid.shape[0], w_mid.shape[1]
    devices = lax.axis_size("patch") * lax.axis_size("sub")
    wide = cols + LANES
    tall = 3 * rows
    tiles = wide // LANES
    (fields,) = kernel_call(
        assemble_kernel, "assemble", 0,
        [((10, rows, cols), f32)], [((rows, cols), jnp.int32), 4],
        displacement, foundation, layup, load, far=(0, 1, 2, 3),
    )
    before, after = from_both(fields, "sub", 2, HY)
    gap = jnp.zeros(fields.shape[:2] + (LANES - 2 * HY,), f32)
    fields = jnp.concatenate([fields, after, gap, before], axis=2)
    sends = [
        jnp.concatenate([*[fields[c, edge] for c in range(3)], fields[6, edge][near]])
        for edge, near in ((slice(rows - MARGIN, rows), slice(1, 2)), (slice(0, MARGIN), slice(0, 1)))
    ]
    up = lax.ppermute(sends[0], "patch", ring("patch", 1))
    down = lax.ppermute(sends[1], "patch", ring("patch", -1))
    fl_up, fl_down = from_both(fields[3:7], "patch", 1, 6)

    halving = jnp.array(HALVING, f32)
    table = (layup_stiffness * halving[:, None] * halving[None, :]).reshape(-1)
    centres, widths = basis_constants(layup_stiffness)
    numbers = jnp.stack(centres + widths + [1.0 / x for x in widths])
    thin = w_first.shape[1]
    blank = jnp.zeros((PADDED - thin, hid), bf16)
    ends = jnp.concatenate([w_first.T, blank, w_last, blank])

    learned, inner_hidden, inner_inputs = kernel_call(
        inner_kernel, "inner", 0,
        [((tiles, FIELDS * rows, LANES), f32), ((layers + 1, (rows - 2) * cols, hid), bf16),
         ((PADDED, (rows - 2) * cols), bf16)],
        [((3, rows, wide), f32)] * 2
        + [((tiles, FIELDS * rows, LANES), f32), ((layers + 1, (rows - 2) * cols, hid), bf16),
           PARTS * (layers + 1)],
        fields, ends, w_mid, far_outs=(1,),
    )
    wide_residual, residual, outer_hidden, outer_inputs = kernel_call(
        outer_kernel, "outer", 1,
        [((3, rows, wide), f32), ((3, rows, cols), f32),
         ((layers + 1, 2 * cols, hid), bf16), ((PADDED, 2 * cols), bf16)],
        [((3, tall, wide), f32)] * 6
        + [((tiles, FIELDS * tall, LANES), f32)] * 2
        + [((len(UPPER), tall, wide), f32), ((PIECES * LANES, 2 * LANES), bf16),
           ((layers + 1, 2 * cols, hid), bf16), layers + 1],
        table, fields, up, down, learned, ends, w_mid, far_outs=(2,),
    )
    stiff, support = kernel_call(
        prepare_kernel, "prepare", 1,
        [((len(UPPER), tall, wide), f32), ((3, tall, wide), f32)], [],
        table, fields, fl_up, fl_down,
    )
    up, down = from_both(wide_residual, "patch", 1, rows)
    kept, bends, sums = kernel_call(
        krylov_kernel, "krylov", 1,
        [((DEGREE + 1, 3, rows, wide), f32), ((DEGREE + 1, tiles, 6 * rows, LANES), f32),
         ((devices, 1, LANES), f32)],
        [((DEGREE + 1, 3, tall, wide), f32)] + [((3, tall, wide), f32)] * 5
        + [((PIECES * LANES, 2 * LANES), bf16)],
        numbers, wide_residual, up, down, stiff, support,
    )
    sums = everyone(sums)
    count = layers * hid + 2 * FIELDS
    chunk = -(-count // devices)
    adjoint, packed = kernel_call(
        backward_kernel, "backward", 1,
        [((3, rows, cols), f32), ((devices, chunk, 1, LANES), f32)],
        [((tiles - 1, FIELDS * rows, LANES), f32),
         ((devices * chunk, LANES), f32), ((layers + 1, (rows - 2) * cols, hid), bf16),
         ((layers + 1, 2 * cols, hid), bf16), rows - 2, 2],
        numbers, sums, kept, bends, inner_hidden, inner_inputs, outer_hidden, outer_inputs,
        w_mid, ends, far=(4, 6),
    )
    (total,) = kernel_call(
        gather_kernel, "gather", 0, [(packed.shape, f32)], [], everyone(packed)
    )
    grad_first, grad_mid, grad_last = kernel_call(
        deliver_kernel, "deliver", 0,
        [((thin, hid), f32), (w_mid.shape, f32), (w_last.shape, f32)],
        [((devices * chunk, LANES), f32)],
        everyone(total),
    )
    return residual, adjoint, grad_first.T, grad_mid, grad_last


def solution(mesh):
    field = P(None, "patch", "sub")
    return jax.shard_map(
        per_device,
        mesh=mesh,
        in_specs=(field, field, field, P("patch", "sub"), P(), P(), P(), P()),
        out_specs=(field, field, P(), P(), P()),
        check_vma=False,
    )
```
